32 devices in a mesh: dp: 4 (over z), hid: 2 (over core), wid: 4 (over y, x).
Axes of the slice: x: 2, y: 2, z: 4, core: 2. Of those that a mesh axis runs over, the one named last changes fastest.
Arguments:
- tokens: bfloat16 [4096, 1536], P('dp', 'wid'), may hold values from -6 to 6
- cotangent: bfloat16 [4096, 1536], P('dp', 'wid'), may hold values from -6 to 6
- lengths: int32 [16], P(('dp', 'wid')), may hold values from 64 to 256, as said below
- w_project: bfloat16 [1536, 4, 1536], P('wid', None, 'hid'), may hold values from -0.15625 to 0.15625
- w_beta: bfloat16 [1536, 12], P('wid', 'hid'), may hold values from -0.15625 to 0.15625
- w_out: bfloat16 [1536, 1536], P('wid', 'hid'), may hold values from -1.25 to 1.25
- w_gate_up: bfloat16 [1536, 2, 4096], P('wid', None, 'hid'), may hold values from -0.15625 to 0.15625
- w_down: bfloat16 [1536, 4096], P('wid', 'hid'), may hold values from -0.09375 to 0.09375
- gain_attn: bfloat16 [1536], P('wid'), may hold values from 0.5 to 1.5
- gain_ffn: bfloat16 [1536], P('wid'), may hold values from 0.5 to 1.5
Outputs:
- output: bfloat16 [4096, 1536], P('dp', 'wid')
- input_grad: bfloat16 [4096, 1536], P('dp', 'wid')
- grad_project: float32 [1536, 4, 1536], P(('dp', 'wid'), None, 'hid')
- grad_beta: float32 [1536, 12], P(('dp', 'wid'), 'hid')
- grad_out: float32 [1536, 1536], P(('dp', 'wid'), 'hid')
- grad_gate_up: float32 [1536, 2, 4096], P(('dp', 'wid'), None, 'hid')
- grad_down: float32 [1536, 4096], P(('dp', 'wid'), 'hid')
- grad_gain_attn: float32 [1536], P(('dp', 'wid'))
- grad_gain_ffn: float32 [1536], P(('dp', 'wid'))
The draws below stay inside these ranges and needn't reach their ends.
Inputs may be any that keep to these rules, and one draw needn't show every extreme that they name: `lengths`: some bucket is full and some bucket holds exactly 64 valid tokens.
All inputs are finite; a program needn't handle non-finite values.
Results may differ from the reference program's by a relative error of at most 0.015.
Values may be sent and summed in bfloat16 or wider, within the bound.
No kernel may reach another device: no remote copies, remote signals or barrier semaphores. Data moves between devices by JAX's collectives and lax.ppermute only.
A program may use at most 192 MiB of HBM per device.

```python
import jax
import jax.numpy as jnp
from jax import lax

D = 1536
HEADS = 12
HEAD_DIM = 128
FF = 4096
SEQ = 256
GROUP = 64
BUCKETS = 16
TOKENS = 4096


def draw_lengths(key, part):
    key_one, key_two = jax.random.split(key)
    drawn = jax.random.randint(key_one, (BUCKETS,), SEQ // 4, SEQ + 1)
    ordering = jax.random.permutation(key_two, BUCKETS)
    drawn = drawn.at[ordering[0]].set(SEQ)
    drawn = drawn.at[ordering[1]].set(SEQ // 4)
    return drawn.astype(jnp.int32)


def shard_levels(own_key, extent, pieces, low, high):
    gain = 1.0
    for position, blocks in pieces:
        draws = jax.random.uniform(jax.random.fold_in(jax.random.fold_in(own_key, 6), position), (blocks,), jnp.float32, low / len(pieces), high / len(pieces))
        gain = gain * jnp.repeat(jnp.exp(draws), extent[position] // blocks).reshape((-1,) + (1,) * (len(extent) - 1 - position))
    return gain


def bell_draw(stream_key, shape, width, most, cuts=(), held_as=jnp.bfloat16):
    values = jax.random.normal(stream_key, shape, jnp.float32) * width
    if len(cuts) > 0:
        values = shard_levels(stream_key, shape, cuts, -0.22, 0.18) * values
    return jnp.clip(values, min=-most, max=most).astype(held_as)


def setup_inputs(seed: int = 0) -> dict:
    keys = jax.random.split(jax.random.key(seed), 11)
    return {
        "tokens": bell_draw(keys[0], (TOKENS, D), 1.0, 6.0, ((0, 4), (1, 4))),
        "cotangent": bell_draw(keys[1], (TOKENS, D), 1.0, 6.0, ((0, 4), (1, 4))),
        "lengths": draw_lengths(jax.random.fold_in(keys[10], 71), 0),
        "w_project": bell_draw(keys[3], (D, 4, HEADS * HEAD_DIM), D ** -0.5, 0.15625, ((0, 4), (2, 2))),
        "w_beta": bell_draw(keys[4], (D, HEADS), D ** -0.5, 0.15625, ((0, 4), (1, 2))),
        "w_out": bell_draw(keys[5], (D, HEADS * HEAD_DIM), (max(HEADS * HEAD_DIM // 64, 1)) ** -0.5, 1.25, ((0, 4), (1, 2))),
        "w_gate_up": bell_draw(keys[6], (D, 2, FF), D ** -0.5, 0.15625, ((0, 4), (2, 2))),
        "w_down": bell_draw(keys[7], (D, FF), FF ** -0.5, 0.09375, ((0, 4), (1, 2))),
        "gain_attn": jnp.clip(1.0 + 0.1 * jax.random.normal(keys[8], (D,), jnp.float32), 0.5, 1.5).astype(jnp.bfloat16),
        "gain_ffn": jnp.clip(1.0 + 0.1 * jax.random.normal(keys[9], (D,), jnp.float32), 0.5, 1.5).astype(jnp.bfloat16),
    }


highest = lax.Precision.HIGHEST
masked_score = -1e+30

@jax.custom_vjp
def low(v):
    return lax.optimization_barrier(v.astype(jnp.bfloat16)).astype(jnp.float32)

@jax.custom_vjp
def low_back(v):
    return v

def low_keep(v):
    return (low(v), None)

def low_pass(kept, grad):
    return (grad,)

def back_keep(v):
    return (v, None)

def back_low(kept, grad):
    return (low(grad),)
low.defvjp(low_keep, low_pass)
low_back.defvjp(back_keep, back_low)

def path_attention(queries, key_rows, value_rows, house_raw, beta_logit, valid):
    seq_len, heads, head_size = queries.shape
    count = seq_len // GROUP
    scale = head_size ** (-0.5)
    house = house_raw * lax.rsqrt(lax.optimization_barrier(jnp.sum(house_raw * house_raw, axis=-1, keepdims=True)) + 1e-06)
    strength = 2.0 * jax.nn.sigmoid(beta_logit)

    def blocks(array):
        return array.reshape(count, GROUP, heads, head_size).transpose(0, 2, 1, 3)
    query_blocks = blocks(queries)
    key_blocks = blocks(key_rows)
    value_blocks = blocks(value_rows)
    house_blocks = blocks(house)
    value_all = value_rows.transpose(1, 0, 2)
    strength_blocks = strength.reshape(count, GROUP, heads).transpose(0, 2, 1)
    inner = jnp.arange(GROUP, dtype=jnp.int32)
    lower_incl = (inner[:, None] >= inner[None, :]).astype(jnp.float32)
    lower_strict = (inner[:, None] > inner[None, :]).astype(jnp.float32)
    gram = jnp.einsum('nhie,nhje->nhij', house_blocks, house_blocks, precision=highest) * lower_strict
    identity = jnp.eye(GROUP, dtype=jnp.float32)
    system = identity + strength_blocks[..., :, None] * gram
    diagonal = identity * strength_blocks[..., None, :]
    mixing = lax.linalg.triangular_solve(system, diagonal, left_side=True, lower=True, unit_diagonal=True)
    update = jnp.einsum('nhst,nhte->nhse', mixing, house_blocks, precision=highest)
    query_house = jnp.einsum('nhie,nhse->nhis', query_blocks, house_blocks, precision=highest) * lower_incl
    house_key = jnp.einsum('nhte,nhje->nhtj', house_blocks, key_blocks, precision=highest) * lower_strict
    carried = jnp.einsum('nhst,nhtj->nhsj', mixing, house_key, precision=highest)
    intra = jnp.einsum('nhie,nhje->nhij', query_blocks, key_blocks, precision=highest) - jnp.einsum('nhis,nhsj->nhij', query_house, carried, precision=highest)
    query_hat = query_blocks - jnp.einsum('nhis,nhse->nhie', query_house, update, precision=highest)
    key_hat = key_blocks - jnp.einsum('nhsj,nhse->nhje', carried, house_blocks, precision=highest)
    positions = jnp.arange(seq_len, dtype=jnp.int32)
    key_valid = valid > 0.5

    def step(state, inputs):
        index, query_part, intra_part, update_part, house_part, key_part, value_part = inputs
        start = index * GROUP
        far = jnp.einsum('hie,hje->hij', query_part, state, precision=highest) * scale
        far_mask = (positions < start) & key_valid
        far = jnp.where(far_mask[None, None, :], far, masked_score)
        group_valid = lax.dynamic_slice_in_dim(valid, start, GROUP) > 0.5
        near_mask = (lower_incl > 0.5) & group_valid[None, :]
        near = jnp.where(near_mask[None], intra_part * scale, masked_score)
        top_score = jnp.maximum(lax.optimization_barrier(jnp.max(far, axis=-1, keepdims=True)), lax.optimization_barrier(jnp.max(near, axis=-1, keepdims=True)))
        far_weight = jnp.exp(far - top_score)
        near_weight = jnp.exp(near - top_score)
        total = lax.optimization_barrier(jnp.sum(far_weight, axis=-1, keepdims=True)) + lax.optimization_barrier(jnp.sum(near_weight, axis=-1, keepdims=True))
        mixed = jnp.einsum('hij,hje->hie', far_weight, value_all, precision=highest) + jnp.einsum('hij,hje->hie', near_weight, value_part, precision=highest)
        mixed = mixed / total
        along = jnp.einsum('hje,hce->hjc', state, update_part, precision=highest)
        moved = state - jnp.einsum('hjc,hce->hje', along, house_part, precision=highest)
        state = lax.dynamic_update_slice_in_dim(moved, key_part, start, axis=1)
        return (state, mixed)
    initial = jnp.zeros((heads, seq_len, head_size), jnp.float32)
    indices = jnp.arange(count, dtype=jnp.int32)
    xs_all = (indices, query_hat, intra, update, house_blocks, key_hat, value_blocks)
    final_state, outputs = lax.scan(jax.checkpoint(step), initial, xs_all)
    result = outputs.transpose(0, 2, 1, 3).reshape(seq_len, heads, head_size)
    return result * valid[:, None, None]

def bucket_layer(rows, length_one, weights):
    project_w, beta_w, out_w, gate_up_w, down_w, gain_one, gain_two = weights
    seq_len = rows.shape[0]
    positions = jnp.arange(seq_len, dtype=jnp.int32)
    valid = (positions < length_one).astype(jnp.float32)
    factor_one = lax.rsqrt(lax.optimization_barrier(jnp.mean(rows * rows, axis=-1, keepdims=True)) + 1e-06)
    normed_one = low(rows * factor_one * gain_one)
    projected = low(low_back(jnp.einsum('sd,dgk->sgk', normed_one, project_w, precision=highest)))
    beta_logit = low_back(jnp.dot(normed_one, beta_w, precision=highest))
    parts = projected.reshape(seq_len, 4, HEADS, HEAD_DIM)
    attended = path_attention(parts[:, 0], parts[:, 1], parts[:, 2], parts[:, 3], beta_logit, valid)
    attended = low(low_back(attended.reshape(seq_len, HEADS * HEAD_DIM)))
    branch = low_back(jnp.einsum('sk,dk->sd', attended, out_w, precision=highest))
    hidden = rows + branch
    factor_two = lax.rsqrt(lax.optimization_barrier(jnp.mean(hidden * hidden, axis=-1, keepdims=True)) + 1e-06)
    normed_two = low(hidden * factor_two * gain_two)
    gate_up = low_back(jnp.einsum('sd,dgf->sgf', normed_two, gate_up_w, precision=highest))
    mixed = low(jax.nn.silu(gate_up[:, 0]) * gate_up[:, 1])
    ffn = jnp.einsum('sf,df->sd', mixed, down_w, precision=highest)
    return (hidden + ffn) * valid[:, None]

def reference(tokens, cotangent, lengths, w_project, w_beta, w_out, w_gate_up, w_down, gain_attn, gain_ffn):
    weights = (w_project.astype(jnp.float32), w_beta.astype(jnp.float32), w_out.astype(jnp.float32), w_gate_up.astype(jnp.float32), w_down.astype(jnp.float32), gain_attn.astype(jnp.float32), gain_ffn.astype(jnp.float32))
    rows_all = tokens.astype(jnp.float32).reshape(BUCKETS, SEQ, D)
    grads_all = cotangent.astype(jnp.float32).reshape(BUCKETS, SEQ, D)

    def one_bucket(totals, inputs):
        rows, grad_rows, length_one = inputs

        def layer_of(rows_in, weight_list):
            return bucket_layer(rows_in, length_one, weight_list)
        result, pullback = jax.vjp(layer_of, rows, weights)
        grad_input, grad_weights = pullback(grad_rows)
        totals = jax.tree.map(lambda running, adding: running + adding, totals, grad_weights)
        return (totals, (result.astype(jnp.bfloat16), grad_input.astype(jnp.bfloat16)))
    zeros = jax.tree.map(jnp.zeros_like, weights)
    totals, stacked = lax.scan(one_bucket, zeros, (rows_all, grads_all, lengths))
    outputs, inputs_back = stacked
    return (outputs.reshape(TOKENS, D), inputs_back.reshape(TOKENS, D), totals[0], totals[1], totals[2], totals[3], totals[4], totals[5], totals[6])
```

```python
import functools

import jax
import jax.numpy as jnp
from jax import lax
from jax.experimental import pallas as pl
from jax.experimental.pallas import tpu as pltpu
from jax.sharding import PartitionSpec as P

f32 = jnp.float32
bf16 = jnp.bfloat16

SEQ = 256
HD = 128


def dot_of(a, b, ca, cb):
    return lax.dot_general(a, b, (((ca,), (cb,)), ((), ())), preferred_element_type=f32)


def halves_of(a):
    high = a.astype(bf16)
    return high, (a - high.astype(f32)).astype(bf16)


def mul(a, b, ca=1, cb=0, passes=3):
    if passes == 1:
        return dot_of(a.astype(bf16), b.astype(bf16), ca, cb)
    if a.dtype == bf16:
        bh, bl = halves_of(b)
        return dot_of(a, bh, ca, cb) + dot_of(a, bl, ca, cb)
    if b.dtype == bf16:
        ah, al = halves_of(a)
        return dot_of(ah, b, ca, cb) + dot_of(al, b, ca, cb)
    ah, al = halves_of(a)
    bh, bl = halves_of(b)
    return dot_of(ah, bh, ca, cb) + (dot_of(ah, bl, ca, cb) + dot_of(al, bh, ca, cb))


def iotas():
    rows = lax.broadcasted_iota(jnp.int32, (SEQ, SEQ), 0)
    cols = lax.broadcasted_iota(jnp.int32, (SEQ, SEQ), 1)
    return rows, cols


def prepare(raw, logit_row, i, j):
    eye = i == j
    raw_f = raw.astype(f32)
    norm = lax.rsqrt(jnp.sum(raw_f * raw_f, axis=1, keepdims=True) + 1e-6)
    norm_row = jnp.sum(jnp.where(eye, norm, 0.0), axis=0, keepdims=True)
    beta_row = 2.0 / (1.0 + jnp.exp(-logit_row))
    beta = jnp.sum(jnp.where(eye, beta_row, 0.0), axis=1, keepdims=True)
    return raw_f, norm, norm_row, beta_row, beta


def inverses(lowers, i, j):
    eye = jnp.where(i == j, 1.0, 0.0)
    first = ((i >> 1) == (j >> 1)) & (i > j)
    inv = [eye - jnp.where(first, n, 0.0) for n in lowers]
    s = 1
    while (1 << s) < SEQ:
        mask = ((i >> (s + 1)) == (j >> (s + 1))) & ((i >> s) > (j >> s))
        mids = [mul(d, jnp.where(mask, n, 0.0)) for d, n in zip(inv, lowers)]
        inv = [d - mul(x, d) for d, x in zip(inv, mids)]
        s += 1
    return inv


def forward_kernel(count, len_ref, x_ref, l_ref, o_ref, inv_ref, carry_ref, prob_ref):
    base = pl.program_id(0) * count
    i, j = iotas()
    row = lax.broadcasted_iota(jnp.int32, (SEQ, 1), 0)
    xs = [x_ref[t] for t in range(count)]
    qs = [x[:, 0:HD] for x in xs]
    ks = [x[:, HD : 2 * HD] for x in xs]
    vs = [x[:, 2 * HD : 3 * HD] for x in xs]
    us = [x[:, 3 * HD : 4 * HD] for x in xs]
    pre = [prepare(us[t], l_ref[t], i, j) for t in range(count)]
    lowers = [
        p[4] * jnp.where(i > j, dot_of(u, u, 1, 1) * p[1] * p[2], 0.0) for u, p in zip(us, pre)
    ]
    inv = inverses(lowers, i, j)
    bs = [jnp.where(i > j, dot_of(u, k, 1, 1) * p[1], 0.0) for u, k, p in zip(us, ks, pre)]
    carries = [mul(d * p[3], b) for d, p, b in zip(inv, pre, bs)]
    as_ = [jnp.where(i >= j, dot_of(q, u, 1, 1) * p[2], 0.0) for q, u, p in zip(qs, us, pre)]
    scores = [
        (dot_of(q, k, 1, 1) - mul(a, c)) * (HD**-0.5) for q, k, a, c in zip(qs, ks, as_, carries)
    ]
    for t in range(count):
        length = len_ref[base + t]
        score = jnp.where((j <= i) & (j < length), scores[t], -1e30)
        weight = jnp.exp(score - jnp.max(score, axis=1, keepdims=True))
        prob = weight * (1.0 / jnp.sum(weight, axis=1, keepdims=True))
        out = jnp.where(row < length, mul(prob, vs[t], passes=1), 0.0)
        o_ref[t] = out.astype(bf16)
        inv_ref[t] = inv[t]
        carry_ref[t] = carries[t]
        prob_ref[t] = prob


def backward_kernel(
    count, len_ref, x_ref, l_ref, inv_ref, carry_ref, prob_ref, do_ref, dx_ref, dl_ref
):
    base = pl.program_id(0) * count
    i, j = iotas()
    row = lax.broadcasted_iota(jnp.int32, (SEQ, 1), 0)
    for t in range(count):
        x = x_ref[t]
        q, k = x[:, 0:HD], x[:, HD : 2 * HD]
        v, u = x[:, 2 * HD : 3 * HD], x[:, 3 * HD : 4 * HD]
        do = do_ref[t]
        do = jnp.where(row < len_ref[base + t], do, jnp.zeros_like(do))
        inv, carry, prob = inv_ref[t], carry_ref[t], prob_ref[t]
        raw, norm, norm_row, beta_row, beta = prepare(u, l_ref[t], i, j)
        gram = jnp.where(i > j, dot_of(u, u, 1, 1) * norm * norm_row, 0.0)
        a = jnp.where(i >= j, dot_of(q, u, 1, 1) * norm_row, 0.0)
        b = jnp.where(i > j, dot_of(u, k, 1, 1) * norm, 0.0)
        m = inv * beta_row
        dv = mul(prob, do, 0, 0, passes=1)
        dprob = dot_of(do, v, 1, 1)
        ds = prob * (dprob - jnp.sum(dprob * prob, axis=1, keepdims=True)) * (HD**-0.5)
        da = jnp.where(i >= j, -mul(ds, carry, 1, 1), 0.0)
        dc = -mul(a, ds, 0, 0)
        dm = mul(dc, b, 1, 1)
        db = jnp.where(i > j, mul(m, dc, 0, 0), 0.0)
        dn = jnp.where(i > j, -mul(mul(inv, dm, 0, 0), m, 1, 1), 0.0)
        dgram = beta * dn
        dbeta = jnp.sum(dm * inv, axis=0, keepdims=True)
        dbeta_col = jnp.sum(dn * gram, axis=1, keepdims=True)
        dbeta = dbeta + jnp.sum(jnp.where(i == j, dbeta_col, 0.0), axis=0, keepdims=True)
        dq = mul(ds, k, passes=1) + mul(da * norm_row, u, passes=1)
        dk = mul(ds, q, 0, 0, passes=1) + mul(db * norm, u, 0, 0, passes=1)
        dw = mul(da, q, 0, 0, passes=1) + mul(db, k, passes=1)
        dw = dw + mul(dgram * norm_row, u, passes=1) + mul(dgram * norm, u, 0, 0, passes=1)
        du = norm * dw - (norm * norm * norm) * raw * jnp.sum(dw * raw, axis=1, keepdims=True)
        dx_ref[t] = jnp.concatenate([dq, dk, dv, du], axis=1).astype(bf16)
        dl_ref[t] = dbeta * beta_row * (1.0 - 0.5 * beta_row)


def block_of(count, *shape):
    return pl.BlockSpec((count,) + shape, lambda g, lens: (g, 0, 0))


def attention_forward(lens, x, logits, count=3):
    pairs = x.shape[0]
    square = jax.ShapeDtypeStruct((pairs, SEQ, SEQ), f32)
    return pl.pallas_call(
        functools.partial(forward_kernel, count),
        out_shape=[jax.ShapeDtypeStruct((pairs, SEQ, HD), bf16), square, square, square],
        grid_spec=pltpu.PrefetchScalarGridSpec(
            num_scalar_prefetch=1,
            grid=(pairs // count,),
            in_specs=[block_of(count, SEQ, 4 * HD), block_of(count, 1, SEQ)],
            out_specs=[block_of(count, SEQ, HD)] + [block_of(count, SEQ, SEQ)] * 3,
        ),
        compiler_params=pltpu.CompilerParams(vmem_limit_bytes=48 << 20),
        cost_estimate=pl.CostEstimate(
            flops=pairs * 1600000000, bytes_accessed=pairs * 1100000, transcendentals=pairs * 65536
        ),
    )(lens, x, logits)


def attention_backward(lens, x, logits, inv, carry, prob, do, count=1):
    pairs = x.shape[0]
    return pl.pallas_call(
        functools.partial(backward_kernel, count),
        out_shape=[
            jax.ShapeDtypeStruct((pairs, SEQ, 4 * HD), bf16),
            jax.ShapeDtypeStruct((pairs, 1, SEQ), f32),
        ],
        grid_spec=pltpu.PrefetchScalarGridSpec(
            num_scalar_prefetch=1,
            grid=(pairs // count,),
            in_specs=[block_of(count, SEQ, 4 * HD), block_of(count, 1, SEQ)]
            + [block_of(count, SEQ, SEQ)] * 3
            + [block_of(count, SEQ, HD)],
            out_specs=[block_of(count, SEQ, 4 * HD), block_of(count, 1, SEQ)],
        ),
        compiler_params=pltpu.CompilerParams(vmem_limit_bytes=48 << 20),
        cost_estimate=pl.CostEstimate(
            flops=pairs * 1400000000, bytes_accessed=pairs * 1400000, transcendentals=pairs * 512
        ),
    )(lens, x, logits, inv, carry, prob, do)


def swap(x, axis, size, k):
    return lax.ppermute(x, axis, [(n, n ^ k) for n in range(size)])


def shift_rows(x, start, size):
    return lax.dynamic_slice_in_dim(x, start, size, axis=0)


def shift_cols(x, start, size):
    return lax.dynamic_slice_in_dim(x, start, size, axis=x.ndim - 1)


def mm(a, b, ca=1, cb=0):
    return dot_of(a, b, ca, cb)


def per_device(
    dp_size,
    wid_size,
    tokens,
    cotangent,
    lengths,
    w_project,
    w_beta,
    w_out,
    w_gate_up,
    w_down,
    gain_attn,
    gain_ffn,
):
    wid = lax.axis_index("wid")
    hid = lax.axis_index("hid")
    dp = lax.axis_index("dp")
    ws = range(wid_size)
    rows, part = tokens.shape
    half = rows // 2
    width = part * wid_size
    ff = w_down.shape[1] // wid_size
    heads = w_beta.shape[1]
    per_half = half // SEQ

    def wid_all(x):
        return [x] + [swap(x, "wid", wid_size, k) for k in ws if k > 0]

    def wid_to(pieces):
        return [pieces[0]] + [swap(pieces[k], "wid", wid_size, k) for k in ws if k > 0]

    def hid_swap(x):
        return swap(x, "hid", 2, 1)

    def head_a(w):
        return (3 * w + 1) // 2

    def head_b(w):
        return 1 + 3 * (w // 2)

    half_b = (wid & 1) ^ hid

    def own_rows(x):
        return shift_rows(x, hid * half, half)

    len_rel = jnp.concatenate(wid_all(lengths))
    len_of = [lax.dynamic_index_in_dim(len_rel, b ^ wid, keepdims=False) for b in ws]
    len_abs = jnp.stack(len_of)
    gains = wid_all(jnp.stack([gain_attn, gain_ffn]))
    gain_one_full = jnp.concatenate([g[0] for g in gains])[None].astype(f32)
    beta_full = jnp.concatenate(wid_all(w_beta), axis=0)

    def gather_rows(x):
        mine = own_rows(x)
        other = shift_rows(x, (1 - hid) * half, half)
        got = [swap(mine, "wid", wid_size, k) for k in ws if k > 0]
        far = [hid_swap(g) for g in got]
        return jnp.concatenate(
            [jnp.concatenate([mine] + got, axis=1), jnp.concatenate([other] + far, axis=1)], axis=0
        )

    x_full = gather_rows(tokens)
    project_flat = w_project.reshape(part, 4, heads, HD)

    def head_of(h):
        piece = lax.dynamic_index_in_dim(project_flat, h, axis=2, keepdims=False)
        return piece.reshape(part, 4 * HD)

    proj_a = jnp.concatenate(wid_to([head_of(head_a(wid ^ k)) for k in ws]), axis=0)
    proj_b = jnp.concatenate(wid_to([head_of(head_b(wid ^ k)) for k in ws]), axis=0)
    gate_up_w = jnp.concatenate(
        wid_to([shift_cols(w_gate_up, (wid ^ k) * ff, ff).reshape(part, 2 * ff) for k in ws]),
        axis=0,
    )
    g_raw = gather_rows(cotangent)
    down_w = jnp.concatenate(
        wid_to([shift_cols(w_down, (wid ^ k) * ff, ff) for k in ws]), axis=0
    )
    out_w = jnp.concatenate(
        [shift_cols(w_out, head_a(wid ^ k) * HD, HD) for k in ws]
        + [shift_cols(w_out, head_b(wid ^ (2 * q)) * HD, HD) for q in range(wid_size // 2)],
        axis=1,
    )

    def bucket_len(place, t):
        return lax.dynamic_index_in_dim(len_abs, (hid ^ place) * per_half + t, keepdims=False)

    lens_a = [bucket_len(p, t) for p in range(2) for t in range(per_half)]
    lens_b = [
        lax.dynamic_index_in_dim(len_abs, (wid & 1) * per_half + t, keepdims=False)
        for t in range(per_half)
    ]
    lens = jnp.stack(lens_a + lens_b)
    slot = jnp.arange(SEQ, dtype=jnp.int32)
    valid_rows = jnp.concatenate([(slot < n).astype(f32) for n in lens_a])[:, None]
    valid_half = valid_rows[:half]

    x_f = x_full.astype(f32)
    factor_one = lax.rsqrt(jnp.mean(x_f * x_f, axis=1, keepdims=True) + 1e-6)
    normed_one = (x_f * factor_one * gain_one_full).astype(bf16)
    normed_b = shift_rows(normed_one, half_b * half, half)
    pa = mm(normed_one, proj_a).astype(bf16)
    pb = mm(normed_b, proj_b).astype(bf16)
    pairs = jnp.concatenate([pa, pb], axis=0).reshape(-1, SEQ, 4 * HD)
    beta_w = jnp.concatenate(
        [shift_cols(beta_full, head_a(wid), 1), shift_cols(beta_full, head_b(wid), 1)], axis=1
    )
    logits = mm(beta_w, normed_one, 0, 1)
    logit_b = shift_cols(logits[1:2], half_b * half, half)
    logit_pairs = jnp.concatenate([logits[0:1], logit_b], axis=1).reshape(-1, 1, SEQ)
    attended, inv, carry, prob = attention_forward(lens, pairs, logit_pairs)

    o_all = wid_all(attended.reshape(-1, HD))
    pair_rows = []
    for q in range(wid_size // 2):
        one, two = o_all[2 * q][rows:], o_all[2 * q + 1][rows:]
        first = jnp.where(half_b == 0, one, two)
        second = jnp.where(half_b == 0, two, one)
        pair_rows.append(jnp.concatenate([first, second], axis=0))
    o_cat = jnp.concatenate([o[:rows] for o in o_all] + pair_rows, axis=1)
    attn_part = mm(o_cat, out_w, 1, 1)
    attn_half = attn_part[:half] + hid_swap(attn_part[half:])
    hidden = own_rows(tokens).astype(f32) + attn_half

    def row_mean(x):
        own = jnp.sum(x, axis=1).reshape(-1, 128)
        total = own
        for k in ws:
            if k > 0:
                total = total + swap(own, "wid", wid_size, k)
        return total.reshape(-1, 1) * (1.0 / width)

    gain_one = gain_attn[None].astype(f32)
    gain_two = gain_ffn[None].astype(f32)
    factor_two = lax.rsqrt(row_mean(hidden * hidden) + 1e-6)
    normed_half = (hidden * factor_two * gain_two).astype(bf16)
    n_got = jnp.concatenate(wid_all(normed_half), axis=1)
    normed_two = jnp.concatenate([n_got, hid_swap(n_got)], axis=0)
    grad_full = jnp.where(valid_rows > 0.5, g_raw, jnp.zeros_like(g_raw))
    gate_up = mm(normed_two, gate_up_w)
    gate, upward = gate_up[:, :ff], gate_up[:, ff:]
    sigmoid_gate = jax.nn.sigmoid(gate)
    active = gate * sigmoid_gate
    mixed = (active * upward).astype(bf16)
    grad_mixed = mm(grad_full, down_w)
    grad_gate = grad_mixed * upward * sigmoid_gate * (1.0 + gate * (1.0 - sigmoid_gate))
    grad_pair = jnp.concatenate([grad_gate, grad_mixed * active], axis=1).astype(bf16)

    def scatter_rows(x):
        low = x.astype(bf16)
        mine = x[:half] + hid_swap(low[half:]).astype(f32)
        sent = mine.astype(bf16)
        pieces = [sent[:, k * part : (k + 1) * part] for k in ws]
        total = mine[:, :part]
        for k in ws:
            if k > 0:
                total = total + swap(pieces[k], "wid", wid_size, k).astype(f32)
        return total

    grad_normed_two = scatter_rows(mm(grad_pair, gate_up_w, 1, 1))

    def dp_sum(pieces):
        k = 1
        held = list(pieces)
        while k < dp_size:
            keep = held[0::2]
            send = jnp.stack([h.astype(bf16) for h in held[1::2]])
            got = swap(send, "dp", dp_size, k)
            held = [a.astype(f32) + got[n].astype(f32) for n, a in enumerate(keep)]
            k *= 2
        return held[0]

    chunk = width // dp_size

    def dp_rows(x):
        low = x.astype(bf16)
        out = []
        for t in range(dp_size):
            row = (dp ^ t) * chunk
            start = ((row // part) ^ wid) * part + row % part
            out.append(shift_rows(low, start, chunk))
        return dp_sum(out)

    sub = chunk // wid_size

    def to_rows(x):
        low = x.astype(bf16)
        return wid_to([shift_rows(low, (wid ^ k) * sub, sub) for k in ws])

    g_down = dp_rows(mm(grad_full, mixed, 0, 0))
    g_gate_up = dp_rows(mm(normed_two, grad_pair, 0, 0))

    scaled = grad_normed_two * gain_two
    mean_two = row_mean(scaled * hidden)
    grad_half = own_rows(cotangent).astype(f32) * valid_half
    grad_hidden = grad_half + factor_two * scaled - (factor_two**3) * hidden * mean_two
    gain_two_part = jnp.sum(grad_normed_two * hidden * factor_two, axis=0)
    da_half = grad_hidden.astype(bf16)
    da = jnp.concatenate([da_half, hid_swap(da_half)], axis=0)
    do_part = mm(da, out_w).astype(bf16)
    do_pieces = []
    for k in ws:
        col = (wid_size + k // 2) * HD
        piece_b = shift_rows(do_part[:, col : col + HD], ((k & 1) ^ half_b) * half, half)
        do_pieces.append(jnp.concatenate([do_part[:, k * HD : (k + 1) * HD], piece_b], axis=0))
    do_sum = sum(d.astype(f32) for d in wid_to(do_pieces)).astype(bf16)
    grad_pairs, grad_logits = attention_backward(
        lens, pairs, logit_pairs, inv, carry, prob, do_sum.reshape(-1, SEQ, HD)
    )
    g_out = mm(da, o_cat, 0, 0)

    grad_pairs = grad_pairs.reshape(-1, 4 * HD)
    flat_logits = grad_logits.reshape(1, -1).astype(bf16)

    def spread(x):
        zero = jnp.zeros_like(x)
        return jnp.concatenate(
            [jnp.where(half_b == 0, x, zero), jnp.where(half_b == 0, zero, x)], axis=0
        )

    logit_a = flat_logits[:, :rows]
    logit_full = jnp.concatenate([logit_a, spread(flat_logits[:, rows:].T).T], axis=0)
    d_all = jnp.concatenate([grad_pairs[:rows], spread(grad_pairs[rows:])], axis=1)
    w_all = jnp.concatenate([proj_a, proj_b], axis=1)
    n1_part = mm(d_all, w_all, 1, 1) + mm(logit_full, beta_w, 0, 1)
    grad_normed_one = scatter_rows(n1_part)
    g_proj = dp_rows(mm(normed_one, d_all, 0, 0))
    g_beta = mm(logit_full, normed_one, 1, 0)

    scaled_one = grad_normed_one * gain_one
    source = own_rows(tokens).astype(f32)
    factor_half = factor_one[:half]
    mean_one = row_mean(scaled_one * source)
    gain_one_part = jnp.sum(grad_normed_one * source * factor_half, axis=0)
    input_half = grad_hidden + factor_half * scaled_one - (factor_half**3) * source * mean_one

    def whole_rows(x):
        other = hid_swap(x)
        return jnp.concatenate(
            [jnp.where(hid == 0, x, other), jnp.where(hid == 0, other, x)], axis=0
        )

    input_grad = whole_rows(input_half.astype(bf16))
    ffn = scatter_rows(mm(mixed, down_w, 1, 1))
    output = whole_rows(((hidden + ffn) * valid_half).astype(bf16))

    def place(pieces):
        stacked = jnp.stack(pieces)
        return [lax.dynamic_index_in_dim(stacked, n ^ wid, keepdims=False) for n in ws]

    down_rows = place(to_rows(g_down))
    out_down = jnp.concatenate(down_rows, axis=1).astype(f32)
    gu_rows = place([r.reshape(sub, 2, ff) for r in to_rows(g_gate_up)])
    out_gate_up = jnp.concatenate(gu_rows, axis=2).astype(f32)

    def heads_of(got, size):
        a = [g[..., :size].astype(f32) for g in got]
        b = [g[..., size:].astype(f32) for g in got]
        return [a[0], b[0] + b[1], a[1], a[2], b[2] + b[3], a[3]]

    proj_rows = heads_of(place(to_rows(g_proj)), 4 * HD)
    out_project = jnp.concatenate([p.reshape(sub, 4, HD) for p in proj_rows], axis=2)

    beta_low = dp_rows(jnp.concatenate([g_beta.T, jnp.zeros((width, 126), f32)], axis=1))
    out_beta = jnp.concatenate(heads_of([b[:, :2] for b in place(to_rows(beta_low))], 1), axis=1)

    fine = part // dp_size
    to_place = [
        (c * wid_size + w, w * dp_size + c) for c in range(dp_size) for w in range(wid_size)
    ]

    def dp_fine(x):
        pieces = [shift_rows(x, (dp ^ t) * fine, fine) for t in range(dp_size)]
        return dp_sum(pieces)

    head_cols = [0 ^ wid, wid_size + (wid // 2), 1 ^ wid, 2 ^ wid, wid_size + (1 ^ (wid // 2)), 3 ^ wid]
    out_sum = dp_fine(g_out)
    out_sum = jnp.concatenate([shift_cols(out_sum, h * HD, HD) for h in head_cols], axis=1)
    out_out = lax.ppermute(out_sum, ("dp", "wid"), to_place)

    gain_part = jnp.stack([gain_one_part, gain_two_part], axis=1)
    gain_part = gain_part + hid_swap(gain_part)
    gain_sum = lax.ppermute(dp_fine(gain_part), ("dp", "wid"), to_place)

    return (
        output,
        input_grad,
        out_project,
        out_beta,
        out_out,
        out_gate_up,
        out_down,
        gain_sum[:, 0],
        gain_sum[:, 1],
    )


def solution(mesh):
    return jax.shard_map(
        functools.partial(per_device, mesh.shape["dp"], mesh.shape["wid"]),
        mesh=mesh,
        in_specs=(
            P("dp", "wid"),
            P("dp", "wid"),
            P(("dp", "wid")),
            P("wid", None, "hid"),
            P("wid", "hid"),
            P("wid", "hid"),
            P("wid", None, "hid"),
            P("wid", "hid"),
            P("wid"),
            P("wid"),
        ),
        out_specs=(
            P("dp", "wid"),
            P("dp", "wid"),
            P(("dp", "wid"), None, "hid"),
            P(("dp", "wid"), "hid"),
            P(("dp", "wid"), "hid"),
            P(("dp", "wid"), None, "hid"),
            P(("dp", "wid"), "hid"),
            P(("dp", "wid")),
            P(("dp", "wid")),
        ),
        check_vma=False,
    )
```

```python
import functools

import jax
import jax.numpy as jnp
from jax import lax
from jax.experimental import pallas as pl
from jax.experimental.pallas import tpu as pltpu
from jax.sharding import PartitionSpec as P

f32 = jnp.float32
bf16 = jnp.bfloat16

SEQ = 256
HD = 128


def dot_of(a, b, ca, cb):
    return lax.dot_general(a, b, (((ca,), (cb,)), ((), ())), preferred_element_type=f32)


def halves_of(a):
    high = a.astype(bf16)
    return high, (a - high.astype(f32)).astype(bf16)


def mul(a, b, ca=1, cb=0, passes=3):
    if passes == 1:
        return dot_of(a.astype(bf16), b.astype(bf16), ca, cb)
    if a.dtype == bf16:
        bh, bl = halves_of(b)
        return dot_of(a, bh, ca, cb) + dot_of(a, bl, ca, cb)
    if b.dtype == bf16:
        ah, al = halves_of(a)
        return dot_of(ah, b, ca, cb) + dot_of(al, b, ca, cb)
    ah, al = halves_of(a)
    bh, bl = halves_of(b)
    return dot_of(ah, bh, ca, cb) + (dot_of(ah, bl, ca, cb) + dot_of(al, bh, ca, cb))


def iotas():
    rows = lax.broadcasted_iota(jnp.int32, (SEQ, SEQ), 0)
    cols = lax.broadcasted_iota(jnp.int32, (SEQ, SEQ), 1)
    return rows, cols


def prepare(raw, logit_row, i, j):
    eye = i == j
    raw_f = raw.astype(f32)
    norm = lax.rsqrt(jnp.sum(raw_f * raw_f, axis=1, keepdims=True) + 1e-6)
    norm_row = jnp.sum(jnp.where(eye, norm, 0.0), axis=0, keepdims=True)
    beta_row = 2.0 / (1.0 + jnp.exp(-logit_row))
    beta = jnp.sum(jnp.where(eye, beta_row, 0.0), axis=1, keepdims=True)
    return raw_f, norm, norm_row, beta_row, beta


def inverses(lowers, i, j):
    eye = jnp.where(i == j, 1.0, 0.0)
    first = ((i >> 1) == (j >> 1)) & (i > j)
    inv = [eye - jnp.where(first, n, 0.0) for n in lowers]
    s = 1
    while (1 << s) < SEQ:
        mask = ((i >> (s + 1)) == (j >> (s + 1))) & ((i >> s) > (j >> s))
        mids = [mul(d, jnp.where(mask, n, 0.0)) for d, n in zip(inv, lowers)]
        inv = [d - mul(x, d) for d, x in zip(inv, mids)]
        s += 1
    return inv


def forward_kernel(count, len_ref, x_ref, l_ref, o_ref, inv_ref, carry_ref, prob_ref):
    base = pl.program_id(0) * count
    i, j = iotas()
    row = lax.broadcasted_iota(jnp.int32, (SEQ, 1), 0)
    xs = [x_ref[t] for t in range(count)]
    qs = [x[:, 0:HD] for x in xs]
    ks = [x[:, HD : 2 * HD] for x in xs]
    vs = [x[:, 2 * HD : 3 * HD] for x in xs]
    us = [x[:, 3 * HD : 4 * HD] for x in xs]
    pre = [prepare(us[t], l_ref[t], i, j) for t in range(count)]
    lowers = [
        p[4] * jnp.where(i > j, dot_of(u, u, 1, 1) * p[1] * p[2], 0.0) for u, p in zip(us, pre)
    ]
    inv = inverses(lowers, i, j)
    bs = [jnp.where(i > j, dot_of(u, k, 1, 1) * p[1], 0.0) for u, k, p in zip(us, ks, pre)]
    carries = [mul(d * p[3], b) for d, p, b in zip(inv, pre, bs)]
    as_ = [jnp.where(i >= j, dot_of(q, u, 1, 1) * p[2], 0.0) for q, u, p in zip(qs, us, pre)]
    scores = [
        (dot_of(q, k, 1, 1) - mul(a, c)) * (HD**-0.5) for q, k, a, c in zip(qs, ks, as_, carries)
    ]
    for t in range(count):
        length = len_ref[base + t]
        score = jnp.where((j <= i) & (j < length), scores[t], -1e30)
        weight = jnp.exp(score - jnp.max(score, axis=1, keepdims=True))
        prob = weight * (1.0 / jnp.sum(weight, axis=1, keepdims=True))
        out = jnp.where(row < length, mul(prob, vs[t], passes=1), 0.0)
        o_ref[t] = out.astype(bf16)
        inv_ref[t] = inv[t]
        carry_ref[t] = carries[t]
        prob_ref[t] = prob


def to_row(col, eye):
    return jnp.sum(jnp.where(eye, col, 0.0), axis=0, keepdims=True)


def backward_kernel(
    count,
    start,
    len_ref,
    x_ref,
    l_ref,
    inv_ref,
    carry_ref,
    prob_ref,
    do_ref,
    dx_ref,
    dl_ref,
    sum_ref,
):
    base = (pl.program_id(0) + start) * count
    i, j = iotas()
    row = lax.broadcasted_iota(jnp.int32, (SEQ, 1), 0)
    for t in range(count):
        x = x_ref[t]
        q, k = x[:, 0:HD], x[:, HD : 2 * HD]
        v, u = x[:, 2 * HD : 3 * HD], x[:, 3 * HD : 4 * HD]
        do = do_ref[0, t].astype(f32) + do_ref[1, t].astype(f32)
        do = (do + (do_ref[2, t].astype(f32) + do_ref[3, t].astype(f32))).astype(bf16)
        do = jnp.where(row < len_ref[base + t], do, jnp.zeros_like(do))
        inv, carry, prob = inv_ref[t], carry_ref[t], prob_ref[t]
        raw, norm, norm_row, beta_row, beta = prepare(u, l_ref[t], i, j)
        gram = jnp.where(i > j, dot_of(u, u, 1, 1) * norm * norm_row, 0.0)
        a = jnp.where(i >= j, dot_of(q, u, 1, 1) * norm_row, 0.0)
        b = jnp.where(i > j, dot_of(u, k, 1, 1) * norm, 0.0)
        m = inv * beta_row
        dv = mul(prob, do, 0, 0, passes=1)
        dprob = dot_of(do, v, 1, 1)
        ds = prob * (dprob - jnp.sum(dprob * prob, axis=1, keepdims=True)) * (HD**-0.5)
        da = jnp.where(i >= j, -mul(ds, carry, 1, 1), 0.0)
        dc = -mul(a, ds, 0, 0)
        dm = mul(dc, b, 1, 1)
        db = jnp.where(i > j, mul(m, dc, 0, 0), 0.0)
        dn = jnp.where(i > j, -mul(mul(inv, dm, 0, 0), m, 1, 1), 0.0)
        dgram = beta * dn
        dbeta = jnp.sum(dm * inv, axis=0, keepdims=True)
        dbeta_col = jnp.sum(dn * gram, axis=1, keepdims=True)
        dbeta = dbeta + jnp.sum(jnp.where(i == j, dbeta_col, 0.0), axis=0, keepdims=True)
        dq = mul(ds, k, passes=1) + mul(da * norm_row, u, passes=1)
        dk = mul(ds, q, 0, 0, passes=1) + mul(db * norm, u, 0, 0, passes=1)
        dw = mul(da, q, 0, 0, passes=1) + mul(db, k, passes=1)
        dw = dw + mul(dgram * norm_row, u, passes=1) + mul(dgram * norm, u, 0, 0, passes=1)
        du = norm * dw - (norm * norm * norm) * raw * jnp.sum(dw * raw, axis=1, keepdims=True)
        dx = jnp.concatenate([dq, dk, dv, du], axis=1)
        dl = dbeta * beta_row * (1.0 - 0.5 * beta_row)
        dx_ref[t] = dx.astype(bf16)
        dl_ref[t] = dl
        total = jnp.sum(dx * x.astype(f32), axis=1, keepdims=True)
        sum_ref[t] = to_row(total, i == j) + dl * l_ref[t]


def block_of(count, *shape):
    return pl.BlockSpec((count,) + shape, lambda g, lens: (g, 0, 0))


def attention_forward(lens, x, logits, count=3):
    pairs = x.shape[0]
    square = jax.ShapeDtypeStruct((pairs, SEQ, SEQ), f32)
    return pl.pallas_call(
        functools.partial(forward_kernel, count),
        out_shape=[jax.ShapeDtypeStruct((pairs, SEQ, HD), bf16), square, square, square],
        grid_spec=pltpu.PrefetchScalarGridSpec(
            num_scalar_prefetch=1,
            grid=(pairs // count,),
            in_specs=[block_of(count, SEQ, 4 * HD), block_of(count, 1, SEQ)],
            out_specs=[block_of(count, SEQ, HD)] + [block_of(count, SEQ, SEQ)] * 3,
        ),
        compiler_params=pltpu.CompilerParams(vmem_limit_bytes=48 << 20),
        cost_estimate=cost(pairs * 1600000000, pairs * 1100000),
    )(lens, x, logits)


def attention_backward(lens, x, logits, inv, carry, prob, do, start, pairs):
    line = jax.ShapeDtypeStruct((pairs, 1, SEQ), f32)

    def from_start(*dims):
        return pl.BlockSpec((1,) + dims, lambda g, lens: (g + start, 0, 0))

    return pl.pallas_call(
        functools.partial(backward_kernel, 1, start),
        out_shape=[jax.ShapeDtypeStruct((pairs, SEQ, 4 * HD), bf16), line, line],
        grid_spec=pltpu.PrefetchScalarGridSpec(
            num_scalar_prefetch=1,
            grid=(pairs,),
            in_specs=[from_start(SEQ, 4 * HD), from_start(1, SEQ)]
            + [from_start(SEQ, SEQ)] * 3
            + [pl.BlockSpec((4, 1, SEQ, HD), lambda g, lens: (0, g + start, 0, 0))],
            out_specs=[block_of(1, SEQ, 4 * HD)] + [block_of(1, 1, SEQ)] * 2,
        ),
        compiler_params=pltpu.CompilerParams(vmem_limit_bytes=48 << 20),
        cost_estimate=cost(pairs * 1400000000, pairs * 1400000),
    )(lens, x, logits, inv, carry, prob, do)


VMEM_LIMIT = 48 << 20
COST_SCALE = 0.001


def shape(*dims, dtype=bf16):
    return jax.ShapeDtypeStruct(dims, dtype)


def rows_block(size, cols):
    return pl.BlockSpec((size, cols), lambda g, *p: (g, 0))


def stack_block(n, size, cols):
    return pl.BlockSpec((n, size, cols), lambda g, *p: (0, g, 0))


def lead_block(size, cols):
    return pl.BlockSpec((1, size, cols), lambda g, *p: (g, 0, 0))


def whole(*dims):
    return pl.BlockSpec(dims, lambda g, *p: (0,) * len(dims))


def cost(flops, moved):
    scale = COST_SCALE
    return pl.CostEstimate(
        flops=int(flops * scale), bytes_accessed=int(moved * scale), transcendentals=0
    )


def project_kernel(n, x_ref, w_ref, misc_ref, a_ref, b_ref, l_ref, r_ref, xg_ref):
    i, j = iotas()
    squares = 0.0
    for k in range(n):
        xf = x_ref[k].astype(f32)
        squares = squares + jnp.sum(xf * xf, axis=1, keepdims=True)
    r = lax.rsqrt(squares * (1.0 / (n * x_ref.shape[2])) + 1e-6)
    acc = 0.0
    logit = 0.0
    for k in range(n):
        gain = misc_ref[k][6:7, :].astype(f32)
        normed = (x_ref[k].astype(f32) * r * gain).astype(bf16)
        xg_ref[k] = normed
        acc = acc + dot_of(normed, w_ref[k], 1, 0)
        logit = logit + dot_of(misc_ref[k], normed, 1, 1)
    out = acc.astype(bf16)
    a_ref[0] = out[:, : 4 * HD]
    b_ref[0] = out[:, 4 * HD :]
    l_ref[0] = logit
    r_ref[0] = to_row(r, i == j)


def project(x, w, misc):
    n, half, part = x.shape
    blocks = half // SEQ
    cols = w.shape[2]
    lines = misc.shape[1]
    return pl.pallas_call(
        functools.partial(project_kernel, n),
        out_shape=[
            shape(blocks, SEQ, 4 * HD),
            shape(blocks, SEQ, 4 * HD),
            shape(blocks, lines, SEQ, dtype=f32),
            shape(blocks, 1, SEQ, dtype=f32),
            shape(n, half, part),
        ],
        grid=(blocks,),
        in_specs=[stack_block(n, SEQ, part), whole(n, part, cols), whole(n, lines, part)],
        out_specs=[
            lead_block(SEQ, 4 * HD),
            lead_block(SEQ, 4 * HD),
            lead_block(lines, SEQ),
            lead_block(1, SEQ),
            stack_block(n, SEQ, part),
        ],
        compiler_params=pltpu.CompilerParams(vmem_limit_bytes=VMEM_LIMIT),
        cost_estimate=cost(2 * half * part * n * cols, 8000000),
    )(x, w, misc)


def ffn_kernel(
    n,
    len_ref,
    side_ref,
    h_ref,
    g_ref,
    wa_ref,
    wb_ref,
    misc_ref,
    n2_ref,
    m_ref,
    d_ref,
    dn_ref,
    sum_ref,
    r_ref,
):
    ff = m_ref.shape[2]
    i, j = iotas()
    row = lax.broadcasted_iota(jnp.int32, (SEQ, 1), 0)
    valid = row < len_ref[pl.program_id(0)]
    squares = 0.0
    for k in range(n):
        hf = h_ref[k].astype(f32)
        squares = squares + jnp.sum(hf * hf, axis=1, keepdims=True)
    r = lax.rsqrt(squares * (1.0 / (n * h_ref.shape[2])) + 1e-6)
    for k in range(n):
        gain = misc_ref[k][7:8, :].astype(f32)
        n2_ref[k] = (h_ref[k].astype(f32) * r * gain).astype(bf16)
    r_ref[...] = r
    both = []
    total = 0.0
    for c, w_ref in enumerate((wa_ref, wb_ref)):
        place = side_ref[0] ^ c
        gate_up = 0.0
        dm = 0.0
        for k in range(n):
            gate_up = gate_up + dot_of(n2_ref[k], w_ref[k, :, : 2 * ff], 1, 0)
            dm = dm + dot_of(g_ref[k], w_ref[k, :, 2 * ff :], 1, 0)
        gate = gate_up[:, :ff]
        up = gate_up[:, ff:]
        sig = 1.0 / (1.0 + jnp.exp(-gate))
        active = gate * sig
        m_ref[place] = jnp.where(valid, active * up, 0.0).astype(bf16)
        dm = jnp.where(valid, dm, 0.0)
        dgate = dm * up * sig * (1.0 + gate * (1.0 - sig))
        dup = dm * active
        total = total + jnp.sum(dgate * gate + dup * up, axis=1, keepdims=True)
        d = jnp.concatenate([dgate, dup], axis=1).astype(bf16)
        d_ref[place] = d
        both.append(d)
    sum_ref[0] = to_row(total, i == j)
    for k in range(n):
        dn = dot_of(both[0], wa_ref[k, :, : 2 * ff], 1, 1)
        dn = dn + dot_of(both[1], wb_ref[k, :, : 2 * ff], 1, 1)
        dn_ref[k] = dn.astype(dn_ref.dtype)


def feed_forward(lens, side, h, g, wa, wb, misc, out_type):
    n, half, part = h.shape
    blocks = half // SEQ
    cols = wa.shape[2]
    ff = cols // 3
    lines = misc.shape[1]
    return pl.pallas_call(
        functools.partial(ffn_kernel, n),
        out_shape=[
            shape(n, half, part),
            shape(2, half, ff),
            shape(2, half, 2 * ff),
            shape(n, half, part, dtype=out_type),
            shape(blocks, 1, SEQ, dtype=f32),
            shape(half, 1, dtype=f32),
        ],
        grid_spec=pltpu.PrefetchScalarGridSpec(
            num_scalar_prefetch=2,
            grid=(blocks,),
            in_specs=[stack_block(n, SEQ, part)] * 2
            + [whole(n, part, cols)] * 2
            + [whole(n, lines, part)],
            out_specs=[
                stack_block(n, SEQ, part),
                stack_block(2, SEQ, ff),
                stack_block(2, SEQ, 2 * ff),
                stack_block(n, SEQ, part),
                lead_block(1, SEQ),
                rows_block(SEQ, 1),
            ],
        ),
        compiler_params=pltpu.CompilerParams(vmem_limit_bytes=VMEM_LIMIT),
        cost_estimate=cost(2 * half * part * n * 10 * ff, 12000000),
    )(lens, side, h, g, wa, wb, misc)


def ffn_out_kernel(n, side_ref, one_ref, two_ref, wa_ref, wb_ref, own_ref, far_ref):
    ff = one_ref.shape[2]
    for m_ref, out_ref in ((one_ref, own_ref), (two_ref, far_ref)):
        first, second = m_ref[side_ref[0]], m_ref[side_ref[0] ^ 1]
        for k in range(n):
            total = dot_of(first, wa_ref[k, :, 2 * ff :], 1, 1)
            total = total + dot_of(second, wb_ref[k, :, 2 * ff :], 1, 1)
            out_ref[k] = total.astype(out_ref.dtype)


def feed_forward_out(side, own, far, wa, wb):
    _, half, ff = own.shape
    n, part, cols = wa.shape
    return pl.pallas_call(
        functools.partial(ffn_out_kernel, n),
        out_shape=[shape(n, half, part, dtype=f32), shape(n, half, part)],
        grid_spec=pltpu.PrefetchScalarGridSpec(
            num_scalar_prefetch=1,
            grid=(half // SEQ,),
            in_specs=[stack_block(2, SEQ, ff)] * 2 + [whole(n, part, cols)] * 2,
            out_specs=[stack_block(n, SEQ, part)] * 2,
        ),
        compiler_params=pltpu.CompilerParams(vmem_limit_bytes=VMEM_LIMIT),
        cost_estimate=cost(8 * half * part * n * ff, 12000000),
    )(side, own, far, wa, wb)


def back_kernel(n, flag_ref, a_ref, b_ref, l_ref, w_ref, misc_ref, out_ref):
    b = b_ref[0]
    b = jnp.where(flag_ref[0] > 0, b, jnp.zeros_like(b))
    d = jnp.concatenate([a_ref[0], b], axis=1)
    line = l_ref[0]
    for k in range(n):
        total = dot_of(d, w_ref[k], 1, 1) + dot_of(line, misc_ref[k], 0, 0)
        out_ref[k] = total.astype(out_ref.dtype)


def project_back(flag, a, start, b, lines, w, misc, out_type):
    n, part, cols = w.shape
    blocks = b.shape[0]
    rows = misc.shape[1]
    return pl.pallas_call(
        functools.partial(back_kernel, n),
        out_shape=shape(n, blocks * SEQ, part, dtype=out_type),
        grid_spec=pltpu.PrefetchScalarGridSpec(
            num_scalar_prefetch=1,
            grid=(blocks,),
            in_specs=[
                pl.BlockSpec((1, SEQ, 4 * HD), lambda g, *p: (g + start, 0, 0)),
                lead_block(SEQ, 4 * HD),
                lead_block(rows, SEQ),
            ]
            + [whole(n, part, cols), whole(n, rows, part)],
            out_specs=stack_block(n, SEQ, part),
        ),
        compiler_params=pltpu.CompilerParams(vmem_limit_bytes=VMEM_LIMIT),
        cost_estimate=cost(2 * blocks * SEQ * part * n * cols, 8000000),
    )(flag, a, b, lines, w, misc)


def weight_call(kernel, idx, picked, rest, cols, flops, flags=0):
    count = idx.shape[0] - flags
    n, half, part = picked[0].shape
    pick = pl.BlockSpec((1, half, part), lambda g, *p: (p[0][g], 0, 0))
    return pl.pallas_call(
        kernel,
        out_shape=shape(count, part, cols),
        grid_spec=pltpu.PrefetchScalarGridSpec(
            num_scalar_prefetch=1,
            grid=(count,),
            in_specs=[pick] * len(picked) + [whole(*x.shape) for x in rest],
            out_specs=lead_block(part, cols),
        ),
        compiler_params=pltpu.CompilerParams(vmem_limit_bytes=VMEM_LIMIT),
        cost_estimate=cost(flops * count, 6000000),
    )(idx, *picked, *rest)


def ffn_weight_kernel(c, idx_ref, n1, n2, g1, g2, d1, d2, m1, m2, out_ref):
    cols = d1.shape[2]
    total = dot_of(n1[0], d1[c], 0, 0) + dot_of(n2[0], d2[c], 0, 0)
    out_ref[0, :, :cols] = total.astype(bf16)
    total = dot_of(g1[0], m1[c], 0, 0) + dot_of(g2[0], m2[c], 0, 0)
    out_ref[0, :, cols:] = total.astype(bf16)


def own_weight_kernel(idx_ref, n1, n2, d, out_ref):
    total = dot_of(n1[0], d[0], 0, 0) + dot_of(n2[0], d[1], 0, 0)
    out_ref[0] = total.astype(bf16)


def shared_weight_kernel(idx_ref, n1, n2, d, l1, l2, out_ref):
    left = jnp.where(idx_ref[idx_ref.shape[0] - 1] == 0, n1[0], n2[0])
    cols = d.shape[1]
    out_ref[0, :, :cols] = dot_of(left, d[...], 0, 0).astype(bf16)
    lines = dot_of(n1[0], l1[...], 0, 1) + dot_of(n2[0], l2[...], 0, 1)
    out_ref[0, :, cols:] = lines.astype(bf16)


def own_head(k):
    return (3 * k + 1) // 2


def shared_head(q):
    return 1 + 3 * q


def head_cols(h):
    return slice(h * HD, (h + 1) * HD)


def mix_kernel(n, half, place_ref, w_ref, o_ref, own_ref, far_ref):
    for p, out_ref in enumerate((own_ref, far_ref)):
        second = place_ref[0] ^ p
        total = 0.0
        for k in range(n):
            ok = o_ref[k, p * half : (p + 1) * half, :]
            total = total + dot_of(ok, w_ref[:, head_cols(own_head(k))], 1, 1)
        for q in range(n // 2):
            one, two = o_ref[2 * q, 2 * half :, :], o_ref[2 * q + 1, 2 * half :, :]
            ob = jnp.where(second == 0, one, two)
            total = total + dot_of(ob, w_ref[:, head_cols(shared_head(q))], 1, 1)
        out_ref[...] = total


def attention_out(place, w_out, o, half):
    n = o.shape[0]
    part, cols = w_out.shape
    return pl.pallas_call(
        functools.partial(mix_kernel, n, half),
        out_shape=[shape(half, part, dtype=f32)] * 2,
        grid_spec=pltpu.PrefetchScalarGridSpec(
            num_scalar_prefetch=1,
            grid=(1,),
            in_specs=[whole(part, cols), whole(*o.shape)],
            out_specs=[whole(half, part)] * 2,
        ),
        compiler_params=pltpu.CompilerParams(vmem_limit_bytes=VMEM_LIMIT),
        cost_estimate=cost(4 * half * part * cols, 4000000),
    )(place, w_out, o)


def unmix_kernel(n, half, place_ref, w_ref, own_ref, far_ref, out_ref):
    place = place_ref[0]
    da = (own_ref[...], far_ref[...])
    for k in range(n):
        w = w_ref[:, head_cols(own_head(k))]
        for p in range(2):
            out_ref[k, p * half : (p + 1) * half, :] = dot_of(da[p], w, 1, 0).astype(bf16)
    for q in range(n // 2):
        w = w_ref[:, head_cols(shared_head(q))]
        both = [dot_of(d, w, 1, 0).astype(bf16) for d in da]
        out_ref[2 * q, 2 * half :, :] = jnp.where(place == 0, both[0], both[1])
        out_ref[2 * q + 1, 2 * half :, :] = jnp.where(place == 0, both[1], both[0])


def attention_out_back(place, w_out, own, far, n):
    half, part = own.shape
    cols = w_out.shape[1]
    return pl.pallas_call(
        functools.partial(unmix_kernel, n, half),
        out_shape=shape(n, 3 * half, HD),
        grid_spec=pltpu.PrefetchScalarGridSpec(
            num_scalar_prefetch=1,
            grid=(1,),
            in_specs=[whole(part, cols), whole(half, part), whole(half, part)],
            out_specs=whole(n, 3 * half, HD),
        ),
        compiler_params=pltpu.CompilerParams(vmem_limit_bytes=VMEM_LIMIT),
        cost_estimate=cost(4 * half * part * cols, 4000000),
    )(place, w_out, own, far)


def out_grad_kernel(n, half, place_ref, own_ref, far_ref, o_ref, out_ref):
    place = place_ref[0]
    da = (own_ref[...], far_ref[...])
    for k in range(n):
        total = dot_of(da[0], o_ref[k, :half, :], 0, 0)
        total = total + dot_of(da[1], o_ref[k, half : 2 * half, :], 0, 0)
        out_ref[:, head_cols(own_head(k))] = total.astype(bf16)
    for q in range(n // 2):
        one, two = o_ref[2 * q, 2 * half :, :], o_ref[2 * q + 1, 2 * half :, :]
        total = dot_of(da[0], jnp.where(place == 0, one, two), 0, 0)
        total = total + dot_of(da[1], jnp.where(place == 0, two, one), 0, 0)
        out_ref[:, head_cols(shared_head(q))] = total.astype(bf16)


def out_gradient(place, own, far, o, cols):
    n = o.shape[0]
    half, part = own.shape
    return pl.pallas_call(
        functools.partial(out_grad_kernel, n, half),
        out_shape=shape(part, cols),
        grid_spec=pltpu.PrefetchScalarGridSpec(
            num_scalar_prefetch=1,
            grid=(1,),
            in_specs=[whole(half, part), whole(half, part), whole(*o.shape)],
            out_specs=whole(part, cols),
        ),
        compiler_params=pltpu.CompilerParams(vmem_limit_bytes=VMEM_LIMIT),
        cost_estimate=cost(4 * half * part * cols, 4000000),
    )(place, own, far, o)


def swap(x, axis, size, k):
    return lax.ppermute(x, axis, [(n, n ^ k) for n in range(size)])


def shift_rows(x, start, size):
    return lax.dynamic_slice_in_dim(x, start, size, axis=0)


def exchange(x, axis):
    return lax.all_to_all(x, axis, split_axis=0, concat_axis=0, tiled=True)


def to_all(x, axis, n):
    return exchange(jnp.broadcast_to(x[None], (n,) + x.shape), axis)


def after(x, *others):
    return lax.optimization_barrier((x,) + others)[0]


def per_device(
    dp_size,
    wid_size,
    tokens,
    cotangent,
    lengths,
    w_project,
    w_beta,
    w_out,
    w_gate_up,
    w_down,
    gain_attn,
    gain_ffn,
):
    wid = lax.axis_index("wid")
    hid = lax.axis_index("hid")
    dp = lax.axis_index("dp")
    ws = range(wid_size)
    rows, part = tokens.shape
    half = rows // 2
    width = part * wid_size
    ff = w_down.shape[1] // wid_size
    heads = w_beta.shape[1]
    per_half = half // SEQ

    def hid_swap(x):
        return swap(x, "hid", 2, 1)

    half_b = (wid & 1) ^ hid
    my_head = own_head(wid)
    my_shared = shared_head(wid // 2)

    x_own = shift_rows(tokens, hid * half, half)
    g_own = shift_rows(cotangent, hid * half, half)

    spare = jnp.zeros((16 - heads - 3, part), bf16)
    length_line = jnp.broadcast_to(lengths.astype(bf16)[:, None], (1, part))
    misc_here = jnp.concatenate(
        [w_beta.T, gain_attn[None], gain_ffn[None], length_line, spare], axis=0
    )
    gathered = to_all(jnp.concatenate([x_own, misc_here], axis=0), "wid", wid_size)
    xs_own, misc = gathered[:, :half], gathered[:, half:]
    xs_far = hid_swap(xs_own)
    len_abs = misc[:, heads + 2, 0].astype(jnp.int32)

    def heads_for(w):
        a = w_project[:, :, head_cols(own_head(w))].reshape(part, 4 * HD)
        b = w_project[:, :, head_cols(shared_head(w // 2))].reshape(part, 4 * HD)
        return jnp.concatenate([a, b], axis=1)

    proj_w = exchange(jnp.stack([heads_for(w) for w in ws]), "wid")

    side = dp & 1
    ffh = ff // 2

    def ffn_for(w):
        at = w * ff + side * ffh
        cut = lax.dynamic_slice_in_dim(w_gate_up, at, ffh, axis=2).reshape(part, 2 * ffh)
        return jnp.concatenate([cut, lax.dynamic_slice_in_dim(w_down, at, ffh, axis=1)], axis=1)

    ffn_own = exchange(after(jnp.stack([ffn_for(w) for w in ws]), proj_w), "wid")
    ffn_other = swap(ffn_own, "dp", dp_size, 1)
    side = side.astype(jnp.int32)[None]

    def lens_of(place):
        return lax.dynamic_slice_in_dim(len_abs, place * per_half, per_half)

    lens_own, lens_far = lens_of(hid), lens_of(1 - hid)
    lens = jnp.concatenate([lens_own, lens_far, lens_of(wid & 1)])
    slot = jnp.arange(SEQ, dtype=jnp.int32)
    valid_half = (slot[None] < lens_own[:, None]).astype(f32).reshape(half, 1)

    a_own, b_own, l_own, r_own, n1_own = project(xs_own, proj_w, misc)
    a_far, b_far, l_far, r_far, n1_far = project(xs_far, proj_w, misc)

    def pick_b(own, far):
        return jnp.where(half_b == 0, own, far)

    pairs = jnp.concatenate([a_own, a_far, pick_b(b_own, b_far)], axis=0)

    def line_of(lines, h):
        return lax.dynamic_slice_in_dim(lines, h, 1, axis=1)

    logit_pairs = jnp.concatenate(
        [
            line_of(l_own, my_head),
            line_of(l_far, my_head),
            line_of(pick_b(l_own, l_far), my_shared),
        ],
        axis=0,
    )
    attended, inv, carry, prob = attention_forward(lens, pairs, logit_pairs)
    o_all = to_all(after(attended, ffn_own).reshape(-1, HD), "wid", wid_size)
    place = hid.astype(jnp.int32)[None]
    attn_own, attn_far = attention_out(place, w_out, o_all, half)
    hidden = x_own.astype(f32) + attn_own + hid_swap(attn_far)

    gain_one = gain_attn[None].astype(f32)
    gain_two = gain_ffn[None].astype(f32)
    hs_own = to_all(hidden.astype(bf16), "wid", wid_size)
    hs_far = hid_swap(hs_own)
    gs_own = exchange(
        after(jnp.broadcast_to(g_own[None], (wid_size,) + g_own.shape), hs_own, ffn_other), "wid"
    )
    gs_far = hid_swap(gs_own)
    n2_own, m_own, d_own, dn_own, s_own, r2_own = feed_forward(
        lens_own, side, hs_own, gs_own, ffn_own, ffn_other, misc, f32
    )
    n2_far, m_far, d_far, dn_far, s_far, r2_far = feed_forward(
        lens_far, side, hs_far, gs_far, ffn_own, ffn_other, misc, bf16
    )

    def partial(own, far):
        return (own + hid_swap(far).astype(f32)).astype(bf16)

    def line_sum(own, far, late):
        here = (own + hid_swap(far)).reshape(-1, 128)
        others = [swap(here, "wid", wid_size, k) for k in range(1, wid_size)]
        others = lax.optimization_barrier((*others, late))[:-1]
        total = here + sum(others)
        return total.reshape(-1, 1) * (1.0 / width)

    dn_here = partial(dn_own, dn_far)
    dn_got = exchange(dn_here, "wid")
    mean_two = line_sum(s_own, s_far, dn_got)
    grad_normed_two = jnp.sum(dn_got.astype(f32), axis=0)

    chunk = width // dp_size
    direct = dp_size == wid_size
    sub = chunk // wid_size

    def dp_pieces(make, odd_first):
        ts = range(1 if odd_first else 0, dp_size, 2)
        if direct:
            return make(jnp.stack([dp ^ t for t in ts]).astype(jnp.int32))
        full = make(jnp.arange(wid_size, dtype=jnp.int32)).reshape(width, -1)
        return jnp.stack([shift_rows(full, (dp ^ t) * chunk, chunk) for t in ts])

    def dp_send(held, k=2):
        return held[0::2], swap(held[1::2].astype(bf16), "dp", dp_size, k)

    def dp_take(keep, got, k=2):
        held = keep + got.astype(f32)
        while held.shape[0] > 1:
            k *= 2
            keep, got = dp_send(held, k)
            held = keep + got.astype(f32)
        return held[0]

    def dp_sum(pieces, *late):
        odd, even = jnp.stack(pieces[1::2]), jnp.stack(pieces[0::2])
        got = after(swap(odd.astype(bf16), "dp", dp_size, 1), *late)
        return dp_take(*dp_send(even.astype(f32) + got.astype(f32)))

    def to_rows(x):
        return exchange(x.astype(bf16).reshape(wid_size, sub, -1), "wid")

    d_then = after(d_own, dn_here)

    def ffn_weights(c, then):
        def make(idx):
            return weight_call(
                functools.partial(ffn_weight_kernel, c),
                idx,
                (n2_own, n2_far, gs_own, gs_far),
                (then, d_far, m_own, m_far),
                3 * ffh,
                12 * half * part * ffh,
            )

        return make

    odd_one = dp_pieces(ffn_weights(0, d_then), True)
    got_one = swap(odd_one, "dp", dp_size, 1)
    d_then = after(d_then, odd_one)
    odd_two = dp_pieces(ffn_weights(1, d_then), True)
    got_two = swap(odd_two, "dp", dp_size, 1)
    d_then = after(d_then, odd_two)
    even_one = dp_pieces(ffn_weights(0, d_then), False)
    even_two = dp_pieces(ffn_weights(1, d_then), False)

    grad_half = g_own.astype(f32) * valid_half
    grad_hidden = grad_half + r2_own * (
        grad_normed_two * gain_two - r2_own * hidden * mean_two
    )
    gain_two_part = jnp.sum(grad_normed_two * hidden * r2_own, axis=0)
    da_own = after(grad_hidden.astype(bf16), even_one, even_two)
    da_far = hid_swap(da_own)
    do_here = attention_out_back(place, w_out, da_own, da_far, wid_size)
    do_pieces = exchange(do_here, "wid")
    ffn_own_out, ffn_far_out = feed_forward_out(
        side, after(m_own, do_here, got_one), m_far, ffn_own, ffn_other
    )
    g_out = out_gradient(place, after(da_own, do_here, got_one), da_far, o_all, w_out.shape[1])
    do_got = do_pieces.reshape(wid_size, -1, SEQ, HD)
    got_one = after(got_one, do_got)
    held_one = even_one.astype(f32) + got_one.astype(f32)
    keep_one, next_one = dp_send(held_one)

    pairs_a, lines_a, sums_a = attention_backward(
        lens, pairs, logit_pairs, inv, carry, prob, after(do_got, held_one, ffn_far_out), 0, 2 * per_half
    )

    head_iota = lax.broadcasted_iota(jnp.int32, (1, 16, 1), 1)
    right_own = pairs_a.reshape(2, half, 4 * HD)

    def own_weights(idx):
        return weight_call(
            own_weight_kernel,
            idx,
            (n1_own, n1_far),
            (right_own,),
            4 * HD,
            4 * half * part * 4 * HD,
        )

    own_odd = dp_pieces(own_weights, True)
    own_got = swap(own_odd, "dp", dp_size, 1)
    pairs_b, lines_b, sums_b = attention_backward(
        lens, pairs, logit_pairs, inv, carry, prob, after(do_got, own_odd), 2 * per_half, per_half
    )

    def spread(a, b, at):
        own = a[at * per_half : (at + 1) * per_half]
        return own, jnp.where(half_b == at, b, 0.0)

    def lines_at(at):
        own, shared = spread(lines_a, lines_b, at)
        own = jnp.where(head_iota == my_head, own, 0.0)
        shared = jnp.where(head_iota == my_shared, shared, 0.0)
        return (own + shared).astype(bf16)

    def flat_lines(x):
        flat = jnp.swapaxes(x, 0, 1).reshape(16, half)
        return jnp.concatenate([flat, jnp.zeros((128 - 16, half), bf16)], axis=0)

    lines_own, lines_far = lines_at(0), lines_at(1)
    flat_own, flat_far = flat_lines(lines_own), flat_lines(lines_far)
    right_shared = after(pairs_b, next_one).reshape(half, 4 * HD)

    def shared_weights(idx):
        return weight_call(
            shared_weight_kernel,
            jnp.concatenate([idx, half_b.astype(jnp.int32)[None]]),
            (n1_own, n1_far),
            (right_shared, flat_own, flat_far),
            5 * HD,
            2 * half * part * 5 * HD,
            1,
        )

    shared_odd = dp_pieces(shared_weights, True)
    shared_got = swap(shared_odd, "dp", dp_size, 1)
    right_own = after(right_own, own_got)
    right_shared = after(right_shared, own_got)
    flags = [(half_b == p).astype(jnp.int32)[None] for p in range(2)]
    got_two = after(got_two, shared_odd)
    held_two = even_two.astype(f32) + got_two.astype(f32)
    keep_two, next_two = dp_send(held_two)
    back_b = after(pairs_b, shared_odd, held_two, own_got)
    dn1_far = project_back(flags[1], pairs_a, per_half, back_b, lines_far, proj_w, misc, bf16)
    own_even = dp_pieces(own_weights, False)
    keep_own, next_own = dp_send(own_even.astype(f32) + own_got.astype(f32))
    shared_even = dp_pieces(shared_weights, False)
    keep_shared, next_shared = dp_send(shared_even.astype(f32) + shared_got.astype(f32))
    back_b = after(back_b, next_two, keep_own, shared_got)
    dn1_own = project_back(flags[0], pairs_a, 0, back_b, lines_own, proj_w, misc, f32)
    dn1_here = after(partial(dn1_own, dn1_far), next_own, keep_shared)
    dn1_got = exchange(dn1_here, "wid")
    ffn_far_out = after(ffn_far_out, pairs_b)
    ffn_here = after(partial(ffn_own_out, ffn_far_out), dn1_got)
    ffn_back = exchange(ffn_here, "wid")
    next_shared = after(next_shared, dn1_got)
    sums = [sum(spread(sums_a, sums_b, p)) for p in range(2)]
    mean_one = line_sum(*sums, dn1_got)
    grad_normed_one = jnp.sum(dn1_got.astype(f32), axis=0)
    ffn = jnp.sum(ffn_back.astype(f32), axis=0)

    source = x_own.astype(f32)
    r1_half = r_own.reshape(half, 1)
    gain_one_part = jnp.sum(grad_normed_one * source * r1_half, axis=0)
    input_half = grad_hidden + r1_half * (
        grad_normed_one * gain_one - r1_half * source * mean_one
    )

    def whole_rows(x):
        other = hid_swap(x)
        return jnp.concatenate(
            [jnp.where(hid == 0, x, other), jnp.where(hid == 0, other, x)], axis=0
        )

    parts = [
        dp_take(keep_one, next_one),
        dp_take(keep_two, next_two),
        dp_take(keep_own, next_own),
        dp_take(keep_shared, next_shared),
    ]
    g_all = jnp.concatenate(parts, axis=1).astype(bf16)
    input_grad = whole_rows(after(input_half.astype(bf16), g_all))
    output = whole_rows(after(((hidden + ffn) * valid_half).astype(bf16), g_all))

    fine = part // dp_size
    to_place = [
        (c * wid_size + w, w * dp_size + c) for c in range(dp_size) for w in range(wid_size)
    ]

    def dp_fine(x, *late):
        return dp_sum([shift_rows(x, (dp ^ t) * fine, fine) for t in range(dp_size)], *late)

    out_out = lax.ppermute(dp_fine(g_out, g_all), ("dp", "wid"), to_place)
    gain_part = after(jnp.stack([gain_one_part, gain_two_part], axis=1), g_all)
    gain_part = gain_part + hid_swap(gain_part)
    gain_sum = lax.ppermute(dp_fine(gain_part), ("dp", "wid"), to_place)

    all_rows = to_rows(after(g_all, ffn_back))
    got = all_rows[:, :, : 3 * ff].reshape(wid_size, sub, 2, 3 * ffh)
    pieces = [got[w, :, c] for w in ws for c in range(2)]
    gate, up, down = (
        jnp.concatenate([p[:, k * ffh : (k + 1) * ffh] for p in pieces], axis=1) for k in range(3)
    )
    out_gate_up = jnp.stack([gate, up], axis=1).astype(f32)
    out_down = down.astype(f32)

    got = all_rows[:, :, 3 * ff :].astype(f32)
    a = [got[w, :, : 4 * HD] for w in ws]
    b = [got[w, :, 4 * HD : 8 * HD] for w in ws]
    proj_rows = [a[0], b[0] + b[1], a[1], a[2], b[2] + b[3], a[3]]
    out_project = jnp.concatenate([p.reshape(sub, 4, HD) for p in proj_rows], axis=2)
    out_beta = jnp.sum(got[:, :, 8 * HD : 8 * HD + heads], axis=0)


    return (
        output,
        input_grad,
        out_project,
        out_beta,
        out_out,
        out_gate_up,
        out_down,
        gain_sum[:, 0],
        gain_sum[:, 1],
    )


def solution(mesh):
    return jax.shard_map(
        functools.partial(per_device, mesh.shape["dp"], mesh.shape["wid"]),
        mesh=mesh,
        in_specs=(
            P("dp", "wid"),
            P("dp", "wid"),
            P(("dp", "wid")),
            P("wid", None, "hid"),
            P("wid", "hid"),
            P("wid", "hid"),
            P("wid", None, "hid"),
            P("wid", "hid"),
            P("wid"),
            P("wid"),
        ),
        out_specs=(
            P("dp", "wid"),
            P("dp", "wid"),
            P(("dp", "wid"), None, "hid"),
            P(("dp", "wid"), "hid"),
            P(("dp", "wid"), "hid"),
            P(("dp", "wid"), None, "hid"),
            P(("dp", "wid"), "hid"),
            P(("dp", "wid")),
            P(("dp", "wid")),
        ),
        check_vma=False,
    )
```

```python
import functools

import jax
import jax.numpy as jnp
from jax import lax
from jax.experimental import pallas as pl
from jax.experimental.pallas import tpu as pltpu
from jax.sharding import PartitionSpec as P

f32 = jnp.float32
bf16 = jnp.bfloat16

SEQ = 256
HD = 128


def dot_of(a, b, ca, cb):
    return lax.dot_general(a, b, (((ca,), (cb,)), ((), ())), preferred_element_type=f32)


def halves_of(a):
    high = a.astype(bf16)
    return high, (a - high.astype(f32)).astype(bf16)


def mul(a, b, ca=1, cb=0, passes=3):
    if passes == 1:
        return dot_of(a.astype(bf16), b.astype(bf16), ca, cb)
    if a.dtype == bf16:
        bh, bl = halves_of(b)
        return dot_of(a, bh, ca, cb) + dot_of(a, bl, ca, cb)
    if b.dtype == bf16:
        ah, al = halves_of(a)
        return dot_of(ah, b, ca, cb) + dot_of(al, b, ca, cb)
    ah, al = halves_of(a)
    bh, bl = halves_of(b)
    return dot_of(ah, bh, ca, cb) + (dot_of(ah, bl, ca, cb) + dot_of(al, bh, ca, cb))


def iotas():
    rows = lax.broadcasted_iota(jnp.int32, (SEQ, SEQ), 0)
    cols = lax.broadcasted_iota(jnp.int32, (SEQ, SEQ), 1)
    return rows, cols


def prepare(raw, logit_row, i, j):
    eye = i == j
    raw_f = raw.astype(f32)
    norm = lax.rsqrt(jnp.sum(raw_f * raw_f, axis=1, keepdims=True) + 1e-6)
    norm_row = jnp.sum(jnp.where(eye, norm, 0.0), axis=0, keepdims=True)
    beta_row = 2.0 / (1.0 + jnp.exp(-logit_row))
    beta = jnp.sum(jnp.where(eye, beta_row, 0.0), axis=1, keepdims=True)
    return raw_f, norm, norm_row, beta_row, beta


def inverses(lowers, i, j):
    eye = jnp.where(i == j, 1.0, 0.0)
    first = ((i >> 1) == (j >> 1)) & (i > j)
    inv = [eye - jnp.where(first, n, 0.0) for n in lowers]
    s = 1
    while (1 << s) < SEQ:
        mask = ((i >> (s + 1)) == (j >> (s + 1))) & ((i >> s) > (j >> s))
        mids = [mul(d, jnp.where(mask, n, 0.0)) for d, n in zip(inv, lowers)]
        inv = [d - mul(x, d) for d, x in zip(inv, mids)]
        s += 1
    return inv


def forward_kernel(count, len_ref, x_ref, l_ref, o_ref, inv_ref, carry_ref, prob_ref):
    base = pl.program_id(0) * count
    i, j = iotas()
    row = lax.broadcasted_iota(jnp.int32, (SEQ, 1), 0)
    xs = [x_ref[t] for t in range(count)]
    qs = [x[:, 0:HD] for x in xs]
    ks = [x[:, HD : 2 * HD] for x in xs]
    vs = [x[:, 2 * HD : 3 * HD] for x in xs]
    us = [x[:, 3 * HD : 4 * HD] for x in xs]
    pre = [prepare(us[t], l_ref[t], i, j) for t in range(count)]
    lowers = [
        p[4] * jnp.where(i > j, dot_of(u, u, 1, 1) * p[1] * p[2], 0.0) for u, p in zip(us, pre)
    ]
    inv = inverses(lowers, i, j)
    bs = [jnp.where(i > j, dot_of(u, k, 1, 1) * p[1], 0.0) for u, k, p in zip(us, ks, pre)]
    carries = [mul(d * p[3], b) for d, p, b in zip(inv, pre, bs)]
    as_ = [jnp.where(i >= j, dot_of(q, u, 1, 1) * p[2], 0.0) for q, u, p in zip(qs, us, pre)]
    scores = [
        (dot_of(q, k, 1, 1) - mul(a, c)) * (HD**-0.5) for q, k, a, c in zip(qs, ks, as_, carries)
    ]
    for t in range(count):
        length = len_ref[base + t]
        score = jnp.where((j <= i) & (j < length), scores[t], -1e30)
        weight = jnp.exp(score - jnp.max(score, axis=1, keepdims=True))
        prob = weight * (1.0 / jnp.sum(weight, axis=1, keepdims=True))
        out = jnp.where(row < length, mul(prob, vs[t], passes=1), 0.0)
        o_ref[t] = out.astype(bf16)
        inv_ref[t] = inv[t]
        carry_ref[t] = carries[t]
        prob_ref[t] = prob


def to_row(col, eye):
    return jnp.sum(jnp.where(eye, col, 0.0), axis=0, keepdims=True)


def backward_kernel(
    count,
    start,
    len_ref,
    x_ref,
    l_ref,
    inv_ref,
    carry_ref,
    prob_ref,
    do_ref,
    dx_ref,
    dl_ref,
    sum_ref,
):
    base = (pl.program_id(0) + start) * count
    i, j = iotas()
    row = lax.broadcasted_iota(jnp.int32, (SEQ, 1), 0)
    for t in range(count):
        x = x_ref[t]
        q, k = x[:, 0:HD], x[:, HD : 2 * HD]
        v, u = x[:, 2 * HD : 3 * HD], x[:, 3 * HD : 4 * HD]
        do = do_ref[0, t].astype(f32) + do_ref[1, t].astype(f32)
        do = (do + (do_ref[2, t].astype(f32) + do_ref[3, t].astype(f32))).astype(bf16)
        do = jnp.where(row < len_ref[base + t], do, jnp.zeros_like(do))
        inv, carry, prob = inv_ref[t], carry_ref[t], prob_ref[t]
        raw, norm, norm_row, beta_row, beta = prepare(u, l_ref[t], i, j)
        gram = jnp.where(i > j, dot_of(u, u, 1, 1) * norm * norm_row, 0.0)
        a = jnp.where(i >= j, dot_of(q, u, 1, 1) * norm_row, 0.0)
        b = jnp.where(i > j, dot_of(u, k, 1, 1) * norm, 0.0)
        m = inv * beta_row
        dv = mul(prob, do, 0, 0, passes=1)
        dprob = dot_of(do, v, 1, 1)
        ds = prob * (dprob - jnp.sum(dprob * prob, axis=1, keepdims=True)) * (HD**-0.5)
        da = jnp.where(i >= j, -mul(ds, carry, 1, 1), 0.0)
        dc = -mul(a, ds, 0, 0)
        dm = mul(dc, b, 1, 1)
        db = jnp.where(i > j, mul(m, dc, 0, 0), 0.0)
        dn = jnp.where(i > j, -mul(mul(inv, dm, 0, 0), m, 1, 1), 0.0)
        dgram = beta * dn
        dbeta = jnp.sum(dm * inv, axis=0, keepdims=True)
        dbeta_col = jnp.sum(dn * gram, axis=1, keepdims=True)
        dbeta = dbeta + jnp.sum(jnp.where(i == j, dbeta_col, 0.0), axis=0, keepdims=True)
        dq = mul(ds, k, passes=1) + mul(da * norm_row, u, passes=1)
        dk = mul(ds, q, 0, 0, passes=1) + mul(db * norm, u, 0, 0, passes=1)
        dw = mul(da, q, 0, 0, passes=1) + mul(db, k, passes=1)
        dw = dw + mul(dgram * norm_row, u, passes=1) + mul(dgram * norm, u, 0, 0, passes=1)
        du = norm * dw - (norm * norm * norm) * raw * jnp.sum(dw * raw, axis=1, keepdims=True)
        dx = jnp.concatenate([dq, dk, dv, du], axis=1)
        dl = dbeta * beta_row * (1.0 - 0.5 * beta_row)
        dx_ref[t] = dx.astype(bf16)
        dl_ref[t] = dl
        total = jnp.sum(dx * x.astype(f32), axis=1, keepdims=True)
        sum_ref[t] = to_row(total, i == j) + dl * l_ref[t]


def block_of(count, *shape):
    return pl.BlockSpec((count,) + shape, lambda g, lens: (g, 0, 0))


def attention_forward(lens, x, logits, count=3):
    pairs = x.shape[0]
    square = jax.ShapeDtypeStruct((pairs, SEQ, SEQ), f32)
    return pl.pallas_call(
        functools.partial(forward_kernel, count),
        out_shape=[jax.ShapeDtypeStruct((pairs, SEQ, HD), bf16), square, square, square],
        grid_spec=pltpu.PrefetchScalarGridSpec(
            num_scalar_prefetch=1,
            grid=(pairs // count,),
            in_specs=[block_of(count, SEQ, 4 * HD), block_of(count, 1, SEQ)],
            out_specs=[block_of(count, SEQ, HD)] + [block_of(count, SEQ, SEQ)] * 3,
        ),
        compiler_params=pltpu.CompilerParams(vmem_limit_bytes=48 << 20),
        cost_estimate=cost(pairs * 1600000000, pairs * 1100000),
    )(lens, x, logits)


def attention_backward(lens, x, logits, inv, carry, prob, do, start, pairs):
    line = jax.ShapeDtypeStruct((pairs, 1, SEQ), f32)

    def from_start(*dims):
        return pl.BlockSpec((1,) + dims, lambda g, lens: (g + start, 0, 0))

    return pl.pallas_call(
        functools.partial(backward_kernel, 1, start),
        out_shape=[jax.ShapeDtypeStruct((pairs, SEQ, 4 * HD), bf16), line, line],
        grid_spec=pltpu.PrefetchScalarGridSpec(
            num_scalar_prefetch=1,
            grid=(pairs,),
            in_specs=[from_start(SEQ, 4 * HD), from_start(1, SEQ)]
            + [from_start(SEQ, SEQ)] * 3
            + [pl.BlockSpec((4, 1, SEQ, HD), lambda g, lens: (0, g + start, 0, 0))],
            out_specs=[block_of(1, SEQ, 4 * HD)] + [block_of(1, 1, SEQ)] * 2,
        ),
        compiler_params=pltpu.CompilerParams(vmem_limit_bytes=48 << 20),
        cost_estimate=cost(pairs * 1400000000, pairs * 1400000),
    )(lens, x, logits, inv, carry, prob, do)


VMEM_LIMIT = 48 << 20
COST_SCALE = 0.001


def shape(*dims, dtype=bf16):
    return jax.ShapeDtypeStruct(dims, dtype)


def rows_block(size, cols):
    return pl.BlockSpec((size, cols), lambda g, *p: (g, 0))


def stack_block(n, size, cols):
    return pl.BlockSpec((n, size, cols), lambda g, *p: (0, g, 0))


def lead_block(size, cols):
    return pl.BlockSpec((1, size, cols), lambda g, *p: (g, 0, 0))


def whole(*dims):
    return pl.BlockSpec(dims, lambda g, *p: (0,) * len(dims))


def cost(flops, moved):
    scale = COST_SCALE
    return pl.CostEstimate(
        flops=int(flops * scale), bytes_accessed=int(moved * scale), transcendentals=0
    )


def project_kernel(n, x_ref, w_ref, misc_ref, a_ref, b_ref, l_ref, r_ref, xg_ref):
    i, j = iotas()
    squares = 0.0
    for k in range(n):
        xf = x_ref[k].astype(f32)
        squares = squares + jnp.sum(xf * xf, axis=1, keepdims=True)
    r = lax.rsqrt(squares * (1.0 / (n * x_ref.shape[2])) + 1e-6)
    acc = 0.0
    logit = 0.0
    for k in range(n):
        gain = misc_ref[k][6:7, :].astype(f32)
        normed = (x_ref[k].astype(f32) * r * gain).astype(bf16)
        xg_ref[k] = normed
        acc = acc + dot_of(normed, w_ref[k], 1, 0)
        logit = logit + dot_of(misc_ref[k], normed, 1, 1)
    out = acc.astype(bf16)
    a_ref[0] = out[:, : 4 * HD]
    b_ref[0] = out[:, 4 * HD :]
    l_ref[0] = logit
    r_ref[0] = to_row(r, i == j)


def project(x, w, misc):
    n, half, part = x.shape
    blocks = half // SEQ
    cols = w.shape[2]
    lines = misc.shape[1]
    return pl.pallas_call(
        functools.partial(project_kernel, n),
        out_shape=[
            shape(blocks, SEQ, 4 * HD),
            shape(blocks, SEQ, 4 * HD),
            shape(blocks, lines, SEQ, dtype=f32),
            shape(blocks, 1, SEQ, dtype=f32),
            shape(n, half, part),
        ],
        grid=(blocks,),
        in_specs=[stack_block(n, SEQ, part), whole(n, part, cols), whole(n, lines, part)],
        out_specs=[
            lead_block(SEQ, 4 * HD),
            lead_block(SEQ, 4 * HD),
            lead_block(lines, SEQ),
            lead_block(1, SEQ),
            stack_block(n, SEQ, part),
        ],
        compiler_params=pltpu.CompilerParams(vmem_limit_bytes=VMEM_LIMIT),
        cost_estimate=cost(2 * half * part * n * cols, 8000000),
    )(x, w, misc)


def ffn_kernel(
    n,
    len_ref,
    side_ref,
    h_ref,
    g_ref,
    wa_ref,
    wb_ref,
    misc_ref,
    n2_ref,
    m_ref,
    d_ref,
    dn_ref,
    sum_ref,
    r_ref,
):
    ff = m_ref.shape[2]
    i, j = iotas()
    row = lax.broadcasted_iota(jnp.int32, (SEQ, 1), 0)
    valid = row < len_ref[pl.program_id(0)]
    squares = 0.0
    for k in range(n):
        hf = h_ref[k].astype(f32)
        squares = squares + jnp.sum(hf * hf, axis=1, keepdims=True)
    r = lax.rsqrt(squares * (1.0 / (n * h_ref.shape[2])) + 1e-6)
    for k in range(n):
        gain = misc_ref[k][7:8, :].astype(f32)
        n2_ref[k] = (h_ref[k].astype(f32) * r * gain).astype(bf16)
    r_ref[...] = r
    both = []
    total = 0.0
    for c, w_ref in enumerate((wa_ref, wb_ref)):
        place = side_ref[0] ^ c
        gate_up = 0.0
        dm = 0.0
        for k in range(n):
            gate_up = gate_up + dot_of(n2_ref[k], w_ref[k, :, : 2 * ff], 1, 0)
            dm = dm + dot_of(g_ref[k], w_ref[k, :, 2 * ff :], 1, 0)
        gate = gate_up[:, :ff]
        up = gate_up[:, ff:]
        sig = 1.0 / (1.0 + jnp.exp(-gate))
        active = gate * sig
        m_ref[place] = jnp.where(valid, active * up, 0.0).astype(bf16)
        dm = jnp.where(valid, dm, 0.0)
        dgate = dm * up * sig * (1.0 + gate * (1.0 - sig))
        dup = dm * active
        total = total + jnp.sum(dgate * gate + dup * up, axis=1, keepdims=True)
        d = jnp.concatenate([dgate, dup], axis=1).astype(bf16)
        d_ref[place] = d
        both.append(d)
    sum_ref[0] = to_row(total, i == j)
    for k in range(n):
        dn = dot_of(both[0], wa_ref[k, :, : 2 * ff], 1, 1)
        dn = dn + dot_of(both[1], wb_ref[k, :, : 2 * ff], 1, 1)
        dn_ref[k] = dn.astype(dn_ref.dtype)


def feed_forward(lens, side, h, g, wa, wb, misc, out_type):
    n, half, part = h.shape
    blocks = half // SEQ
    cols = wa.shape[2]
    ff = cols // 3
    lines = misc.shape[1]
    return pl.pallas_call(
        functools.partial(ffn_kernel, n),
        out_shape=[
            shape(n, half, part),
            shape(2, half, ff),
            shape(2, half, 2 * ff),
            shape(n, half, part, dtype=out_type),
            shape(blocks, 1, SEQ, dtype=f32),
            shape(half, 1, dtype=f32),
        ],
        grid_spec=pltpu.PrefetchScalarGridSpec(
            num_scalar_prefetch=2,
            grid=(blocks,),
            in_specs=[stack_block(n, SEQ, part)] * 2
            + [whole(n, part, cols)] * 2
            + [whole(n, lines, part)],
            out_specs=[
                stack_block(n, SEQ, part),
                stack_block(2, SEQ, ff),
                stack_block(2, SEQ, 2 * ff),
                stack_block(n, SEQ, part),
                lead_block(1, SEQ),
                rows_block(SEQ, 1),
            ],
        ),
        compiler_params=pltpu.CompilerParams(vmem_limit_bytes=VMEM_LIMIT),
        cost_estimate=cost(2 * half * part * n * 10 * ff, 12000000),
    )(lens, side, h, g, wa, wb, misc)


def ffn_out_kernel(n, side_ref, one_ref, two_ref, wa_ref, wb_ref, own_ref, far_ref):
    ff = one_ref.shape[2]
    for m_ref, out_ref in ((one_ref, own_ref), (two_ref, far_ref)):
        first, second = m_ref[side_ref[0]], m_ref[side_ref[0] ^ 1]
        for k in range(n):
            total = dot_of(first, wa_ref[k, :, 2 * ff :], 1, 1)
            total = total + dot_of(second, wb_ref[k, :, 2 * ff :], 1, 1)
            out_ref[k] = total.astype(out_ref.dtype)


def feed_forward_out(side, own, far, wa, wb):
    _, half, ff = own.shape
    n, part, cols = wa.shape
    return pl.pallas_call(
        functools.partial(ffn_out_kernel, n),
        out_shape=[shape(n, half, part, dtype=f32), shape(n, half, part)],
        grid_spec=pltpu.PrefetchScalarGridSpec(
            num_scalar_prefetch=1,
            grid=(half // SEQ,),
            in_specs=[stack_block(2, SEQ, ff)] * 2 + [whole(n, part, cols)] * 2,
            out_specs=[stack_block(n, SEQ, part)] * 2,
        ),
        compiler_params=pltpu.CompilerParams(vmem_limit_bytes=VMEM_LIMIT),
        cost_estimate=cost(8 * half * part * n * ff, 12000000),
    )(side, own, far, wa, wb)


def back_kernel(n, flag_ref, a_ref, b_ref, l_ref, w_ref, misc_ref, out_ref):
    b = b_ref[0]
    b = jnp.where(flag_ref[0] > 0, b, jnp.zeros_like(b))
    d = jnp.concatenate([a_ref[0], b], axis=1)
    line = l_ref[0]
    for k in range(n):
        total = dot_of(d, w_ref[k], 1, 1) + dot_of(line, misc_ref[k], 0, 0)
        out_ref[k] = total.astype(out_ref.dtype)


def project_back(flag, a, start, b, lines, w, misc, out_type):
    n, part, cols = w.shape
    blocks = b.shape[0]
    rows = misc.shape[1]
    return pl.pallas_call(
        functools.partial(back_kernel, n),
        out_shape=shape(n, blocks * SEQ, part, dtype=out_type),
        grid_spec=pltpu.PrefetchScalarGridSpec(
            num_scalar_prefetch=1,
            grid=(blocks,),
            in_specs=[
                pl.BlockSpec((1, SEQ, 4 * HD), lambda g, *p: (g + start, 0, 0)),
                lead_block(SEQ, 4 * HD),
                lead_block(rows, SEQ),
            ]
            + [whole(n, part, cols), whole(n, rows, part)],
            out_specs=stack_block(n, SEQ, part),
        ),
        compiler_params=pltpu.CompilerParams(vmem_limit_bytes=VMEM_LIMIT),
        cost_estimate=cost(2 * blocks * SEQ * part * n * cols, 8000000),
    )(flag, a, b, lines, w, misc)


def picked_block(half, part):
    return pl.BlockSpec((1, half, part), lambda g, *p: (p[0][g], 0, 0))


def weight_kernel(terms, *refs):
    out_ref = refs[-1]
    for at, total in terms(*refs[:-1]):
        out_ref[0, :, at : at + total.shape[1]] = total.astype(bf16)


def weight_call(terms, idx, picked, rest, cols, flops, flags=0):
    count = idx.shape[0] - flags
    n, half, part = picked[0].shape
    return pl.pallas_call(
        functools.partial(weight_kernel, terms),
        out_shape=shape(count, part, cols),
        grid_spec=pltpu.PrefetchScalarGridSpec(
            num_scalar_prefetch=1,
            grid=(count,),
            in_specs=[picked_block(half, part)] * len(picked) + [whole(*x.shape) for x in rest],
            out_specs=lead_block(part, cols),
        ),
        compiler_params=pltpu.CompilerParams(vmem_limit_bytes=VMEM_LIMIT),
        cost_estimate=cost(flops * count, 6000000),
    )(idx, *picked, *rest)


def weight_add_kernel(terms, *refs):
    got_ref, keep_ref, send_ref = refs[-3:]
    step = pl.program_id(0)
    for at, total in terms(*refs[:-3]):
        cols = slice(at, at + total.shape[1])
        total = total + got_ref[0, :, cols].astype(f32)

        @pl.when(step == 0)
        def _():
            keep_ref[0, :, cols] = total

        @pl.when(step != 0)
        def _():
            send_ref[0, :, cols] = total.astype(bf16)


def weight_add(terms, idx, picked, rest, got, cols, flops):
    n, half, part = picked[0].shape
    return pl.pallas_call(
        functools.partial(weight_add_kernel, terms),
        out_shape=[shape(1, part, cols, dtype=f32), shape(1, part, cols)],
        grid_spec=pltpu.PrefetchScalarGridSpec(
            num_scalar_prefetch=1,
            grid=(2,),
            in_specs=[picked_block(half, part)] * len(picked)
            + [whole(*x.shape) for x in rest]
            + [lead_block(part, cols)],
            out_specs=[whole(1, part, cols)] * 2,
        ),
        compiler_params=pltpu.CompilerParams(vmem_limit_bytes=VMEM_LIMIT),
        cost_estimate=cost(flops * 2, 6000000),
    )(idx, *picked, *rest, got)


def gate_up_terms(c, idx_ref, n1, n2, d1, d2):
    yield 0, dot_of(n1[0], d1[c], 0, 0) + dot_of(n2[0], d2[c], 0, 0)


def down_terms(idx_ref, g1, g2, m1, m2):
    for c in range(2):
        yield c * m1.shape[2], dot_of(g1[0], m1[c], 0, 0) + dot_of(g2[0], m2[c], 0, 0)


def own_terms(idx_ref, n1, n2, d):
    yield 0, dot_of(n1[0], d[0], 0, 0) + dot_of(n2[0], d[1], 0, 0)


def shared_terms(idx_ref, n1, n2, d, l1, l2):
    left = jnp.where(idx_ref[idx_ref.shape[0] - 1] == 0, n1[0], n2[0])
    yield 0, dot_of(left, d[...], 0, 0)
    yield d.shape[1], dot_of(n1[0], l1[...], 0, 1) + dot_of(n2[0], l2[...], 0, 1)


def own_head(k):
    return (3 * k + 1) // 2


def shared_head(q):
    return 1 + 3 * q


def head_cols(h):
    return slice(h * HD, (h + 1) * HD)


def mix_kernel(n, half, place_ref, w_ref, o_ref, own_ref, far_ref):
    for p, out_ref in enumerate((own_ref, far_ref)):
        second = place_ref[0] ^ p
        total = 0.0
        for k in range(n):
            ok = o_ref[k, p * half : (p + 1) * half, :]
            total = total + dot_of(ok, w_ref[:, head_cols(own_head(k))], 1, 1)
        for q in range(n // 2):
            one, two = o_ref[2 * q, 2 * half :, :], o_ref[2 * q + 1, 2 * half :, :]
            ob = jnp.where(second == 0, one, two)
            total = total + dot_of(ob, w_ref[:, head_cols(shared_head(q))], 1, 1)
        out_ref[...] = total


def attention_out(place, w_out, o, half):
    n = o.shape[0]
    part, cols = w_out.shape
    return pl.pallas_call(
        functools.partial(mix_kernel, n, half),
        out_shape=[shape(half, part, dtype=f32)] * 2,
        grid_spec=pltpu.PrefetchScalarGridSpec(
            num_scalar_prefetch=1,
            grid=(1,),
            in_specs=[whole(part, cols), whole(*o.shape)],
            out_specs=[whole(half, part)] * 2,
        ),
        compiler_params=pltpu.CompilerParams(vmem_limit_bytes=VMEM_LIMIT),
        cost_estimate=cost(4 * half * part * cols, 4000000),
    )(place, w_out, o)


def unmix_kernel(n, half, place_ref, w_ref, own_ref, far_ref, out_ref):
    place = place_ref[0]
    da = (own_ref[...], far_ref[...])
    for k in range(n):
        w = w_ref[:, head_cols(own_head(k))]
        for p in range(2):
            out_ref[k, p * half : (p + 1) * half, :] = dot_of(da[p], w, 1, 0).astype(bf16)
    for q in range(n // 2):
        w = w_ref[:, head_cols(shared_head(q))]
        both = [dot_of(d, w, 1, 0).astype(bf16) for d in da]
        out_ref[2 * q, 2 * half :, :] = jnp.where(place == 0, both[0], both[1])
        out_ref[2 * q + 1, 2 * half :, :] = jnp.where(place == 0, both[1], both[0])


def attention_out_back(place, w_out, own, far, n):
    half, part = own.shape
    cols = w_out.shape[1]
    return pl.pallas_call(
        functools.partial(unmix_kernel, n, half),
        out_shape=shape(n, 3 * half, HD),
        grid_spec=pltpu.PrefetchScalarGridSpec(
            num_scalar_prefetch=1,
            grid=(1,),
            in_specs=[whole(part, cols), whole(half, part), whole(half, part)],
            out_specs=whole(n, 3 * half, HD),
        ),
        compiler_params=pltpu.CompilerParams(vmem_limit_bytes=VMEM_LIMIT),
        cost_estimate=cost(4 * half * part * cols, 4000000),
    )(place, w_out, own, far)


def out_grad_kernel(n, half, place_ref, own_ref, far_ref, o_ref, out_ref):
    place = place_ref[0]
    da = (own_ref[...], far_ref[...])
    for k in range(n):
        total = dot_of(da[0], o_ref[k, :half, :], 0, 0)
        total = total + dot_of(da[1], o_ref[k, half : 2 * half, :], 0, 0)
        out_ref[:, head_cols(own_head(k))] = total.astype(bf16)
    for q in range(n // 2):
        one, two = o_ref[2 * q, 2 * half :, :], o_ref[2 * q + 1, 2 * half :, :]
        total = dot_of(da[0], jnp.where(place == 0, one, two), 0, 0)
        total = total + dot_of(da[1], jnp.where(place == 0, two, one), 0, 0)
        out_ref[:, head_cols(shared_head(q))] = total.astype(bf16)


def out_gradient(place, own, far, o, cols):
    n = o.shape[0]
    half, part = own.shape
    return pl.pallas_call(
        functools.partial(out_grad_kernel, n, half),
        out_shape=shape(part, cols),
        grid_spec=pltpu.PrefetchScalarGridSpec(
            num_scalar_prefetch=1,
            grid=(1,),
            in_specs=[whole(half, part), whole(half, part), whole(*o.shape)],
            out_specs=whole(part, cols),
        ),
        compiler_params=pltpu.CompilerParams(vmem_limit_bytes=VMEM_LIMIT),
        cost_estimate=cost(4 * half * part * cols, 4000000),
    )(place, own, far, o)


def swap(x, axis, size, k):
    return lax.ppermute(x, axis, [(n, n ^ k) for n in range(size)])


def shift_rows(x, start, size):
    return lax.dynamic_slice_in_dim(x, start, size, axis=0)


def exchange(x, axis):
    return lax.all_to_all(x, axis, split_axis=0, concat_axis=0, tiled=True)


def to_all(x, axis, n):
    return exchange(jnp.broadcast_to(x[None], (n,) + x.shape), axis)


def after(x, *others):
    return lax.optimization_barrier((x,) + others)[0]


def per_device(
    dp_size,
    wid_size,
    tokens,
    cotangent,
    lengths,
    w_project,
    w_beta,
    w_out,
    w_gate_up,
    w_down,
    gain_attn,
    gain_ffn,
):
    wid = lax.axis_index("wid")
    hid = lax.axis_index("hid")
    dp = lax.axis_index("dp")
    ws = range(wid_size)
    rows, part = tokens.shape
    half = rows // 2
    width = part * wid_size
    ff = w_down.shape[1] // wid_size
    heads = w_beta.shape[1]
    per_half = half // SEQ

    def hid_swap(x):
        return swap(x, "hid", 2, 1)

    half_b = (wid & 1) ^ hid
    my_head = own_head(wid)
    my_shared = shared_head(wid // 2)

    x_own = shift_rows(tokens, hid * half, half)
    g_own = shift_rows(cotangent, hid * half, half)

    spare = jnp.zeros((16 - heads - 3, part), bf16)
    length_line = jnp.broadcast_to(lengths.astype(bf16)[:, None], (1, part))
    misc_here = jnp.concatenate(
        [w_beta.T, gain_attn[None], gain_ffn[None], length_line, spare], axis=0
    )
    gathered = to_all(jnp.concatenate([x_own, misc_here], axis=0), "wid", wid_size)
    xs_own, misc = gathered[:, :half], gathered[:, half:]
    xs_far = hid_swap(xs_own)
    len_abs = misc[:, heads + 2, 0].astype(jnp.int32)

    def heads_for(w):
        a = w_project[:, :, head_cols(own_head(w))].reshape(part, 4 * HD)
        b = w_project[:, :, head_cols(shared_head(w // 2))].reshape(part, 4 * HD)
        return jnp.concatenate([a, b], axis=1)

    side = dp & 1
    ffh = ff // 2

    def ffn_for(w):
        at = w * ff + side * ffh
        cut = lax.dynamic_slice_in_dim(w_gate_up, at, ffh, axis=2).reshape(part, 2 * ffh)
        return jnp.concatenate([cut, lax.dynamic_slice_in_dim(w_down, at, ffh, axis=1)], axis=1)

    ffn_own = exchange(after(jnp.stack([ffn_for(w) for w in ws]), gathered), "wid")
    proj_w = exchange(after(jnp.stack([heads_for(w) for w in ws]), ffn_own), "wid")
    ffn_other = swap(ffn_own, "dp", dp_size, 1)
    side = side.astype(jnp.int32)[None]

    def lens_of(place):
        return lax.dynamic_slice_in_dim(len_abs, place * per_half, per_half)

    lens_own, lens_far = lens_of(hid), lens_of(1 - hid)
    lens = jnp.concatenate([lens_own, lens_far, lens_of(wid & 1)])
    slot = jnp.arange(SEQ, dtype=jnp.int32)
    valid_half = (slot[None] < lens_own[:, None]).astype(f32).reshape(half, 1)

    a_own, b_own, l_own, r_own, n1_own = project(xs_own, proj_w, misc)
    a_far, b_far, l_far, r_far, n1_far = project(xs_far, proj_w, misc)

    def pick_b(own, far):
        return jnp.where(half_b == 0, own, far)

    pairs = jnp.concatenate([a_own, a_far, pick_b(b_own, b_far)], axis=0)

    def line_of(lines, h):
        return lax.dynamic_slice_in_dim(lines, h, 1, axis=1)

    logit_pairs = jnp.concatenate(
        [
            line_of(l_own, my_head),
            line_of(l_far, my_head),
            line_of(pick_b(l_own, l_far), my_shared),
        ],
        axis=0,
    )
    gs_own = exchange(
        after(jnp.broadcast_to(g_own[None], (wid_size,) + g_own.shape), proj_w), "wid"
    )
    attended, inv, carry, prob = attention_forward(lens, after(pairs, ffn_other), logit_pairs)
    o_all = to_all(after(attended, gs_own).reshape(-1, HD), "wid", wid_size)
    place = hid.astype(jnp.int32)[None]
    attn_own, attn_far = attention_out(place, w_out, o_all, half)
    hidden = x_own.astype(f32) + attn_own + hid_swap(attn_far)

    gain_one = gain_attn[None].astype(f32)
    gain_two = gain_ffn[None].astype(f32)
    hs_own = to_all(hidden.astype(bf16), "wid", wid_size)
    hs_far = hid_swap(hs_own)
    gs_far = hid_swap(gs_own)
    n2_own, m_own, d_own, dn_own, s_own, r2_own = feed_forward(
        lens_own, side, hs_own, gs_own, ffn_own, ffn_other, misc, f32
    )
    n2_far, m_far, d_far, dn_far, s_far, r2_far = feed_forward(
        lens_far, side, hs_far, gs_far, ffn_own, ffn_other, misc, bf16
    )

    def partial(own, far):
        return (own + hid_swap(far).astype(f32)).astype(bf16)

    def line_sum(own, far, late):
        here = (own + hid_swap(far)).reshape(-1, 128)
        others = [swap(here, "wid", wid_size, k) for k in range(1, wid_size)]
        others = lax.optimization_barrier((*others, late))[:-1]
        total = here + sum(others)
        return total.reshape(-1, 1) * (1.0 / width)

    dn_here = partial(dn_own, dn_far)
    dn_got = exchange(dn_here, "wid")
    mean_two = line_sum(s_own, s_far, dn_got)
    grad_normed_two = jnp.sum(dn_got.astype(f32), axis=0)

    chunk = width // dp_size
    direct = dp_size == wid_size
    sub = chunk // wid_size

    def dp_pieces(terms, picked, rest, cols, flags, ts):
        if direct:
            idx = jnp.stack([dp ^ t for t in ts]).astype(jnp.int32)
            idx = jnp.concatenate([idx, *flags])
            return weight_call(terms, idx, picked, rest, cols, 2 * half * part * cols, len(flags))
        idx = jnp.concatenate([jnp.arange(wid_size, dtype=jnp.int32), *flags])
        full = weight_call(terms, idx, picked, rest, cols, 2 * half * part * cols, len(flags))
        full = full.reshape(width, -1)
        return jnp.stack([shift_rows(full, (dp ^ t) * chunk, chunk) for t in ts])

    def dp_odd(terms, picked, rest, cols, flags=()):
        return dp_pieces(terms, picked, rest, cols, flags, range(1, dp_size, 2))

    def dp_even(terms, picked, rest, cols, got, flags=()):
        if direct and dp_size == 4:
            idx = jnp.stack([dp, dp ^ 2]).astype(jnp.int32)
            idx = jnp.concatenate([idx, *flags])
            flops = 2 * half * part * cols
            keep, send = weight_add(terms, idx, picked, rest, got, cols, flops)
            return keep, swap(send, "dp", dp_size, 2)
        here = dp_pieces(terms, picked, rest, cols, flags, range(0, dp_size, 2))
        return dp_send(here.astype(f32) + got.astype(f32))

    def dp_send(held, k=2):
        return held[0::2], swap(held[1::2].astype(bf16), "dp", dp_size, k)

    def dp_take(keep, got, k=2):
        held = keep + got.astype(f32)
        while held.shape[0] > 1:
            k *= 2
            keep, got = dp_send(held, k)
            held = keep + got.astype(f32)
        return held[0]

    def dp_sum(pieces, *late):
        odd, even = jnp.stack(pieces[1::2]), jnp.stack(pieces[0::2])
        got = after(swap(odd.astype(bf16), "dp", dp_size, 1), *late)
        return dp_take(*dp_send(even.astype(f32) + got.astype(f32)))

    def to_rows(x):
        return exchange(x.astype(bf16).reshape(wid_size, sub, -1), "wid")

    gate_up = [functools.partial(gate_up_terms, c) for c in range(2)]
    n2_both, gs_both = (n2_own, n2_far), (gs_own, gs_far)
    odd = [dp_odd(gate_up[0], n2_both, (after(d_own, dn_here), d_far), ff)]
    odd.append(dp_odd(gate_up[1], n2_both, (after(d_own, odd[0]), d_far), ff))
    odd.append(dp_odd(down_terms, gs_both, (after(m_own, odd[1]), m_far), ff))
    got_odd = [swap(x, "dp", dp_size, 1) for x in odd]

    grad_half = g_own.astype(f32) * valid_half
    grad_hidden = grad_half + r2_own * (
        grad_normed_two * gain_two - r2_own * hidden * mean_two
    )
    gain_two_part = jnp.sum(grad_normed_two * hidden * r2_own, axis=0)
    da_own = after(grad_hidden.astype(bf16), odd[2])
    da_far = hid_swap(da_own)
    keep_0, next_0 = dp_even(gate_up[0], n2_both, (after(d_own, odd[2]), d_far), ff, got_odd[0])
    do_here = attention_out_back(place, w_out, after(da_own, keep_0), da_far, wid_size)
    do_pieces = exchange(do_here, "wid")
    ffn_own_out, ffn_far_out = feed_forward_out(
        side, after(m_own, do_here), m_far, ffn_own, ffn_other
    )
    g_out = out_gradient(place, after(da_own, ffn_far_out), da_far, o_all, w_out.shape[1])
    do_got = do_pieces.reshape(wid_size, -1, SEQ, HD)

    pairs_a, lines_a, sums_a = attention_backward(
        lens, pairs, logit_pairs, inv, carry, prob, after(do_got, ffn_far_out, g_out), 0, 2 * per_half
    )

    head_iota = lax.broadcasted_iota(jnp.int32, (1, 16, 1), 1)
    m_then = after(m_own, pairs_a)
    keep_2, next_2 = dp_even(down_terms, gs_both, (m_then, m_far), ff, got_odd[2])
    right_own = pairs_a.reshape(2, half, 4 * HD)
    ffn_here = after(partial(ffn_own_out, after(ffn_far_out, do_got)), pairs_a)
    ffn_back = exchange(ffn_here, "wid")

    n1_both = (n1_own, n1_far)
    own_odd = dp_odd(own_terms, n1_both, (right_own,), 4 * HD)
    own_got = swap(own_odd, "dp", dp_size, 1)
    d_then = after(d_own, own_odd)
    keep_1, next_1 = dp_even(gate_up[1], n2_both, (d_then, d_far), ff, got_odd[1])
    pairs_b, lines_b, sums_b = attention_backward(
        lens, pairs, logit_pairs, inv, carry, prob, after(do_got, own_odd, keep_1, next_0), 2 * per_half, per_half
    )

    def spread(a, b, at):
        own = a[at * per_half : (at + 1) * per_half]
        return own, jnp.where(half_b == at, b, 0.0)

    def lines_at(at):
        own, shared = spread(lines_a, lines_b, at)
        own = jnp.where(head_iota == my_head, own, 0.0)
        shared = jnp.where(head_iota == my_shared, shared, 0.0)
        return (own + shared).astype(bf16)

    def flat_lines(x):
        flat = jnp.swapaxes(x, 0, 1).reshape(16, half)
        return jnp.concatenate([flat, jnp.zeros((128 - 16, half), bf16)], axis=0)

    lines_own, lines_far = lines_at(0), lines_at(1)
    flat_own, flat_far = flat_lines(lines_own), flat_lines(lines_far)
    right_shared = after(pairs_b, keep_2, next_1).reshape(half, 4 * HD)

    flat_both = (flat_own, flat_far)
    half_flag = (half_b.astype(jnp.int32)[None],)
    shared_odd = dp_odd(shared_terms, n1_both, (right_shared, *flat_both), 5 * HD, half_flag)
    shared_got = swap(shared_odd, "dp", dp_size, 1)
    fine = part // dp_size
    to_place = [
        (c * wid_size + w, w * dp_size + c) for c in range(dp_size) for w in range(wid_size)
    ]

    def dp_fine(x, *late):
        return dp_sum([shift_rows(x, (dp ^ t) * fine, fine) for t in range(dp_size)], *late)

    out_pieces = [shift_rows(g_out, (dp ^ t) * fine, fine) for t in range(dp_size)]
    out_got = swap(jnp.stack(out_pieces[1::2]), "dp", dp_size, 1)
    flags = [(half_b == p).astype(jnp.int32)[None] for p in range(2)]
    back_b = after(pairs_b, shared_odd, own_got, ffn_back)
    dn1_far = project_back(flags[1], pairs_a, per_half, back_b, lines_far, proj_w, misc, bf16)
    right_own = after(right_own, dn1_far, own_got)
    keep_own, next_own = dp_even(own_terms, n1_both, (right_own,), 4 * HD, own_got)
    back_b = after(back_b, keep_own)
    dn1_own = project_back(flags[0], pairs_a, 0, back_b, lines_own, proj_w, misc, f32)
    dn1_here = partial(dn1_own, dn1_far)
    dn1_got = exchange(dn1_here, "wid")
    right_shared = after(right_shared, dn1_here, shared_got)
    right_shared = after(right_shared, next_own)
    keep_shared, next_shared = dp_even(
        shared_terms, n1_both, (right_shared, *flat_both), 5 * HD, shared_got, half_flag
    )
    next_own, next_shared = lax.optimization_barrier((next_own, next_shared, dn1_got))[:2]
    next_2 = after(next_2, dn1_got)
    sums = [sum(spread(sums_a, sums_b, p)) for p in range(2)]
    mean_one = line_sum(*sums, dn1_got)
    grad_normed_one = jnp.sum(dn1_got.astype(f32), axis=0)
    ffn = jnp.sum(ffn_back.astype(f32), axis=0)

    source = x_own.astype(f32)
    r1_half = r_own.reshape(half, 1)
    gain_one_part = jnp.sum(grad_normed_one * source * r1_half, axis=0)
    input_half = grad_hidden + r1_half * (
        grad_normed_one * gain_one - r1_half * source * mean_one
    )

    def whole_rows(x):
        other = hid_swap(x)
        return jnp.concatenate(
            [jnp.where(hid == 0, x, other), jnp.where(hid == 0, other, x)], axis=0
        )

    ffn_sums = [dp_take(keep_0, next_0), dp_take(keep_1, next_1), dp_take(keep_2, next_2)]
    ffn_sums = after(jnp.concatenate(ffn_sums, axis=1).astype(bf16), dn1_got)
    ffn_rows = to_rows(ffn_sums)
    input_grad = whole_rows(after(input_half.astype(bf16), ffn_sums))
    output = whole_rows(after(((hidden + ffn) * valid_half).astype(bf16), ffn_sums))

    proj_sums = [dp_take(keep_own, next_own), dp_take(keep_shared, next_shared)]
    proj_sums = jnp.concatenate(proj_sums, axis=1).astype(bf16)
    out_even = jnp.stack(out_pieces[0::2]).astype(f32)
    out_got = after(out_got, dn1_got)
    out_sum = dp_take(*dp_send(out_even + out_got.astype(f32))).astype(bf16)
    out_sum = after(out_sum, proj_sums, ffn_rows)
    out_out = lax.ppermute(out_sum, ("dp", "wid"), to_place).astype(f32)
    gain_part = after(jnp.stack([gain_one_part, gain_two_part], axis=1), proj_sums, ffn_rows)
    gain_part = gain_part + hid_swap(gain_part)
    gain_sum = lax.ppermute(dp_fine(gain_part), ("dp", "wid"), to_place)

    got = ffn_rows[:, :, : 2 * ff].reshape(wid_size, sub, 2, 2, ffh)
    gate, up = (
        jnp.concatenate([got[w, :, c, k] for w in ws for c in range(2)], axis=1) for k in range(2)
    )
    down = jnp.concatenate([ffn_rows[w, :, 2 * ff :] for w in ws], axis=1)
    out_gate_up = jnp.stack([gate, up], axis=1).astype(f32)
    out_down = down.astype(f32)

    got = to_rows(after(proj_sums, ffn_rows)).astype(f32)
    a = [got[w, :, : 4 * HD] for w in ws]
    b = [got[w, :, 4 * HD : 8 * HD] for w in ws]
    proj_rows = [a[0], b[0] + b[1], a[1], a[2], b[2] + b[3], a[3]]
    out_project = jnp.concatenate([p.reshape(sub, 4, HD) for p in proj_rows], axis=2)
    out_beta = jnp.sum(got[:, :, 8 * HD : 8 * HD + heads], axis=0)


    return (
        output,
        input_grad,
        out_project,
        out_beta,
        out_out,
        out_gate_up,
        out_down,
        gain_sum[:, 0],
        gain_sum[:, 1],
    )


def solution(mesh):
    return jax.shard_map(
        functools.partial(per_device, mesh.shape["dp"], mesh.shape["wid"]),
        mesh=mesh,
        in_specs=(
            P("dp", "wid"),
            P("dp", "wid"),
            P(("dp", "wid")),
            P("wid", None, "hid"),
            P("wid", "hid"),
            P("wid", "hid"),
            P("wid", None, "hid"),
            P("wid", "hid"),
            P("wid"),
            P("wid"),
        ),
        out_specs=(
            P("dp", "wid"),
            P("dp", "wid"),
            P(("dp", "wid"), None, "hid"),
            P(("dp", "wid"), "hid"),
            P(("dp", "wid"), "hid"),
            P(("dp", "wid"), None, "hid"),
            P(("dp", "wid"), "hid"),
            P(("dp", "wid")),
            P(("dp", "wid")),
        ),
        check_vma=False,
    )
```

```python
import functools

import jax
import jax.numpy as jnp
from jax import lax
from jax.experimental import pallas as pl
from jax.experimental.pallas import tpu as pltpu
from jax.sharding import PartitionSpec as P

f32 = jnp.float32
bf16 = jnp.bfloat16

SEQ = 256
HD = 128


def dot_of(a, b, ca, cb):
    return lax.dot_general(a, b, (((ca,), (cb,)), ((), ())), preferred_element_type=f32)


def halves_of(a):
    high = a.astype(bf16)
    return high, (a - high.astype(f32)).astype(bf16)


def mul(a, b, ca=1, cb=0, passes=3):
    if passes == 1:
        return dot_of(a.astype(bf16), b.astype(bf16), ca, cb)
    if a.dtype == bf16:
        bh, bl = halves_of(b)
        return dot_of(a, bh, ca, cb) + dot_of(a, bl, ca, cb)
    if b.dtype == bf16:
        ah, al = halves_of(a)
        return dot_of(ah, b, ca, cb) + dot_of(al, b, ca, cb)
    ah, al = halves_of(a)
    bh, bl = halves_of(b)
    return dot_of(ah, bh, ca, cb) + (dot_of(ah, bl, ca, cb) + dot_of(al, bh, ca, cb))


def iotas():
    rows = lax.broadcasted_iota(jnp.int32, (SEQ, SEQ), 0)
    cols = lax.broadcasted_iota(jnp.int32, (SEQ, SEQ), 1)
    return rows, cols


def prepare(raw, logit_row, i, j):
    eye = i == j
    raw_f = raw.astype(f32)
    norm = lax.rsqrt(jnp.sum(raw_f * raw_f, axis=1, keepdims=True) + 1e-6)
    norm_row = jnp.sum(jnp.where(eye, norm, 0.0), axis=0, keepdims=True)
    beta_row = 2.0 / (1.0 + jnp.exp(-logit_row))
    beta = jnp.sum(jnp.where(eye, beta_row, 0.0), axis=1, keepdims=True)
    return raw_f, norm, norm_row, beta_row, beta


def inverses(lowers, i, j):
    eye = jnp.where(i == j, 1.0, 0.0)
    first = ((i >> 1) == (j >> 1)) & (i > j)
    inv = [eye - jnp.where(first, n, 0.0) for n in lowers]
    s = 1
    while (1 << s) < SEQ:
        mask = ((i >> (s + 1)) == (j >> (s + 1))) & ((i >> s) > (j >> s))
        mids = [mul(d, jnp.where(mask, n, 0.0)) for d, n in zip(inv, lowers)]
        inv = [d - mul(x, d) for d, x in zip(inv, mids)]
        s += 1
    return inv


def forward_kernel(count, len_ref, x_ref, l_ref, o_ref, inv_ref, carry_ref, prob_ref):
    base = pl.program_id(0) * count
    i, j = iotas()
    row = lax.broadcasted_iota(jnp.int32, (SEQ, 1), 0)
    xs = [x_ref[t] for t in range(count)]
    qs = [x[:, 0:HD] for x in xs]
    ks = [x[:, HD : 2 * HD] for x in xs]
    vs = [x[:, 2 * HD : 3 * HD] for x in xs]
    us = [x[:, 3 * HD : 4 * HD] for x in xs]
    pre = [prepare(us[t], l_ref[t], i, j) for t in range(count)]
    lowers = [
        p[4] * jnp.where(i > j, dot_of(u, u, 1, 1) * p[1] * p[2], 0.0) for u, p in zip(us, pre)
    ]
    inv = inverses(lowers, i, j)
    bs = [jnp.where(i > j, dot_of(u, k, 1, 1) * p[1], 0.0) for u, k, p in zip(us, ks, pre)]
    carries = [mul(d * p[3], b) for d, p, b in zip(inv, pre, bs)]
    as_ = [jnp.where(i >= j, dot_of(q, u, 1, 1) * p[2], 0.0) for q, u, p in zip(qs, us, pre)]
    scores = [
        (dot_of(q, k, 1, 1) - mul(a, c)) * (HD**-0.5) for q, k, a, c in zip(qs, ks, as_, carries)
    ]
    for t in range(count):
        length = len_ref[base + t]
        score = jnp.where((j <= i) & (j < length), scores[t], -1e30)
        weight = jnp.exp(score - jnp.max(score, axis=1, keepdims=True))
        prob = weight * (1.0 / jnp.sum(weight, axis=1, keepdims=True))
        out = jnp.where(row < length, mul(prob, vs[t], passes=1), 0.0)
        o_ref[t] = out.astype(bf16)
        inv_ref[t] = inv[t]
        carry_ref[t] = carries[t]
        prob_ref[t] = prob


def to_row(col, eye):
    return jnp.sum(jnp.where(eye, col, 0.0), axis=0, keepdims=True)


def backward_kernel(
    count,
    start,
    len_ref,
    x_ref,
    l_ref,
    inv_ref,
    carry_ref,
    prob_ref,
    do_ref,
    dx_ref,
    dl_ref,
    sum_ref,
):
    base = (pl.program_id(0) + start) * count
    i, j = iotas()
    row = lax.broadcasted_iota(jnp.int32, (SEQ, 1), 0)
    for t in range(count):
        x = x_ref[t]
        q, k = x[:, 0:HD], x[:, HD : 2 * HD]
        v, u = x[:, 2 * HD : 3 * HD], x[:, 3 * HD : 4 * HD]
        do = do_ref[0, t].astype(f32) + do_ref[1, t].astype(f32)
        do = (do + (do_ref[2, t].astype(f32) + do_ref[3, t].astype(f32))).astype(bf16)
        do = jnp.where(row < len_ref[base + t], do, jnp.zeros_like(do))
        inv, carry, prob = inv_ref[t], carry_ref[t], prob_ref[t]
        raw, norm, norm_row, beta_row, beta = prepare(u, l_ref[t], i, j)
        gram = jnp.where(i > j, dot_of(u, u, 1, 1) * norm * norm_row, 0.0)
        a = jnp.where(i >= j, dot_of(q, u, 1, 1) * norm_row, 0.0)
        b = jnp.where(i > j, dot_of(u, k, 1, 1) * norm, 0.0)
        m = inv * beta_row
        dv = mul(prob, do, 0, 0, passes=1)
        dprob = dot_of(do, v, 1, 1)
        ds = prob * (dprob - jnp.sum(dprob * prob, axis=1, keepdims=True)) * (HD**-0.5)
        da = jnp.where(i >= j, -mul(ds, carry, 1, 1), 0.0)
        dc = -mul(a, ds, 0, 0)
        dm = mul(dc, b, 1, 1)
        db = jnp.where(i > j, mul(m, dc, 0, 0), 0.0)
        dn = jnp.where(i > j, -mul(mul(inv, dm, 0, 0), m, 1, 1), 0.0)
        dgram = beta * dn
        dbeta = jnp.sum(dm * inv, axis=0, keepdims=True)
        dbeta_col = jnp.sum(dn * gram, axis=1, keepdims=True)
        dbeta = dbeta + jnp.sum(jnp.where(i == j, dbeta_col, 0.0), axis=0, keepdims=True)
        dq = mul(ds, k, passes=1) + mul(da * norm_row, u, passes=1)
        dk = mul(ds, q, 0, 0, passes=1) + mul(db * norm, u, 0, 0, passes=1)
        dw = mul(da, q, 0, 0, passes=1) + mul(db, k, passes=1)
        dw = dw + mul(dgram * norm_row, u, passes=1) + mul(dgram * norm, u, 0, 0, passes=1)
        du = norm * dw - (norm * norm * norm) * raw * jnp.sum(dw * raw, axis=1, keepdims=True)
        dx = jnp.concatenate([dq, dk, dv, du], axis=1)
        dl = dbeta * beta_row * (1.0 - 0.5 * beta_row)
        dx_ref[t] = dx.astype(bf16)
        dl_ref[t] = dl
        total = jnp.sum(dx * x.astype(f32), axis=1, keepdims=True)
        sum_ref[t] = to_row(total, i == j) + dl * l_ref[t]


def block_of(count, *shape):
    return pl.BlockSpec((count,) + shape, lambda g, lens: (g, 0, 0))


def attention_forward(lens, x, logits, count=3):
    pairs = x.shape[0]
    square = jax.ShapeDtypeStruct((pairs, SEQ, SEQ), f32)
    return pl.pallas_call(
        functools.partial(forward_kernel, count),
        out_shape=[jax.ShapeDtypeStruct((pairs, SEQ, HD), bf16), square, square, square],
        grid_spec=pltpu.PrefetchScalarGridSpec(
            num_scalar_prefetch=1,
            grid=(pairs // count,),
            in_specs=[block_of(count, SEQ, 4 * HD), block_of(count, 1, SEQ)],
            out_specs=[block_of(count, SEQ, HD)] + [block_of(count, SEQ, SEQ)] * 3,
        ),
        compiler_params=pltpu.CompilerParams(vmem_limit_bytes=48 << 20),
        cost_estimate=cost(pairs * 1600000000, pairs * 1100000),
    )(lens, x, logits)


def attention_backward(lens, x, logits, inv, carry, prob, do, start, pairs):
    line = jax.ShapeDtypeStruct((pairs, 1, SEQ), f32)

    def from_start(*dims):
        return pl.BlockSpec((1,) + dims, lambda g, lens: (g + start, 0, 0))

    return pl.pallas_call(
        functools.partial(backward_kernel, 1, start),
        out_shape=[jax.ShapeDtypeStruct((pairs, SEQ, 4 * HD), bf16), line, line],
        grid_spec=pltpu.PrefetchScalarGridSpec(
            num_scalar_prefetch=1,
            grid=(pairs,),
            in_specs=[from_start(SEQ, 4 * HD), from_start(1, SEQ)]
            + [from_start(SEQ, SEQ)] * 3
            + [pl.BlockSpec((4, 1, SEQ, HD), lambda g, lens: (0, g + start, 0, 0))],
            out_specs=[block_of(1, SEQ, 4 * HD)] + [block_of(1, 1, SEQ)] * 2,
        ),
        compiler_params=pltpu.CompilerParams(vmem_limit_bytes=48 << 20),
        cost_estimate=cost(pairs * 1400000000, pairs * 1400000),
    )(lens, x, logits, inv, carry, prob, do)


VMEM_LIMIT = 48 << 20
COST_SCALE = 0.001


def shape(*dims, dtype=bf16):
    return jax.ShapeDtypeStruct(dims, dtype)


def rows_block(size, cols):
    return pl.BlockSpec((size, cols), lambda g, *p: (g, 0))


def stack_block(n, size, cols):
    return pl.BlockSpec((n, size, cols), lambda g, *p: (0, g, 0))


def lead_block(size, cols):
    return pl.BlockSpec((1, size, cols), lambda g, *p: (g, 0, 0))


def whole(*dims):
    return pl.BlockSpec(dims, lambda g, *p: (0,) * len(dims))


def cost(flops, moved):
    scale = COST_SCALE
    return pl.CostEstimate(
        flops=int(flops * scale), bytes_accessed=int(moved * scale), transcendentals=0
    )


def project_kernel(n, x_ref, w_ref, misc_ref, a_ref, b_ref, l_ref, r_ref, xg_ref):
    i, j = iotas()
    squares = 0.0
    for k in range(n):
        xf = x_ref[k].astype(f32)
        squares = squares + jnp.sum(xf * xf, axis=1, keepdims=True)
    r = lax.rsqrt(squares * (1.0 / (n * x_ref.shape[2])) + 1e-6)
    acc = 0.0
    logit = 0.0
    for k in range(n):
        gain = misc_ref[k][6:7, :].astype(f32)
        normed = (x_ref[k].astype(f32) * r * gain).astype(bf16)
        xg_ref[k] = normed
        acc = acc + dot_of(normed, w_ref[k], 1, 0)
        logit = logit + dot_of(misc_ref[k], normed, 1, 1)
    out = acc.astype(bf16)
    a_ref[0] = out[:, : 4 * HD]
    b_ref[0] = out[:, 4 * HD :]
    l_ref[0] = logit
    r_ref[0] = to_row(r, i == j)


def project(x, w, misc):
    n, half, part = x.shape
    blocks = half // SEQ
    cols = w.shape[2]
    lines = misc.shape[1]
    return pl.pallas_call(
        functools.partial(project_kernel, n),
        out_shape=[
            shape(blocks, SEQ, 4 * HD),
            shape(blocks, SEQ, 4 * HD),
            shape(blocks, lines, SEQ, dtype=f32),
            shape(blocks, 1, SEQ, dtype=f32),
            shape(n, half, part),
        ],
        grid=(blocks,),
        in_specs=[stack_block(n, SEQ, part), whole(n, part, cols), whole(n, lines, part)],
        out_specs=[
            lead_block(SEQ, 4 * HD),
            lead_block(SEQ, 4 * HD),
            lead_block(lines, SEQ),
            lead_block(1, SEQ),
            stack_block(n, SEQ, part),
        ],
        compiler_params=pltpu.CompilerParams(vmem_limit_bytes=VMEM_LIMIT),
        cost_estimate=cost(2 * half * part * n * cols, 8000000),
    )(x, w, misc)


def ffn_kernel(
    n,
    len_ref,
    side_ref,
    h_ref,
    g_ref,
    wa_ref,
    wb_ref,
    misc_ref,
    n2_ref,
    m_ref,
    d_ref,
    dn_ref,
    sum_ref,
    r_ref,
):
    ff = m_ref.shape[2]
    i, j = iotas()
    row = lax.broadcasted_iota(jnp.int32, (SEQ, 1), 0)
    valid = row < len_ref[pl.program_id(0)]
    squares = 0.0
    for k in range(n):
        hf = h_ref[k].astype(f32)
        squares = squares + jnp.sum(hf * hf, axis=1, keepdims=True)
    r = lax.rsqrt(squares * (1.0 / (n * h_ref.shape[2])) + 1e-6)
    for k in range(n):
        gain = misc_ref[k][7:8, :].astype(f32)
        n2_ref[k] = (h_ref[k].astype(f32) * r * gain).astype(bf16)
    r_ref[...] = r
    both = []
    total = 0.0
    for c, w_ref in enumerate((wa_ref, wb_ref)):
        place = side_ref[0] ^ c
        gate_up = 0.0
        dm = 0.0
        for k in range(n):
            gate_up = gate_up + dot_of(n2_ref[k], w_ref[k, :, : 2 * ff], 1, 0)
            dm = dm + dot_of(g_ref[k], w_ref[k, :, 2 * ff :], 1, 0)
        gate = gate_up[:, :ff]
        up = gate_up[:, ff:]
        sig = 1.0 / (1.0 + jnp.exp(-gate))
        active = gate * sig
        m_ref[place] = jnp.where(valid, active * up, 0.0).astype(bf16)
        dm = jnp.where(valid, dm, 0.0)
        dgate = dm * up * sig * (1.0 + gate * (1.0 - sig))
        dup = dm * active
        total = total + jnp.sum(dgate * gate + dup * up, axis=1, keepdims=True)
        d = jnp.concatenate([dgate, dup], axis=1).astype(bf16)
        d_ref[place] = d
        both.append(d)
    sum_ref[0] = to_row(total, i == j)
    for k in range(n):
        dn = dot_of(both[0], wa_ref[k, :, : 2 * ff], 1, 1)
        dn = dn + dot_of(both[1], wb_ref[k, :, : 2 * ff], 1, 1)
        dn_ref[k] = dn.astype(dn_ref.dtype)


def feed_forward(lens, side, h, g, wa, wb, misc, out_type):
    n, half, part = h.shape
    blocks = half // SEQ
    cols = wa.shape[2]
    ff = cols // 3
    lines = misc.shape[1]
    return pl.pallas_call(
        functools.partial(ffn_kernel, n),
        out_shape=[
            shape(n, half, part),
            shape(2, half, ff),
            shape(2, half, 2 * ff),
            shape(n, half, part, dtype=out_type),
            shape(blocks, 1, SEQ, dtype=f32),
            shape(half, 1, dtype=f32),
        ],
        grid_spec=pltpu.PrefetchScalarGridSpec(
            num_scalar_prefetch=2,
            grid=(blocks,),
            in_specs=[stack_block(n, SEQ, part)] * 2
            + [whole(n, part, cols)] * 2
            + [whole(n, lines, part)],
            out_specs=[
                stack_block(n, SEQ, part),
                stack_block(2, SEQ, ff),
                stack_block(2, SEQ, 2 * ff),
                stack_block(n, SEQ, part),
                lead_block(1, SEQ),
                rows_block(SEQ, 1),
            ],
        ),
        compiler_params=pltpu.CompilerParams(vmem_limit_bytes=VMEM_LIMIT),
        cost_estimate=cost(2 * half * part * n * 10 * ff, 12000000),
    )(lens, side, h, g, wa, wb, misc)


def ffn_out_kernel(n, side_ref, one_ref, two_ref, wa_ref, wb_ref, own_ref, far_ref):
    ff = one_ref.shape[2]
    for m_ref, out_ref in ((one_ref, own_ref), (two_ref, far_ref)):
        first, second = m_ref[side_ref[0]], m_ref[side_ref[0] ^ 1]
        for k in range(n):
            total = dot_of(first, wa_ref[k, :, 2 * ff :], 1, 1)
            total = total + dot_of(second, wb_ref[k, :, 2 * ff :], 1, 1)
            out_ref[k] = total.astype(out_ref.dtype)


def feed_forward_out(side, own, far, wa, wb):
    _, half, ff = own.shape
    n, part, cols = wa.shape
    return pl.pallas_call(
        functools.partial(ffn_out_kernel, n),
        out_shape=[shape(n, half, part, dtype=f32), shape(n, half, part)],
        grid_spec=pltpu.PrefetchScalarGridSpec(
            num_scalar_prefetch=1,
            grid=(half // SEQ,),
            in_specs=[stack_block(2, SEQ, ff)] * 2 + [whole(n, part, cols)] * 2,
            out_specs=[stack_block(n, SEQ, part)] * 2,
        ),
        compiler_params=pltpu.CompilerParams(vmem_limit_bytes=VMEM_LIMIT),
        cost_estimate=cost(8 * half * part * n * ff, 12000000),
    )(side, own, far, wa, wb)


def back_kernel(n, flag_ref, a_ref, b_ref, l_ref, w_ref, misc_ref, out_ref):
    b = b_ref[0]
    b = jnp.where(flag_ref[0] > 0, b, jnp.zeros_like(b))
    d = jnp.concatenate([a_ref[0], b], axis=1)
    line = l_ref[0]
    for k in range(n):
        total = dot_of(d, w_ref[k], 1, 1) + dot_of(line, misc_ref[k], 0, 0)
        out_ref[k] = total.astype(out_ref.dtype)


def project_back(flag, a, start, b, lines, w, misc, out_type):
    n, part, cols = w.shape
    blocks = b.shape[0]
    rows = misc.shape[1]
    return pl.pallas_call(
        functools.partial(back_kernel, n),
        out_shape=shape(n, blocks * SEQ, part, dtype=out_type),
        grid_spec=pltpu.PrefetchScalarGridSpec(
            num_scalar_prefetch=1,
            grid=(blocks,),
            in_specs=[
                pl.BlockSpec((1, SEQ, 4 * HD), lambda g, *p: (g + start, 0, 0)),
                lead_block(SEQ, 4 * HD),
                lead_block(rows, SEQ),
            ]
            + [whole(n, part, cols), whole(n, rows, part)],
            out_specs=stack_block(n, SEQ, part),
        ),
        compiler_params=pltpu.CompilerParams(vmem_limit_bytes=VMEM_LIMIT),
        cost_estimate=cost(2 * blocks * SEQ * part * n * cols, 8000000),
    )(flag, a, b, lines, w, misc)


def picked_block(half, part):
    return pl.BlockSpec((1, half, part), lambda g, *p: (p[0][g], 0, 0))


def weight_kernel(terms, *refs):
    out_ref = refs[-1]
    for at, total in terms(*refs[:-1]):
        out_ref[0, :, at : at + total.shape[1]] = total.astype(bf16)


def weight_call(terms, idx, picked, rest, cols, flops, flags=0):
    count = idx.shape[0] - flags
    n, half, part = picked[0].shape
    return pl.pallas_call(
        functools.partial(weight_kernel, terms),
        out_shape=shape(count, part, cols),
        grid_spec=pltpu.PrefetchScalarGridSpec(
            num_scalar_prefetch=1,
            grid=(count,),
            in_specs=[picked_block(half, part)] * len(picked) + [whole(*x.shape) for x in rest],
            out_specs=lead_block(part, cols),
        ),
        compiler_params=pltpu.CompilerParams(vmem_limit_bytes=VMEM_LIMIT),
        cost_estimate=cost(flops * count, 6000000),
    )(idx, *picked, *rest)


def weight_add_kernel(terms, *refs):
    got_ref, keep_ref, send_ref = refs[-3:]
    step = pl.program_id(0)
    for at, total in terms(*refs[:-3]):
        cols = slice(at, at + total.shape[1])
        total = total + got_ref[0, :, cols].astype(f32)

        @pl.when(step == 0)
        def _():
            keep_ref[0, :, cols] = total

        @pl.when(step != 0)
        def _():
            send_ref[0, :, cols] = total.astype(bf16)


def weight_add(terms, idx, picked, rest, got, cols, flops):
    n, half, part = picked[0].shape
    return pl.pallas_call(
        functools.partial(weight_add_kernel, terms),
        out_shape=[shape(1, part, cols, dtype=f32), shape(1, part, cols)],
        grid_spec=pltpu.PrefetchScalarGridSpec(
            num_scalar_prefetch=1,
            grid=(2,),
            in_specs=[picked_block(half, part)] * len(picked)
            + [whole(*x.shape) for x in rest]
            + [lead_block(part, cols)],
            out_specs=[whole(1, part, cols)] * 2,
        ),
        compiler_params=pltpu.CompilerParams(vmem_limit_bytes=VMEM_LIMIT),
        cost_estimate=cost(flops * 2, 6000000),
    )(idx, *picked, *rest, got)


def gate_up_terms(c, idx_ref, n1, n2, d1, d2):
    yield 0, dot_of(n1[0], d1[c], 0, 0) + dot_of(n2[0], d2[c], 0, 0)


def down_terms(idx_ref, g1, g2, m1, m2):
    for c in range(2):
        yield c * m1.shape[2], dot_of(g1[0], m1[c], 0, 0) + dot_of(g2[0], m2[c], 0, 0)


def own_terms(idx_ref, n1, n2, d):
    yield 0, dot_of(n1[0], d[0], 0, 0) + dot_of(n2[0], d[1], 0, 0)


def shared_terms(idx_ref, n1, n2, d, l1, l2):
    left = jnp.where(idx_ref[idx_ref.shape[0] - 1] == 0, n1[0], n2[0])
    yield 0, dot_of(left, d[...], 0, 0)
    yield d.shape[1], dot_of(n1[0], l1[...], 0, 1) + dot_of(n2[0], l2[...], 0, 1)


def own_head(k):
    return (3 * k + 1) // 2


def shared_head(q):
    return 1 + 3 * q


def head_cols(h):
    return slice(h * HD, (h + 1) * HD)


def mix_kernel(n, half, place_ref, w_ref, o_ref, own_ref, far_ref):
    for p, out_ref in enumerate((own_ref, far_ref)):
        second = place_ref[0] ^ p
        total = 0.0
        for k in range(n):
            ok = o_ref[k, p * half : (p + 1) * half, :]
            total = total + dot_of(ok, w_ref[:, head_cols(own_head(k))], 1, 1)
        for q in range(n // 2):
            one, two = o_ref[2 * q, 2 * half :, :], o_ref[2 * q + 1, 2 * half :, :]
            ob = jnp.where(second == 0, one, two)
            total = total + dot_of(ob, w_ref[:, head_cols(shared_head(q))], 1, 1)
        out_ref[...] = total


def attention_out(place, w_out, o, half):
    n = o.shape[0]
    part, cols = w_out.shape
    return pl.pallas_call(
        functools.partial(mix_kernel, n, half),
        out_shape=[shape(half, part, dtype=f32)] * 2,
        grid_spec=pltpu.PrefetchScalarGridSpec(
            num_scalar_prefetch=1,
            grid=(1,),
            in_specs=[whole(part, cols), whole(*o.shape)],
            out_specs=[whole(half, part)] * 2,
        ),
        compiler_params=pltpu.CompilerParams(vmem_limit_bytes=VMEM_LIMIT),
        cost_estimate=cost(4 * half * part * cols, 4000000),
    )(place, w_out, o)


def unmix_kernel(n, half, place_ref, w_ref, own_ref, far_ref, out_ref):
    place = place_ref[0]
    da = (own_ref[...], far_ref[...])
    for k in range(n):
        w = w_ref[:, head_cols(own_head(k))]
        for p in range(2):
            out_ref[k, p * half : (p + 1) * half, :] = dot_of(da[p], w, 1, 0).astype(bf16)
    for q in range(n // 2):
        w = w_ref[:, head_cols(shared_head(q))]
        both = [dot_of(d, w, 1, 0).astype(bf16) for d in da]
        out_ref[2 * q, 2 * half :, :] = jnp.where(place == 0, both[0], both[1])
        out_ref[2 * q + 1, 2 * half :, :] = jnp.where(place == 0, both[1], both[0])


def attention_out_back(place, w_out, own, far, n):
    half, part = own.shape
    cols = w_out.shape[1]
    return pl.pallas_call(
        functools.partial(unmix_kernel, n, half),
        out_shape=shape(n, 3 * half, HD),
        grid_spec=pltpu.PrefetchScalarGridSpec(
            num_scalar_prefetch=1,
            grid=(1,),
            in_specs=[whole(part, cols), whole(half, part), whole(half, part)],
            out_specs=whole(n, 3 * half, HD),
        ),
        compiler_params=pltpu.CompilerParams(vmem_limit_bytes=VMEM_LIMIT),
        cost_estimate=cost(4 * half * part * cols, 4000000),
    )(place, w_out, own, far)


def out_grad_kernel(n, half, place_ref, own_ref, far_ref, o_ref, out_ref):
    place = place_ref[0]
    da = (own_ref[...], far_ref[...])
    for k in range(n):
        total = dot_of(da[0], o_ref[k, :half, :], 0, 0)
        total = total + dot_of(da[1], o_ref[k, half : 2 * half, :], 0, 0)
        out_ref[:, head_cols(own_head(k))] = total.astype(bf16)
    for q in range(n // 2):
        one, two = o_ref[2 * q, 2 * half :, :], o_ref[2 * q + 1, 2 * half :, :]
        total = dot_of(da[0], jnp.where(place == 0, one, two), 0, 0)
        total = total + dot_of(da[1], jnp.where(place == 0, two, one), 0, 0)
        out_ref[:, head_cols(shared_head(q))] = total.astype(bf16)


def out_gradient(place, own, far, o, cols):
    n = o.shape[0]
    half, part = own.shape
    return pl.pallas_call(
        functools.partial(out_grad_kernel, n, half),
        out_shape=shape(part, cols),
        grid_spec=pltpu.PrefetchScalarGridSpec(
            num_scalar_prefetch=1,
            grid=(1,),
            in_specs=[whole(half, part), whole(half, part), whole(*o.shape)],
            out_specs=whole(part, cols),
        ),
        compiler_params=pltpu.CompilerParams(vmem_limit_bytes=VMEM_LIMIT),
        cost_estimate=cost(4 * half * part * cols, 4000000),
    )(place, own, far, o)


def swap(x, axis, size, k):
    return lax.ppermute(x, axis, [(n, n ^ k) for n in range(size)])


def shift_rows(x, start, size):
    return lax.dynamic_slice_in_dim(x, start, size, axis=0)


def exchange(x, axis):
    return lax.all_to_all(x, axis, split_axis=0, concat_axis=0, tiled=True)


def to_all(x, axis, n):
    return exchange(jnp.broadcast_to(x[None], (n,) + x.shape), axis)


def after(x, *others):
    return lax.optimization_barrier((x,) + others)[0]


def per_device(
    dp_size,
    wid_size,
    tokens,
    cotangent,
    lengths,
    w_project,
    w_beta,
    w_out,
    w_gate_up,
    w_down,
    gain_attn,
    gain_ffn,
):
    wid = lax.axis_index("wid")
    hid = lax.axis_index("hid")
    dp = lax.axis_index("dp")
    ws = range(wid_size)
    rows, part = tokens.shape
    half = rows // 2
    width = part * wid_size
    ff = w_down.shape[1] // wid_size
    heads = w_beta.shape[1]
    per_half = half // SEQ

    def hid_swap(x):
        return swap(x, "hid", 2, 1)

    half_b = (wid & 1) ^ hid
    my_head = own_head(wid)
    my_shared = shared_head(wid // 2)

    x_own = shift_rows(tokens, hid * half, half)
    g_own = shift_rows(cotangent, hid * half, half)

    spare = jnp.zeros((16 - heads - 3, part), bf16)
    length_line = jnp.broadcast_to(lengths.astype(bf16)[:, None], (1, part))
    misc_here = jnp.concatenate(
        [w_beta.T, gain_attn[None], gain_ffn[None], length_line, spare], axis=0
    )
    gathered = to_all(jnp.concatenate([x_own, misc_here], axis=0), "wid", wid_size)
    xs_own, misc = gathered[:, :half], gathered[:, half:]
    xs_far = hid_swap(xs_own)
    len_abs = misc[:, heads + 2, 0].astype(jnp.int32)

    def heads_for(w):
        a = w_project[:, :, head_cols(own_head(w))].reshape(part, 4 * HD)
        b = w_project[:, :, head_cols(shared_head(w // 2))].reshape(part, 4 * HD)
        return jnp.concatenate([a, b], axis=1)

    side = dp & 1
    ffh = ff // 2

    def ffn_for(w):
        at = w * ff + side * ffh
        cut = lax.dynamic_slice_in_dim(w_gate_up, at, ffh, axis=2).reshape(part, 2 * ffh)
        return jnp.concatenate([cut, lax.dynamic_slice_in_dim(w_down, at, ffh, axis=1)], axis=1)

    ffn_own = exchange(after(jnp.stack([ffn_for(w) for w in ws]), gathered), "wid")
    proj_w = exchange(after(jnp.stack([heads_for(w) for w in ws]), ffn_own), "wid")
    ffn_other = swap(ffn_own, "dp", dp_size, 1)
    side = side.astype(jnp.int32)[None]

    def lens_of(place):
        return lax.dynamic_slice_in_dim(len_abs, place * per_half, per_half)

    lens_own, lens_far = lens_of(hid), lens_of(1 - hid)
    lens = jnp.concatenate([lens_own, lens_far, lens_of(wid & 1)])
    slot = jnp.arange(SEQ, dtype=jnp.int32)
    valid_half = (slot[None] < lens_own[:, None]).astype(f32).reshape(half, 1)

    a_own, b_own, l_own, r_own, n1_own = project(xs_own, proj_w, misc)
    a_far, b_far, l_far, r_far, n1_far = project(xs_far, proj_w, misc)

    def pick_b(own, far):
        return jnp.where(half_b == 0, own, far)

    pairs = jnp.concatenate([a_own, a_far, pick_b(b_own, b_far)], axis=0)

    def line_of(lines, h):
        return lax.dynamic_slice_in_dim(lines, h, 1, axis=1)

    logit_pairs = jnp.concatenate(
        [
            line_of(l_own, my_head),
            line_of(l_far, my_head),
            line_of(pick_b(l_own, l_far), my_shared),
        ],
        axis=0,
    )
    gs_own = exchange(
        after(jnp.broadcast_to(g_own[None], (wid_size,) + g_own.shape), proj_w), "wid"
    )
    attended, inv, carry, prob = attention_forward(lens, after(pairs, ffn_other), logit_pairs)
    o_all = to_all(after(attended, gs_own).reshape(-1, HD), "wid", wid_size)
    place = hid.astype(jnp.int32)[None]
    attn_own, attn_far = attention_out(place, w_out, o_all, half)
    hidden = x_own.astype(f32) + attn_own + hid_swap(attn_far)

    gain_one = gain_attn[None].astype(f32)
    gain_two = gain_ffn[None].astype(f32)
    hs_own = to_all(hidden.astype(bf16), "wid", wid_size)
    hs_far = hid_swap(hs_own)
    gs_far = hid_swap(gs_own)
    n2_own, m_own, d_own, dn_own, s_own, r2_own = feed_forward(
        lens_own, side, hs_own, gs_own, ffn_own, ffn_other, misc, f32
    )
    n2_far, m_far, d_far, dn_far, s_far, r2_far = feed_forward(
        lens_far, side, hs_far, gs_far, ffn_own, ffn_other, misc, bf16
    )

    def partial(own, far):
        return (own + hid_swap(far).astype(f32)).astype(bf16)

    def line_sum(own, far, late):
        here = (own + hid_swap(far)).reshape(-1, 128)
        others = [swap(here, "wid", wid_size, k) for k in range(1, wid_size)]
        others = lax.optimization_barrier((*others, late))[:-1]
        total = here + sum(others)
        return total.reshape(-1, 1) * (1.0 / width)

    dn_here = partial(dn_own, dn_far)
    dn_got = exchange(dn_here, "wid")
    mean_two = line_sum(s_own, s_far, dn_got)
    grad_normed_two = jnp.sum(dn_got.astype(f32), axis=0)

    chunk = width // dp_size
    direct = dp_size == wid_size
    sub = chunk // wid_size

    def dp_pieces(terms, picked, rest, cols, flags, ts):
        if direct:
            idx = jnp.stack([dp ^ t for t in ts]).astype(jnp.int32)
            idx = jnp.concatenate([idx, *flags])
            return weight_call(terms, idx, picked, rest, cols, 2 * half * part * cols, len(flags))
        idx = jnp.concatenate([jnp.arange(wid_size, dtype=jnp.int32), *flags])
        full = weight_call(terms, idx, picked, rest, cols, 2 * half * part * cols, len(flags))
        full = full.reshape(width, -1)
        return jnp.stack([shift_rows(full, (dp ^ t) * chunk, chunk) for t in ts])

    def dp_odd(terms, picked, rest, cols, flags=()):
        return dp_pieces(terms, picked, rest, cols, flags, range(1, dp_size, 2))

    def dp_even(terms, picked, rest, cols, got, flags=()):
        if direct and dp_size == 4:
            idx = jnp.stack([dp, dp ^ 2]).astype(jnp.int32)
            idx = jnp.concatenate([idx, *flags])
            flops = 2 * half * part * cols
            keep, send = weight_add(terms, idx, picked, rest, got, cols, flops)
            return keep, swap(send, "dp", dp_size, 2)
        here = dp_pieces(terms, picked, rest, cols, flags, range(0, dp_size, 2))
        return dp_send(here.astype(f32) + got.astype(f32))

    def dp_send(held, k=2):
        return held[0::2], swap(held[1::2].astype(bf16), "dp", dp_size, k)

    def dp_take(keep, got, k=2):
        held = keep + got.astype(f32)
        while held.shape[0] > 1:
            k *= 2
            keep, got = dp_send(held, k)
            held = keep + got.astype(f32)
        return held[0]

    def dp_sum(pieces, *late):
        odd, even = jnp.stack(pieces[1::2]), jnp.stack(pieces[0::2])
        got = after(swap(odd.astype(bf16), "dp", dp_size, 1), *late)
        return dp_take(*dp_send(even.astype(f32) + got.astype(f32)))

    def to_rows(x):
        return exchange(x.astype(bf16).reshape(wid_size, sub, -1), "wid")

    gate_up = [functools.partial(gate_up_terms, c) for c in range(2)]
    n2_both, gs_both = (n2_own, n2_far), (gs_own, gs_far)
    odd = [dp_odd(gate_up[0], n2_both, (after(d_own, dn_here), d_far), ff)]
    odd.append(dp_odd(gate_up[1], n2_both, (after(d_own, odd[0]), d_far), ff))
    odd.append(dp_odd(down_terms, gs_both, (after(m_own, odd[1]), m_far), ff))
    got_odd = [swap(x, "dp", dp_size, 1) for x in odd]

    grad_half = g_own.astype(f32) * valid_half
    grad_hidden = grad_half + r2_own * (
        grad_normed_two * gain_two - r2_own * hidden * mean_two
    )
    gain_two_part = jnp.sum(grad_normed_two * hidden * r2_own, axis=0)
    da_own = after(grad_hidden.astype(bf16), odd[2])
    da_far = hid_swap(da_own)
    keep_0, next_0 = dp_even(gate_up[0], n2_both, (after(d_own, odd[2]), d_far), ff, got_odd[0])
    do_here = attention_out_back(place, w_out, after(da_own, keep_0), da_far, wid_size)
    do_pieces = exchange(do_here, "wid")
    ffn_own_out, ffn_far_out = feed_forward_out(
        side, after(m_own, do_here), m_far, ffn_own, ffn_other
    )
    g_out = out_gradient(place, after(da_own, ffn_far_out), da_far, o_all, w_out.shape[1])
    do_got = do_pieces.reshape(wid_size, -1, SEQ, HD)

    pairs_a, lines_a, sums_a = attention_backward(
        lens, pairs, logit_pairs, inv, carry, prob, after(do_got, ffn_far_out, g_out), 0, 2 * per_half
    )

    head_iota = lax.broadcasted_iota(jnp.int32, (1, 16, 1), 1)
    m_then = after(m_own, pairs_a)
    keep_2, next_2 = dp_even(down_terms, gs_both, (m_then, m_far), ff, got_odd[2])
    right_own = pairs_a.reshape(2, half, 4 * HD)
    ffn_here = after(partial(ffn_own_out, after(ffn_far_out, do_got)), pairs_a)
    ffn_back = exchange(ffn_here, "wid")

    n1_both = (n1_own, n1_far)
    own_odd = dp_odd(own_terms, n1_both, (right_own,), 4 * HD)
    own_got = swap(own_odd, "dp", dp_size, 1)
    d_then = after(d_own, own_odd)
    keep_1, next_1 = dp_even(gate_up[1], n2_both, (d_then, d_far), ff, got_odd[1])
    pairs_b, lines_b, sums_b = attention_backward(
        lens, pairs, logit_pairs, inv, carry, prob, after(do_got, own_odd, keep_1, next_0), 2 * per_half, per_half
    )

    def spread(a, b, at):
        own = a[at * per_half : (at + 1) * per_half]
        return own, jnp.where(half_b == at, b, 0.0)

    def lines_at(at):
        own, shared = spread(lines_a, lines_b, at)
        own = jnp.where(head_iota == my_head, own, 0.0)
        shared = jnp.where(head_iota == my_shared, shared, 0.0)
        return (own + shared).astype(bf16)

    def flat_lines(x):
        flat = jnp.swapaxes(x, 0, 1).reshape(16, half)
        return jnp.concatenate([flat, jnp.zeros((128 - 16, half), bf16)], axis=0)

    lines_own, lines_far = lines_at(0), lines_at(1)
    flat_own, flat_far = flat_lines(lines_own), flat_lines(lines_far)
    right_shared = after(pairs_b, keep_2, next_1).reshape(half, 4 * HD)

    flat_both = (flat_own, flat_far)
    half_flag = (half_b.astype(jnp.int32)[None],)
    shared_odd = dp_odd(shared_terms, n1_both, (right_shared, *flat_both), 5 * HD, half_flag)
    shared_got = swap(shared_odd, "dp", dp_size, 1)
    fine = part // dp_size
    to_place = [
        (c * wid_size + w, w * dp_size + c) for c in range(dp_size) for w in range(wid_size)
    ]

    def dp_fine(x, *late):
        return dp_sum([shift_rows(x, (dp ^ t) * fine, fine) for t in range(dp_size)], *late)

    out_pieces = [shift_rows(g_out, (dp ^ t) * fine, fine) for t in range(dp_size)]
    out_got = swap(jnp.stack(out_pieces[1::2]), "dp", dp_size, 1)
    flags = [(half_b == p).astype(jnp.int32)[None] for p in range(2)]
    back_b = after(pairs_b, shared_odd, own_got, ffn_back)
    dn1_far = project_back(flags[1], pairs_a, per_half, back_b, lines_far, proj_w, misc, bf16)
    right_own = after(right_own, dn1_far, own_got)
    keep_own, next_own = dp_even(own_terms, n1_both, (right_own,), 4 * HD, own_got)
    back_b = after(back_b, keep_own)
    dn1_own = project_back(flags[0], pairs_a, 0, back_b, lines_own, proj_w, misc, f32)
    dn1_here = partial(dn1_own, dn1_far)
    dn1_got = exchange(dn1_here, "wid")
    right_shared = after(right_shared, dn1_here, shared_got)
    keep_shared, next_shared = dp_even(
        shared_terms, n1_both, (right_shared, *flat_both), 5 * HD, shared_got, half_flag
    )
    next_own, next_shared = lax.optimization_barrier((next_own, next_shared, dn1_got))[:2]
    next_2 = after(next_2, dn1_got)
    sums = [sum(spread(sums_a, sums_b, p)) for p in range(2)]
    mean_one = line_sum(*sums, dn1_got)
    grad_normed_one = jnp.sum(dn1_got.astype(f32), axis=0)
    ffn = jnp.sum(ffn_back.astype(f32), axis=0)

    source = x_own.astype(f32)
    r1_half = r_own.reshape(half, 1)
    gain_one_part = jnp.sum(grad_normed_one * source * r1_half, axis=0)
    input_half = grad_hidden + r1_half * (
        grad_normed_one * gain_one - r1_half * source * mean_one
    )

    def whole_rows(x):
        other = hid_swap(x)
        return jnp.concatenate(
            [jnp.where(hid == 0, x, other), jnp.where(hid == 0, other, x)], axis=0
        )

    ffn_sums = [dp_take(keep_0, next_0), dp_take(keep_1, next_1), dp_take(keep_2, next_2)]
    ffn_sums = after(jnp.concatenate(ffn_sums, axis=1).astype(bf16), dn1_got)
    ffn_rows = to_rows(ffn_sums)
    input_grad = whole_rows(after(input_half.astype(bf16), ffn_sums))
    output = whole_rows(after(((hidden + ffn) * valid_half).astype(bf16), ffn_sums))

    proj_sums = [dp_take(keep_own, next_own), dp_take(keep_shared, next_shared)]
    proj_sums = jnp.concatenate(proj_sums, axis=1).astype(bf16)
    out_even = jnp.stack(out_pieces[0::2]).astype(f32)
    out_got = after(out_got, dn1_got)
    out_sum = dp_take(*dp_send(out_even + out_got.astype(f32))).astype(bf16)
    out_sum = after(out_sum, proj_sums, ffn_rows)
    out_out = lax.ppermute(out_sum, ("dp", "wid"), to_place).astype(f32)
    gain_part = after(jnp.stack([gain_one_part, gain_two_part], axis=1), proj_sums, ffn_rows)
    gain_part = gain_part + hid_swap(gain_part)
    gain_sum = lax.ppermute(dp_fine(gain_part), ("dp", "wid"), to_place)

    got = ffn_rows[:, :, : 2 * ff].reshape(wid_size, sub, 2, 2, ffh)
    gate, up = (
        jnp.concatenate([got[w, :, c, k] for w in ws for c in range(2)], axis=1) for k in range(2)
    )
    down = jnp.concatenate([ffn_rows[w, :, 2 * ff :] for w in ws], axis=1)
    out_gate_up = jnp.stack([gate, up], axis=1).astype(f32)
    out_down = down.astype(f32)

    got = to_rows(after(proj_sums, ffn_rows)).astype(f32)
    a = [got[w, :, : 4 * HD] for w in ws]
    b = [got[w, :, 4 * HD : 8 * HD] for w in ws]
    proj_rows = [a[0], b[0] + b[1], a[1], a[2], b[2] + b[3], a[3]]
    out_project = jnp.concatenate([p.reshape(sub, 4, HD) for p in proj_rows], axis=2)
    out_beta = jnp.sum(got[:, :, 8 * HD : 8 * HD + heads], axis=0)


    return (
        output,
        input_grad,
        out_project,
        out_beta,
        out_out,
        out_gate_up,
        out_down,
        gain_sum[:, 0],
        gain_sum[:, 1],
    )


def solution(mesh):
    return jax.shard_map(
        functools.partial(per_device, mesh.shape["dp"], mesh.shape["wid"]),
        mesh=mesh,
        in_specs=(
            P("dp", "wid"),
            P("dp", "wid"),
            P(("dp", "wid")),
            P("wid", None, "hid"),
            P("wid", "hid"),
            P("wid", "hid"),
            P("wid", None, "hid"),
            P("wid", "hid"),
            P("wid"),
            P("wid"),
        ),
        out_specs=(
            P("dp", "wid"),
            P("dp", "wid"),
            P(("dp", "wid"), None, "hid"),
            P(("dp", "wid"), "hid"),
            P(("dp", "wid"), "hid"),
            P(("dp", "wid"), None, "hid"),
            P(("dp", "wid"), "hid"),
            P(("dp", "wid")),
            P(("dp", "wid")),
        ),
        check_vma=False,
    )
```

```python
import functools

import jax
import jax.numpy as jnp
from jax import lax
from jax.experimental import pallas as pl
from jax.experimental.pallas import tpu as pltpu
from jax.sharding import PartitionSpec as P

f32 = jnp.float32
bf16 = jnp.bfloat16

SEQ = 256
HD = 128


def dot_of(a, b, ca, cb):
    return lax.dot_general(a, b, (((ca,), (cb,)), ((), ())), preferred_element_type=f32)


def halves_of(a):
    high = a.astype(bf16)
    return high, (a - high.astype(f32)).astype(bf16)


def mul(a, b, ca=1, cb=0, passes=3):
    if passes == 1:
        return dot_of(a.astype(bf16), b.astype(bf16), ca, cb)
    if a.dtype == bf16:
        bh, bl = halves_of(b)
        return dot_of(a, bh, ca, cb) + dot_of(a, bl, ca, cb)
    if b.dtype == bf16:
        ah, al = halves_of(a)
        return dot_of(ah, b, ca, cb) + dot_of(al, b, ca, cb)
    ah, al = halves_of(a)
    bh, bl = halves_of(b)
    return dot_of(ah, bh, ca, cb) + (dot_of(ah, bl, ca, cb) + dot_of(al, bh, ca, cb))


def iotas():
    rows = lax.broadcasted_iota(jnp.int32, (SEQ, SEQ), 0)
    cols = lax.broadcasted_iota(jnp.int32, (SEQ, SEQ), 1)
    return rows, cols


def prepare(raw, logit_row, i, j):
    eye = i == j
    raw_f = raw.astype(f32)
    norm = lax.rsqrt(jnp.sum(raw_f * raw_f, axis=1, keepdims=True) + 1e-6)
    norm_row = jnp.sum(jnp.where(eye, norm, 0.0), axis=0, keepdims=True)
    beta_row = 2.0 / (1.0 + jnp.exp(-logit_row))
    beta = jnp.sum(jnp.where(eye, beta_row, 0.0), axis=1, keepdims=True)
    return raw_f, norm, norm_row, beta_row, beta


def inverses(lowers, i, j):
    eye = jnp.where(i == j, 1.0, 0.0)
    first = ((i >> 1) == (j >> 1)) & (i > j)
    inv = [eye - jnp.where(first, n, 0.0) for n in lowers]
    s = 1
    while (1 << s) < SEQ:
        mask = ((i >> (s + 1)) == (j >> (s + 1))) & ((i >> s) > (j >> s))
        mids = [mul(d, jnp.where(mask, n, 0.0)) for d, n in zip(inv, lowers)]
        inv = [d - mul(x, d) for d, x in zip(inv, mids)]
        s += 1
    return inv


def forward_kernel(count, len_ref, x_ref, l_ref, o_ref, inv_ref, carry_ref, prob_ref):
    base = pl.program_id(0) * count
    i, j = iotas()
    row = lax.broadcasted_iota(jnp.int32, (SEQ, 1), 0)
    xs = [x_ref[t] for t in range(count)]
    qs = [x[:, 0:HD] for x in xs]
    ks = [x[:, HD : 2 * HD] for x in xs]
    vs = [x[:, 2 * HD : 3 * HD] for x in xs]
    us = [x[:, 3 * HD : 4 * HD] for x in xs]
    pre = [prepare(us[t], l_ref[t], i, j) for t in range(count)]
    lowers = [
        p[4] * jnp.where(i > j, dot_of(u, u, 1, 1) * p[1] * p[2], 0.0) for u, p in zip(us, pre)
    ]
    inv = inverses(lowers, i, j)
    bs = [jnp.where(i > j, dot_of(u, k, 1, 1) * p[1], 0.0) for u, k, p in zip(us, ks, pre)]
    carries = [mul(d * p[3], b) for d, p, b in zip(inv, pre, bs)]
    as_ = [jnp.where(i >= j, dot_of(q, u, 1, 1) * p[2], 0.0) for q, u, p in zip(qs, us, pre)]
    scores = [
        (dot_of(q, k, 1, 1) - mul(a, c)) * (HD**-0.5) for q, k, a, c in zip(qs, ks, as_, carries)
    ]
    for t in range(count):
        length = len_ref[base + t]
        score = jnp.where((j <= i) & (j < length), scores[t], -1e30)
        weight = jnp.exp(score - jnp.max(score, axis=1, keepdims=True))
        prob = weight * (1.0 / jnp.sum(weight, axis=1, keepdims=True))
        out = jnp.where(row < length, mul(prob, vs[t], passes=1), 0.0)
        o_ref[t] = out.astype(bf16)
        inv_ref[t] = inv[t]
        carry_ref[t] = carries[t]
        prob_ref[t] = prob


def to_row(col, eye):
    return jnp.sum(jnp.where(eye, col, 0.0), axis=0, keepdims=True)


def backward_kernel(
    count,
    start,
    len_ref,
    x_ref,
    l_ref,
    inv_ref,
    carry_ref,
    prob_ref,
    do_ref,
    dx_ref,
    dl_ref,
    sum_ref,
):
    base = (pl.program_id(0) + start) * count
    i, j = iotas()
    row = lax.broadcasted_iota(jnp.int32, (SEQ, 1), 0)
    for t in range(count):
        x = x_ref[t]
        q, k = x[:, 0:HD], x[:, HD : 2 * HD]
        v, u = x[:, 2 * HD : 3 * HD], x[:, 3 * HD : 4 * HD]
        do = do_ref[0, t].astype(f32) + do_ref[1, t].astype(f32)
        do = (do + (do_ref[2, t].astype(f32) + do_ref[3, t].astype(f32))).astype(bf16)
        do = jnp.where(row < len_ref[base + t], do, jnp.zeros_like(do))
        inv, carry, prob = inv_ref[t], carry_ref[t], prob_ref[t]
        raw, norm, norm_row, beta_row, beta = prepare(u, l_ref[t], i, j)
        gram = jnp.where(i > j, dot_of(u, u, 1, 1) * norm * norm_row, 0.0)
        a = jnp.where(i >= j, dot_of(q, u, 1, 1) * norm_row, 0.0)
        b = jnp.where(i > j, dot_of(u, k, 1, 1) * norm, 0.0)
        m = inv * beta_row
        dv = mul(prob, do, 0, 0, passes=1)
        dprob = dot_of(do, v, 1, 1)
        ds = prob * (dprob - jnp.sum(dprob * prob, axis=1, keepdims=True)) * (HD**-0.5)
        da = jnp.where(i >= j, -mul(ds, carry, 1, 1), 0.0)
        dc = -mul(a, ds, 0, 0)
        dm = mul(dc, b, 1, 1)
        db = jnp.where(i > j, mul(m, dc, 0, 0), 0.0)
        dn = jnp.where(i > j, -mul(mul(inv, dm, 0, 0), m, 1, 1), 0.0)
        dgram = beta * dn
        dbeta = jnp.sum(dm * inv, axis=0, keepdims=True)
        dbeta_col = jnp.sum(dn * gram, axis=1, keepdims=True)
        dbeta = dbeta + jnp.sum(jnp.where(i == j, dbeta_col, 0.0), axis=0, keepdims=True)
        dq = mul(ds, k, passes=1) + mul(da * norm_row, u, passes=1)
        dk = mul(ds, q, 0, 0, passes=1) + mul(db * norm, u, 0, 0, passes=1)
        dw = mul(da, q, 0, 0, passes=1) + mul(db, k, passes=1)
        dw = dw + mul(dgram * norm_row, u, passes=1) + mul(dgram * norm, u, 0, 0, passes=1)
        du = norm * dw - (norm * norm * norm) * raw * jnp.sum(dw * raw, axis=1, keepdims=True)
        dx = jnp.concatenate([dq, dk, dv, du], axis=1)
        dl = dbeta * beta_row * (1.0 - 0.5 * beta_row)
        dx_ref[t] = dx.astype(bf16)
        dl_ref[t] = dl
        total = jnp.sum(dx * x.astype(f32), axis=1, keepdims=True)
        sum_ref[t] = to_row(total, i == j) + dl * l_ref[t]


def block_of(count, *shape):
    return pl.BlockSpec((count,) + shape, lambda g, lens: (g, 0, 0))


def attention_forward(lens, x, logits, count=3):
    pairs = x.shape[0]
    square = jax.ShapeDtypeStruct((pairs, SEQ, SEQ), f32)
    return pl.pallas_call(
        functools.partial(forward_kernel, count),
        out_shape=[jax.ShapeDtypeStruct((pairs, SEQ, HD), bf16), square, square, square],
        grid_spec=pltpu.PrefetchScalarGridSpec(
            num_scalar_prefetch=1,
            grid=(pairs // count,),
            in_specs=[block_of(count, SEQ, 4 * HD), block_of(count, 1, SEQ)],
            out_specs=[block_of(count, SEQ, HD)] + [block_of(count, SEQ, SEQ)] * 3,
        ),
        compiler_params=pltpu.CompilerParams(vmem_limit_bytes=48 << 20),
        cost_estimate=cost(pairs * 1600000000, pairs * 1100000),
    )(lens, x, logits)


def attention_backward(lens, x, logits, inv, carry, prob, do, start, pairs):
    line = jax.ShapeDtypeStruct((pairs, 1, SEQ), f32)

    def from_start(*dims):
        return pl.BlockSpec((1,) + dims, lambda g, lens: (g + start, 0, 0))

    return pl.pallas_call(
        functools.partial(backward_kernel, 1, start),
        out_shape=[jax.ShapeDtypeStruct((pairs, SEQ, 4 * HD), bf16), line, line],
        grid_spec=pltpu.PrefetchScalarGridSpec(
            num_scalar_prefetch=1,
            grid=(pairs,),
            in_specs=[from_start(SEQ, 4 * HD), from_start(1, SEQ)]
            + [from_start(SEQ, SEQ)] * 3
            + [pl.BlockSpec((4, 1, SEQ, HD), lambda g, lens: (0, g + start, 0, 0))],
            out_specs=[block_of(1, SEQ, 4 * HD)] + [block_of(1, 1, SEQ)] * 2,
        ),
        compiler_params=pltpu.CompilerParams(vmem_limit_bytes=48 << 20),
        cost_estimate=cost(pairs * 1400000000, pairs * 1400000),
    )(lens, x, logits, inv, carry, prob, do)


VMEM_LIMIT = 48 << 20
COST_SCALE = 0.001


def shape(*dims, dtype=bf16):
    return jax.ShapeDtypeStruct(dims, dtype)


def rows_block(size, cols):
    return pl.BlockSpec((size, cols), lambda g, *p: (g, 0))


def stack_block(n, size, cols):
    return pl.BlockSpec((n, size, cols), lambda g, *p: (0, g, 0))


def lead_block(size, cols):
    return pl.BlockSpec((1, size, cols), lambda g, *p: (g, 0, 0))


def whole(*dims):
    return pl.BlockSpec(dims, lambda g, *p: (0,) * len(dims))


def cost(flops, moved):
    scale = COST_SCALE
    return pl.CostEstimate(
        flops=int(flops * scale), bytes_accessed=int(moved * scale), transcendentals=0
    )


def project_kernel(n, x_ref, w_ref, misc_ref, a_ref, b_ref, l_ref, r_ref, xg_ref):
    i, j = iotas()
    squares = 0.0
    for k in range(n):
        xf = x_ref[k].astype(f32)
        squares = squares + jnp.sum(xf * xf, axis=1, keepdims=True)
    r = lax.rsqrt(squares * (1.0 / (n * x_ref.shape[2])) + 1e-6)
    acc = 0.0
    logit = 0.0
    for k in range(n):
        gain = misc_ref[k][6:7, :].astype(f32)
        normed = (x_ref[k].astype(f32) * r * gain).astype(bf16)
        xg_ref[k] = normed
        acc = acc + dot_of(normed, w_ref[k], 1, 0)
        logit = logit + dot_of(misc_ref[k], normed, 1, 1)
    out = acc.astype(bf16)
    a_ref[0] = out[:, : 4 * HD]
    b_ref[0] = out[:, 4 * HD :]
    l_ref[0] = logit
    r_ref[0] = to_row(r, i == j)


def project(x, w, misc):
    n, half, part = x.shape
    blocks = half // SEQ
    cols = w.shape[2]
    lines = misc.shape[1]
    return pl.pallas_call(
        functools.partial(project_kernel, n),
        out_shape=[
            shape(blocks, SEQ, 4 * HD),
            shape(blocks, SEQ, 4 * HD),
            shape(blocks, lines, SEQ, dtype=f32),
            shape(blocks, 1, SEQ, dtype=f32),
            shape(n, half, part),
        ],
        grid=(blocks,),
        in_specs=[stack_block(n, SEQ, part), whole(n, part, cols), whole(n, lines, part)],
        out_specs=[
            lead_block(SEQ, 4 * HD),
            lead_block(SEQ, 4 * HD),
            lead_block(lines, SEQ),
            lead_block(1, SEQ),
            stack_block(n, SEQ, part),
        ],
        compiler_params=pltpu.CompilerParams(vmem_limit_bytes=VMEM_LIMIT),
        cost_estimate=cost(2 * half * part * n * cols, 8000000),
    )(x, w, misc)


def ffn_kernel(
    n,
    len_ref,
    side_ref,
    h_ref,
    g_ref,
    wa_ref,
    wb_ref,
    misc_ref,
    n2_ref,
    m_ref,
    d_ref,
    dn_ref,
    sum_ref,
    r_ref,
):
    ff = m_ref.shape[2]
    i, j = iotas()
    row = lax.broadcasted_iota(jnp.int32, (SEQ, 1), 0)
    valid = row < len_ref[pl.program_id(0)]
    squares = 0.0
    for k in range(n):
        hf = h_ref[k].astype(f32)
        squares = squares + jnp.sum(hf * hf, axis=1, keepdims=True)
    r = lax.rsqrt(squares * (1.0 / (n * h_ref.shape[2])) + 1e-6)
    for k in range(n):
        gain = misc_ref[k][7:8, :].astype(f32)
        n2_ref[k] = (h_ref[k].astype(f32) * r * gain).astype(bf16)
    r_ref[...] = r
    both = []
    total = 0.0
    for c, w_ref in enumerate((wa_ref, wb_ref)):
        place = side_ref[0] ^ c
        gate_up = 0.0
        dm = 0.0
        for k in range(n):
            gate_up = gate_up + dot_of(n2_ref[k], w_ref[k, :, : 2 * ff], 1, 0)
            dm = dm + dot_of(g_ref[k], w_ref[k, :, 2 * ff :], 1, 0)
        gate = gate_up[:, :ff]
        up = gate_up[:, ff:]
        sig = 1.0 / (1.0 + jnp.exp(-gate))
        active = gate * sig
        m_ref[place] = jnp.where(valid, active * up, 0.0).astype(bf16)
        dm = jnp.where(valid, dm, 0.0)
        dgate = dm * up * sig * (1.0 + gate * (1.0 - sig))
        dup = dm * active
        total = total + jnp.sum(dgate * gate + dup * up, axis=1, keepdims=True)
        d = jnp.concatenate([dgate, dup], axis=1).astype(bf16)
        d_ref[place] = d
        both.append(d)
    sum_ref[0] = to_row(total, i == j)
    for k in range(n):
        dn = dot_of(both[0], wa_ref[k, :, : 2 * ff], 1, 1)
        dn = dn + dot_of(both[1], wb_ref[k, :, : 2 * ff], 1, 1)
        dn_ref[k] = dn.astype(dn_ref.dtype)


def feed_forward(lens, side, h, g, wa, wb, misc, out_type):
    n, half, part = h.shape
    blocks = half // SEQ
    cols = wa.shape[2]
    ff = cols // 3
    lines = misc.shape[1]
    return pl.pallas_call(
        functools.partial(ffn_kernel, n),
        out_shape=[
            shape(n, half, part),
            shape(2, half, ff),
            shape(2, half, 2 * ff),
            shape(n, half, part, dtype=out_type),
            shape(blocks, 1, SEQ, dtype=f32),
            shape(half, 1, dtype=f32),
        ],
        grid_spec=pltpu.PrefetchScalarGridSpec(
            num_scalar_prefetch=2,
            grid=(blocks,),
            in_specs=[stack_block(n, SEQ, part)] * 2
            + [whole(n, part, cols)] * 2
            + [whole(n, lines, part)],
            out_specs=[
                stack_block(n, SEQ, part),
                stack_block(2, SEQ, ff),
                stack_block(2, SEQ, 2 * ff),
                stack_block(n, SEQ, part),
                lead_block(1, SEQ),
                rows_block(SEQ, 1),
            ],
        ),
        compiler_params=pltpu.CompilerParams(vmem_limit_bytes=VMEM_LIMIT),
        cost_estimate=cost(2 * half * part * n * 10 * ff, 12000000),
    )(lens, side, h, g, wa, wb, misc)


def ffn_out_kernel(n, side_ref, one_ref, two_ref, wa_ref, wb_ref, own_ref, far_ref):
    ff = one_ref.shape[2]
    for m_ref, out_ref in ((one_ref, own_ref), (two_ref, far_ref)):
        first, second = m_ref[side_ref[0]], m_ref[side_ref[0] ^ 1]
        for k in range(n):
            total = dot_of(first, wa_ref[k, :, 2 * ff :], 1, 1)
            total = total + dot_of(second, wb_ref[k, :, 2 * ff :], 1, 1)
            out_ref[k] = total.astype(out_ref.dtype)


def feed_forward_out(side, own, far, wa, wb):
    _, half, ff = own.shape
    n, part, cols = wa.shape
    return pl.pallas_call(
        functools.partial(ffn_out_kernel, n),
        out_shape=[shape(n, half, part, dtype=f32), shape(n, half, part)],
        grid_spec=pltpu.PrefetchScalarGridSpec(
            num_scalar_prefetch=1,
            grid=(half // SEQ,),
            in_specs=[stack_block(2, SEQ, ff)] * 2 + [whole(n, part, cols)] * 2,
            out_specs=[stack_block(n, SEQ, part)] * 2,
        ),
        compiler_params=pltpu.CompilerParams(vmem_limit_bytes=VMEM_LIMIT),
        cost_estimate=cost(8 * half * part * n * ff, 12000000),
    )(side, own, far, wa, wb)


def back_kernel(n, flag_ref, a_ref, b_ref, l_ref, w_ref, misc_ref, out_ref):
    b = b_ref[0]
    b = jnp.where(flag_ref[0] > 0, b, jnp.zeros_like(b))
    d = jnp.concatenate([a_ref[0], b], axis=1)
    line = l_ref[0]
    for k in range(n):
        total = dot_of(d, w_ref[k], 1, 1) + dot_of(line, misc_ref[k], 0, 0)
        out_ref[k] = total.astype(out_ref.dtype)


def project_back(flag, a, start, b, lines, w, misc, out_type):
    n, part, cols = w.shape
    blocks = b.shape[0]
    rows = misc.shape[1]
    return pl.pallas_call(
        functools.partial(back_kernel, n),
        out_shape=shape(n, blocks * SEQ, part, dtype=out_type),
        grid_spec=pltpu.PrefetchScalarGridSpec(
            num_scalar_prefetch=1,
            grid=(blocks,),
            in_specs=[
                pl.BlockSpec((1, SEQ, 4 * HD), lambda g, *p: (g + start, 0, 0)),
                lead_block(SEQ, 4 * HD),
                lead_block(rows, SEQ),
            ]
            + [whole(n, part, cols), whole(n, rows, part)],
            out_specs=stack_block(n, SEQ, part),
        ),
        compiler_params=pltpu.CompilerParams(vmem_limit_bytes=VMEM_LIMIT),
        cost_estimate=cost(2 * blocks * SEQ * part * n * cols, 8000000),
    )(flag, a, b, lines, w, misc)


def picked_block(half, part):
    return pl.BlockSpec((1, half, part), lambda g, *p: (p[0][g], 0, 0))


def weight_kernel(terms, *refs):
    out_ref = refs[-1]
    for at, total in terms(*refs[:-1]):
        out_ref[0, :, at : at + total.shape[1]] = total.astype(bf16)


def weight_call(terms, idx, picked, rest, cols, flops, flags=0):
    count = idx.shape[0] - flags
    n, half, part = picked[0].shape
    return pl.pallas_call(
        functools.partial(weight_kernel, terms),
        out_shape=shape(count, part, cols),
        grid_spec=pltpu.PrefetchScalarGridSpec(
            num_scalar_prefetch=1,
            grid=(count,),
            in_specs=[picked_block(half, part)] * len(picked) + [whole(*x.shape) for x in rest],
            out_specs=lead_block(part, cols),
        ),
        compiler_params=pltpu.CompilerParams(vmem_limit_bytes=VMEM_LIMIT),
        cost_estimate=cost(flops * count, 6000000),
    )(idx, *picked, *rest)


def weight_add_kernel(terms, *refs):
    got_ref, keep_ref, send_ref = refs[-3:]
    step = pl.program_id(0)
    for at, total in terms(*refs[:-3]):
        cols = slice(at, at + total.shape[1])
        total = total + got_ref[0, :, cols].astype(f32)

        @pl.when(step == 0)
        def _():
            keep_ref[0, :, cols] = total

        @pl.when(step != 0)
        def _():
            send_ref[0, :, cols] = total.astype(bf16)


def weight_add(terms, idx, picked, rest, got, cols, flops):
    n, half, part = picked[0].shape
    return pl.pallas_call(
        functools.partial(weight_add_kernel, terms),
        out_shape=[shape(1, part, cols, dtype=f32), shape(1, part, cols)],
        grid_spec=pltpu.PrefetchScalarGridSpec(
            num_scalar_prefetch=1,
            grid=(2,),
            in_specs=[picked_block(half, part)] * len(picked)
            + [whole(*x.shape) for x in rest]
            + [lead_block(part, cols)],
            out_specs=[whole(1, part, cols)] * 2,
        ),
        compiler_params=pltpu.CompilerParams(vmem_limit_bytes=VMEM_LIMIT),
        cost_estimate=cost(flops * 2, 6000000),
    )(idx, *picked, *rest, got)


def gate_up_terms(c, idx_ref, n1, n2, d1, d2):
    yield 0, dot_of(n1[0], d1[c], 0, 0) + dot_of(n2[0], d2[c], 0, 0)


def down_terms(idx_ref, g1, g2, m1, m2):
    for c in range(2):
        yield c * m1.shape[2], dot_of(g1[0], m1[c], 0, 0) + dot_of(g2[0], m2[c], 0, 0)


def own_terms(idx_ref, n1, n2, d):
    yield 0, dot_of(n1[0], d[0], 0, 0) + dot_of(n2[0], d[1], 0, 0)


def shared_terms(idx_ref, n1, n2, d, l1, l2):
    left = jnp.where(idx_ref[idx_ref.shape[0] - 1] == 0, n1[0], n2[0])
    yield 0, dot_of(left, d[...], 0, 0)
    yield d.shape[1], dot_of(n1[0], l1[...], 0, 1) + dot_of(n2[0], l2[...], 0, 1)


def own_head(k):
    return (3 * k + 1) // 2


def shared_head(q):
    return 1 + 3 * q


def head_cols(h):
    return slice(h * HD, (h + 1) * HD)


def mix_kernel(n, half, place_ref, w_ref, o_ref, own_ref, far_ref):
    for p, out_ref in enumerate((own_ref, far_ref)):
        second = place_ref[0] ^ p
        total = 0.0
        for k in range(n):
            ok = o_ref[k, p * half : (p + 1) * half, :]
            total = total + dot_of(ok, w_ref[:, head_cols(own_head(k))], 1, 1)
        for q in range(n // 2):
            one, two = o_ref[2 * q, 2 * half :, :], o_ref[2 * q + 1, 2 * half :, :]
            ob = jnp.where(second == 0, one, two)
            total = total + dot_of(ob, w_ref[:, head_cols(shared_head(q))], 1, 1)
        out_ref[...] = total


def attention_out(place, w_out, o, half):
    n = o.shape[0]
    part, cols = w_out.shape
    return pl.pallas_call(
        functools.partial(mix_kernel, n, half),
        out_shape=[shape(half, part, dtype=f32)] * 2,
        grid_spec=pltpu.PrefetchScalarGridSpec(
            num_scalar_prefetch=1,
            grid=(1,),
            in_specs=[whole(part, cols), whole(*o.shape)],
            out_specs=[whole(half, part)] * 2,
        ),
        compiler_params=pltpu.CompilerParams(vmem_limit_bytes=VMEM_LIMIT),
        cost_estimate=cost(4 * half * part * cols, 4000000),
    )(place, w_out, o)


def unmix_kernel(n, half, place_ref, w_ref, own_ref, far_ref, out_ref):
    place = place_ref[0]
    da = (own_ref[...], far_ref[...])
    for k in range(n):
        w = w_ref[:, head_cols(own_head(k))]
        for p in range(2):
            out_ref[k, p * half : (p + 1) * half, :] = dot_of(da[p], w, 1, 0).astype(bf16)
    for q in range(n // 2):
        w = w_ref[:, head_cols(shared_head(q))]
        both = [dot_of(d, w, 1, 0).astype(bf16) for d in da]
        out_ref[2 * q, 2 * half :, :] = jnp.where(place == 0, both[0], both[1])
        out_ref[2 * q + 1, 2 * half :, :] = jnp.where(place == 0, both[1], both[0])


def attention_out_back(place, w_out, own, far, n):
    half, part = own.shape
    cols = w_out.shape[1]
    return pl.pallas_call(
        functools.partial(unmix_kernel, n, half),
        out_shape=shape(n, 3 * half, HD),
        grid_spec=pltpu.PrefetchScalarGridSpec(
            num_scalar_prefetch=1,
            grid=(1,),
            in_specs=[whole(part, cols), whole(half, part), whole(half, part)],
            out_specs=whole(n, 3 * half, HD),
        ),
        compiler_params=pltpu.CompilerParams(vmem_limit_bytes=VMEM_LIMIT),
        cost_estimate=cost(4 * half * part * cols, 4000000),
    )(place, w_out, own, far)


def out_grad_kernel(n, half, place_ref, own_ref, far_ref, o_ref, out_ref):
    place = place_ref[0]
    da = (own_ref[...], far_ref[...])
    for k in range(n):
        total = dot_of(da[0], o_ref[k, :half, :], 0, 0)
        total = total + dot_of(da[1], o_ref[k, half : 2 * half, :], 0, 0)
        out_ref[:, head_cols(own_head(k))] = total.astype(bf16)
    for q in range(n // 2):
        one, two = o_ref[2 * q, 2 * half :, :], o_ref[2 * q + 1, 2 * half :, :]
        total = dot_of(da[0], jnp.where(place == 0, one, two), 0, 0)
        total = total + dot_of(da[1], jnp.where(place == 0, two, one), 0, 0)
        out_ref[:, head_cols(shared_head(q))] = total.astype(bf16)


def out_gradient(place, own, far, o, cols):
    n = o.shape[0]
    half, part = own.shape
    return pl.pallas_call(
        functools.partial(out_grad_kernel, n, half),
        out_shape=shape(part, cols),
        grid_spec=pltpu.PrefetchScalarGridSpec(
            num_scalar_prefetch=1,
            grid=(1,),
            in_specs=[whole(half, part), whole(half, part), whole(*o.shape)],
            out_specs=whole(part, cols),
        ),
        compiler_params=pltpu.CompilerParams(vmem_limit_bytes=VMEM_LIMIT),
        cost_estimate=cost(4 * half * part * cols, 4000000),
    )(place, own, far, o)


def swap(x, axis, size, k):
    return lax.ppermute(x, axis, [(n, n ^ k) for n in range(size)])


def shift_rows(x, start, size):
    return lax.dynamic_slice_in_dim(x, start, size, axis=0)


def exchange(x, axis):
    return lax.all_to_all(x, axis, split_axis=0, concat_axis=0, tiled=True)


def to_all(x, axis, n):
    return exchange(jnp.broadcast_to(x[None], (n,) + x.shape), axis)


def after(x, *others):
    return lax.optimization_barrier((x,) + others)[0]


def per_device(
    dp_size,
    wid_size,
    tokens,
    cotangent,
    lengths,
    w_project,
    w_beta,
    w_out,
    w_gate_up,
    w_down,
    gain_attn,
    gain_ffn,
):
    wid = lax.axis_index("wid")
    hid = lax.axis_index("hid")
    dp = lax.axis_index("dp")
    ws = range(wid_size)
    rows, part = tokens.shape
    half = rows // 2
    width = part * wid_size
    ff = w_down.shape[1] // wid_size
    heads = w_beta.shape[1]
    per_half = half // SEQ

    def hid_swap(x):
        return swap(x, "hid", 2, 1)

    half_b = (wid & 1) ^ hid
    my_head = own_head(wid)
    my_shared = shared_head(wid // 2)

    x_own = shift_rows(tokens, hid * half, half)
    g_own = shift_rows(cotangent, hid * half, half)

    spare = jnp.zeros((16 - heads - 3, part), bf16)
    length_line = jnp.broadcast_to(lengths.astype(bf16)[:, None], (1, part))
    misc_here = jnp.concatenate(
        [w_beta.T, gain_attn[None], gain_ffn[None], length_line, spare], axis=0
    )
    gathered = to_all(jnp.concatenate([x_own, misc_here], axis=0), "wid", wid_size)
    xs_own, misc = gathered[:, :half], gathered[:, half:]
    xs_far = hid_swap(xs_own)
    len_abs = misc[:, heads + 2, 0].astype(jnp.int32)

    def heads_for(w):
        a = w_project[:, :, head_cols(own_head(w))].reshape(part, 4 * HD)
        b = w_project[:, :, head_cols(shared_head(w // 2))].reshape(part, 4 * HD)
        return jnp.concatenate([a, b], axis=1)

    side = dp & 1
    ffh = ff // 2

    def ffn_for(w):
        at = w * ff + side * ffh
        cut = lax.dynamic_slice_in_dim(w_gate_up, at, ffh, axis=2).reshape(part, 2 * ffh)
        return jnp.concatenate([cut, lax.dynamic_slice_in_dim(w_down, at, ffh, axis=1)], axis=1)

    ffn_own = exchange(after(jnp.stack([ffn_for(w) for w in ws]), gathered), "wid")
    proj_w = exchange(after(jnp.stack([heads_for(w) for w in ws]), ffn_own), "wid")
    ffn_other = swap(ffn_own, "dp", dp_size, 1)
    side = side.astype(jnp.int32)[None]

    def lens_of(place):
        return lax.dynamic_slice_in_dim(len_abs, place * per_half, per_half)

    lens_own, lens_far = lens_of(hid), lens_of(1 - hid)
    lens = jnp.concatenate([lens_own, lens_far, lens_of(wid & 1)])
    slot = jnp.arange(SEQ, dtype=jnp.int32)
    valid_half = (slot[None] < lens_own[:, None]).astype(f32).reshape(half, 1)

    a_own, b_own, l_own, r_own, n1_own = project(xs_own, proj_w, misc)
    a_far, b_far, l_far, r_far, n1_far = project(xs_far, proj_w, misc)

    def pick_b(own, far):
        return jnp.where(half_b == 0, own, far)

    pairs = jnp.concatenate([a_own, a_far, pick_b(b_own, b_far)], axis=0)

    def line_of(lines, h):
        return lax.dynamic_slice_in_dim(lines, h, 1, axis=1)

    logit_pairs = jnp.concatenate(
        [
            line_of(l_own, my_head),
            line_of(l_far, my_head),
            line_of(pick_b(l_own, l_far), my_shared),
        ],
        axis=0,
    )
    gs_own = exchange(
        after(jnp.broadcast_to(g_own[None], (wid_size,) + g_own.shape), proj_w), "wid"
    )
    attended, inv, carry, prob = attention_forward(lens, after(pairs, ffn_other), logit_pairs)
    o_all = to_all(after(attended, gs_own).reshape(-1, HD), "wid", wid_size)
    place = hid.astype(jnp.int32)[None]
    attn_own, attn_far = attention_out(place, w_out, o_all, half)
    hidden = x_own.astype(f32) + attn_own + hid_swap(attn_far)

    gain_one = gain_attn[None].astype(f32)
    gain_two = gain_ffn[None].astype(f32)
    hs_own = to_all(hidden.astype(bf16), "wid", wid_size)
    hs_far = hid_swap(hs_own)
    gs_far = hid_swap(gs_own)
    n2_own, m_own, d_own, dn_own, s_own, r2_own = feed_forward(
        lens_own, side, hs_own, gs_own, ffn_own, ffn_other, misc, f32
    )
    n2_far, m_far, d_far, dn_far, s_far, r2_far = feed_forward(
        lens_far, side, hs_far, gs_far, ffn_own, ffn_other, misc, bf16
    )

    def partial(own, far):
        return (own + hid_swap(far).astype(f32)).astype(bf16)

    def line_sum(own, far, late):
        here = (own + hid_swap(far)).reshape(-1, 128)
        others = [swap(here, "wid", wid_size, k) for k in range(1, wid_size)]
        others = lax.optimization_barrier((*others, late))[:-1]
        total = here + sum(others)
        return total.reshape(-1, 1) * (1.0 / width)

    dn_here = partial(dn_own, dn_far)
    dn_got = exchange(dn_here, "wid")
    mean_two = line_sum(s_own, s_far, dn_got)
    grad_normed_two = jnp.sum(dn_got.astype(f32), axis=0)

    chunk = width // dp_size
    direct = dp_size == wid_size
    sub = chunk // wid_size

    def dp_pieces(terms, picked, rest, cols, flags, ts):
        if direct:
            idx = jnp.stack([dp ^ t for t in ts]).astype(jnp.int32)
            idx = jnp.concatenate([idx, *flags])
            return weight_call(terms, idx, picked, rest, cols, 2 * half * part * cols, len(flags))
        idx = jnp.concatenate([jnp.arange(wid_size, dtype=jnp.int32), *flags])
        full = weight_call(terms, idx, picked, rest, cols, 2 * half * part * cols, len(flags))
        full = full.reshape(width, -1)
        return jnp.stack([shift_rows(full, (dp ^ t) * chunk, chunk) for t in ts])

    def dp_odd(terms, picked, rest, cols, flags=()):
        return dp_pieces(terms, picked, rest, cols, flags, range(1, dp_size, 2))

    def dp_even(terms, picked, rest, cols, got, flags=()):
        if direct and dp_size == 4:
            idx = jnp.stack([dp, dp ^ 2]).astype(jnp.int32)
            idx = jnp.concatenate([idx, *flags])
            flops = 2 * half * part * cols
            keep, send = weight_add(terms, idx, picked, rest, got, cols, flops)
            return keep, swap(send, "dp", dp_size, 2)
        here = dp_pieces(terms, picked, rest, cols, flags, range(0, dp_size, 2))
        return dp_send(here.astype(f32) + got.astype(f32))

    def dp_send(held, k=2):
        return held[0::2], swap(held[1::2].astype(bf16), "dp", dp_size, k)

    def dp_take(keep, got, k=2):
        held = keep + got.astype(f32)
        while held.shape[0] > 1:
            k *= 2
            keep, got = dp_send(held, k)
            held = keep + got.astype(f32)
        return held[0]

    def dp_sum(pieces, *late):
        odd, even = jnp.stack(pieces[1::2]), jnp.stack(pieces[0::2])
        got = after(swap(odd.astype(bf16), "dp", dp_size, 1), *late)
        return dp_take(*dp_send(even.astype(f32) + got.astype(f32)))

    def to_rows(x):
        return exchange(x.astype(bf16).reshape(wid_size, sub, -1), "wid")

    gate_up = [functools.partial(gate_up_terms, c) for c in range(2)]
    n2_both, gs_both = (n2_own, n2_far), (gs_own, gs_far)
    odd = [dp_odd(gate_up[0], n2_both, (after(d_own, dn_here), d_far), ff)]
    odd.append(dp_odd(gate_up[1], n2_both, (after(d_own, odd[0]), d_far), ff))
    odd.append(dp_odd(down_terms, gs_both, (after(m_own, odd[1]), m_far), ff))
    got_odd = [swap(x, "dp", dp_size, 1) for x in odd]

    grad_half = g_own.astype(f32) * valid_half
    grad_hidden = grad_half + r2_own * (
        grad_normed_two * gain_two - r2_own * hidden * mean_two
    )
    gain_two_part = jnp.sum(grad_normed_two * hidden * r2_own, axis=0)
    da_own = after(grad_hidden.astype(bf16), odd[2])
    da_far = hid_swap(da_own)
    keep_0, next_0 = dp_even(gate_up[0], n2_both, (after(d_own, odd[2]), d_far), ff, got_odd[0])
    do_here = attention_out_back(place, w_out, after(da_own, keep_0), da_far, wid_size)
    do_pieces = exchange(do_here, "wid")
    ffn_own_out, ffn_far_out = feed_forward_out(
        side, after(m_own, do_here), m_far, ffn_own, ffn_other
    )
    g_out = out_gradient(place, after(da_own, ffn_far_out), da_far, o_all, w_out.shape[1])
    do_got = do_pieces.reshape(wid_size, -1, SEQ, HD)

    pairs_a, lines_a, sums_a = attention_backward(
        lens, pairs, logit_pairs, inv, carry, prob, after(do_got, ffn_far_out, g_out), 0, 2 * per_half
    )

    head_iota = lax.broadcasted_iota(jnp.int32, (1, 16, 1), 1)
    m_then = after(m_own, pairs_a)
    keep_2, next_2 = dp_even(down_terms, gs_both, (m_then, m_far), ff, got_odd[2])
    right_own = pairs_a.reshape(2, half, 4 * HD)
    ffn_here = after(partial(ffn_own_out, after(ffn_far_out, do_got)), pairs_a)
    ffn_back = exchange(ffn_here, "wid")

    n1_both = (n1_own, n1_far)
    own_odd = dp_odd(own_terms, n1_both, (right_own,), 4 * HD)
    own_got = swap(own_odd, "dp", dp_size, 1)
    d_then = after(d_own, own_odd)
    keep_1, next_1 = dp_even(gate_up[1], n2_both, (d_then, d_far), ff, got_odd[1])
    pairs_b, lines_b, sums_b = attention_backward(
        lens, pairs, logit_pairs, inv, carry, prob, after(do_got, own_odd, keep_1, next_0), 2 * per_half, per_half
    )

    def spread(a, b, at):
        own = a[at * per_half : (at + 1) * per_half]
        return own, jnp.where(half_b == at, b, 0.0)

    def lines_at(at):
        own, shared = spread(lines_a, lines_b, at)
        own = jnp.where(head_iota == my_head, own, 0.0)
        shared = jnp.where(head_iota == my_shared, shared, 0.0)
        return (own + shared).astype(bf16)

    def flat_lines(x):
        flat = jnp.swapaxes(x, 0, 1).reshape(16, half)
        return jnp.concatenate([flat, jnp.zeros((128 - 16, half), bf16)], axis=0)

    lines_own, lines_far = lines_at(0), lines_at(1)
    flat_own, flat_far = flat_lines(lines_own), flat_lines(lines_far)
    right_shared = after(pairs_b, keep_2, next_1).reshape(half, 4 * HD)

    flat_both = (flat_own, flat_far)
    half_flag = (half_b.astype(jnp.int32)[None],)
    shared_odd = dp_odd(shared_terms, n1_both, (right_shared, *flat_both), 5 * HD, half_flag)
    shared_got = swap(shared_odd, "dp", dp_size, 1)
    fine = part // dp_size
    to_place = [
        (c * wid_size + w, w * dp_size + c) for c in range(dp_size) for w in range(wid_size)
    ]

    def dp_fine(x, *late):
        return dp_sum([shift_rows(x, (dp ^ t) * fine, fine) for t in range(dp_size)], *late)

    out_pieces = [shift_rows(g_out, (dp ^ t) * fine, fine) for t in range(dp_size)]
    out_got = swap(jnp.stack(out_pieces[1::2]), "dp", dp_size, 1)
    flags = [(half_b == p).astype(jnp.int32)[None] for p in range(2)]
    back_b = after(pairs_b, shared_odd, own_got, ffn_back)
    dn1_far = project_back(flags[1], pairs_a, per_half, back_b, lines_far, proj_w, misc, bf16)
    right_own = after(right_own, dn1_far, own_got)
    keep_own, next_own = dp_even(own_terms, n1_both, (right_own,), 4 * HD, own_got)
    back_b = after(back_b, keep_own, next_2)
    dn1_own = project_back(flags[0], pairs_a, 0, back_b, lines_own, proj_w, misc, f32)
    dn1_here = partial(dn1_own, dn1_far)
    dn1_got = exchange(dn1_here, "wid")
    right_shared = after(right_shared, dn1_here, shared_got)
    right_shared = after(right_shared, next_own)
    keep_shared, next_shared = dp_even(
        shared_terms, n1_both, (right_shared, *flat_both), 5 * HD, shared_got, half_flag
    )
    next_own, next_shared = lax.optimization_barrier((next_own, next_shared, dn1_got))[:2]
    sums = [sum(spread(sums_a, sums_b, p)) for p in range(2)]
    mean_one = line_sum(*sums, dn1_got)
    grad_normed_one = jnp.sum(dn1_got.astype(f32), axis=0)
    ffn = jnp.sum(ffn_back.astype(f32), axis=0)

    source = x_own.astype(f32)
    r1_half = r_own.reshape(half, 1)
    gain_one_part = jnp.sum(grad_normed_one * source * r1_half, axis=0)
    input_half = grad_hidden + r1_half * (
        grad_normed_one * gain_one - r1_half * source * mean_one
    )

    def whole_rows(x):
        other = hid_swap(x)
        return jnp.concatenate(
            [jnp.where(hid == 0, x, other), jnp.where(hid == 0, other, x)], axis=0
        )

    ffn_sums = [dp_take(keep_0, next_0), dp_take(keep_1, next_1), dp_take(keep_2, next_2)]
    ffn_sums = after(jnp.concatenate(ffn_sums, axis=1).astype(bf16), dn1_got)
    ffn_rows = to_rows(ffn_sums)
    input_grad = whole_rows(after(input_half.astype(bf16), ffn_sums))
    output = whole_rows(after(((hidden + ffn) * valid_half).astype(bf16), ffn_sums))

    proj_sums = [dp_take(keep_own, next_own), dp_take(keep_shared, next_shared)]
    proj_sums = jnp.concatenate(proj_sums, axis=1).astype(bf16)
    out_even = jnp.stack(out_pieces[0::2]).astype(f32)
    out_got = after(out_got, dn1_got)
    out_sum = dp_take(*dp_send(out_even + out_got.astype(f32))).astype(bf16)
    out_sum = after(out_sum, proj_sums, ffn_rows)
    out_out = lax.ppermute(out_sum, ("dp", "wid"), to_place).astype(f32)
    gain_part = after(jnp.stack([gain_one_part, gain_two_part], axis=1), proj_sums, ffn_rows)
    gain_part = gain_part + hid_swap(gain_part)
    gain_sum = lax.ppermute(dp_fine(gain_part), ("dp", "wid"), to_place)

    got = ffn_rows[:, :, : 2 * ff].reshape(wid_size, sub, 2, 2, ffh)
    gate, up = (
        jnp.concatenate([got[w, :, c, k] for w in ws for c in range(2)], axis=1) for k in range(2)
    )
    down = jnp.concatenate([ffn_rows[w, :, 2 * ff :] for w in ws], axis=1)
    out_gate_up = jnp.stack([gate, up], axis=1).astype(f32)
    out_down = down.astype(f32)

    got = to_rows(after(proj_sums, ffn_rows)).astype(f32)
    a = [got[w, :, : 4 * HD] for w in ws]
    b = [got[w, :, 4 * HD : 8 * HD] for w in ws]
    proj_rows = [a[0], b[0] + b[1], a[1], a[2], b[2] + b[3], a[3]]
    out_project = jnp.concatenate([p.reshape(sub, 4, HD) for p in proj_rows], axis=2)
    out_beta = jnp.sum(got[:, :, 8 * HD : 8 * HD + heads], axis=0)


    return (
        output,
        input_grad,
        out_project,
        out_beta,
        out_out,
        out_gate_up,
        out_down,
        gain_sum[:, 0],
        gain_sum[:, 1],
    )


def solution(mesh):
    return jax.shard_map(
        functools.partial(per_device, mesh.shape["dp"], mesh.shape["wid"]),
        mesh=mesh,
        in_specs=(
            P("dp", "wid"),
            P("dp", "wid"),
            P(("dp", "wid")),
            P("wid", None, "hid"),
            P("wid", "hid"),
            P("wid", "hid"),
            P("wid", None, "hid"),
            P("wid", "hid"),
            P("wid"),
            P("wid"),
        ),
        out_specs=(
            P("dp", "wid"),
            P("dp", "wid"),
            P(("dp", "wid"), None, "hid"),
            P(("dp", "wid"), "hid"),
            P(("dp", "wid"), "hid"),
            P(("dp", "wid"), None, "hid"),
            P(("dp", "wid"), "hid"),
            P(("dp", "wid")),
            P(("dp", "wid")),
        ),
        check_vma=False,
    )
```
